32 devices in a mesh: dp: 4 (over z), seq: 8 (over y, x, core).
Axes of the slice: x: 2, y: 2, z: 4, core: 2. Of those that a mesh axis runs over, the one named last changes fastest.
Arguments:
- tokens: bfloat16 [8192, 768], P(('dp', 'seq')), may hold values from -6 to 6
- doc_ids: int32 [8192], P(('dp', 'seq')), may hold values from 0 to 1, as said below
- cotangent: bfloat16 [8192, 768], P(('dp', 'seq')), may hold values from -6 to 6
- w_qkv: bfloat16 [768, 2304], P(('dp', 'seq')), may hold values from -0.3125 to 0.3125
- bias_qv: bfloat16 [2, 768], P(None, ('dp', 'seq')), may hold values from -3 to 3
- w_o: bfloat16 [768, 768], P(('dp', 'seq')), may hold values from -0.875 to 0.875
- bias_o: bfloat16 [768], P(('dp', 'seq')), may hold values from -2 to 2
- ln_gain: bfloat16 [2, 768], P(None, ('dp', 'seq')), may hold values from 0.25 to 1.75
- ln_bias: bfloat16 [2, 768], P(None, ('dp', 'seq')), may hold values from -2 to 2
- w_in: bfloat16 [768, 3072], P(('dp', 'seq')), may hold values from -0.21875 to 0.21875
- bias_in: bfloat16 [3072], P(('dp', 'seq')), may hold values from -3 to 3
- w_out: bfloat16 [3072, 768], P(('dp', 'seq')), may hold values from -0.109375 to 0.109375
- bias_out: bfloat16 [768], P(('dp', 'seq')), may hold values from -2 to 2
Outputs:
- block_out: bfloat16 [8192, 768], P(('dp', 'seq'))
- input_grad: float32 [8192, 768], P(('dp', 'seq'))
- grad_w_qkv: float32 [768, 2304], P(('dp', 'seq'))
- grad_bias_qv: float32 [2, 768], P(None, ('dp', 'seq'))
- grad_w_o: float32 [768, 768], P(('dp', 'seq'))
- grad_bias_o: float32 [768], P(('dp', 'seq'))
- grad_ln_gain: float32 [2, 768], P(None, ('dp', 'seq'))
- grad_ln_bias: float32 [2, 768], P(None, ('dp', 'seq'))
- grad_w_in: float32 [768, 3072], P(('dp', 'seq'))
- grad_bias_in: float32 [3072], P(('dp', 'seq'))
- grad_w_out: float32 [3072, 768], P(('dp', 'seq'))
- grad_bias_out: float32 [768], P(('dp', 'seq'))
The draws below stay inside these ranges and needn't reach their ends.
Inputs may be any that keep to these rules, and one draw needn't show every extreme that they name: `doc_ids`: each stream holds exactly two sequences: ids 0 then 1, never falling; the first covers b whole aligned blocks of 256 positions, with 1 <= b <= 2, and the second the rest of the stream.
All inputs are finite; a program needn't handle non-finite values.
Results may differ from the reference program's by a relative error of at most 0.02.
The reference program's roundings to bfloat16 on the way count: a program that leaves them out, or rounds other values in their place, can miss the bound.
Values may be sent and summed in bfloat16 or wider, within the bound.
No kernel may reach another device: no remote copies, remote signals or barrier semaphores. Data moves between devices by JAX's collectives and lax.ppermute only.
A program may use at most 192 MiB of HBM per device.

```python
import math
import jax
import jax.numpy as jnp
from jax import lax

D = 768
HEADS = 12
HDIM = 64
FF = 3072
BLK = 256
STREAM = 2048
TOKENS = 8192
N_DP = 4


def draw_doc_ids(key, part):
    count = STREAM // BLK
    streams = TOKENS // STREAM
    boundary = jax.random.randint(key, (streams,), count // 8, count // 4 + 1)
    block_index = jnp.arange(count, dtype=jnp.int32)
    labels = (block_index[None, :] >= boundary[:, None]).astype(jnp.int32)
    return jnp.repeat(labels, BLK, axis=1).reshape(TOKENS).astype(jnp.int32)


def spiked(drawn, stream_key, source, target, parts, factor):
    def block_of(position):
        return (jnp.arange(drawn.shape[position]) // (drawn.shape[position] // parts)).reshape((-1,) + (1,) * (drawn.ndim - 1 - position))

    one_side = jax.random.permutation(stream_key, parts)[block_of(target)]
    other_side = (block_of(target) + parts // 2) % parts
    return jnp.where((block_of(source) == one_side) | (block_of(source) == other_side), factor * drawn, drawn)


def level_of(stream_key, extent, pieces, smallest, top_value):
    level, own = 1.0, jax.random.fold_in(stream_key, 6)
    for dim, blocks in pieces:
        steps = jnp.exp(jax.random.uniform(jax.random.fold_in(own, dim), (blocks,), jnp.float32, smallest / len(pieces), top_value / len(pieces)))
        level = level * jnp.repeat(steps, extent[dim] // blocks).reshape([-1 if axis == dim else 1 for axis in range(len(extent))])
    return level


def noise(stream_key, extent, scale, limit, cuts=(), kind=jnp.bfloat16):
    loudness = level_of(stream_key, extent, cuts, -0.22, 0.18) if cuts else 1.0
    values = jax.random.normal(stream_key, extent, jnp.float32) * scale * loudness
    return jnp.minimum(jnp.maximum(values, -limit), limit).astype(kind)


def noise_with(rng, dims, scale, reach, cuts, heavy, kind=jnp.bfloat16):
    values = scale * jax.random.normal(rng, dims, jnp.float32)
    if cuts:
        values = values * level_of(rng, dims, cuts, -0.22, 0.18)
    return jnp.clip(spiked(values, jax.random.fold_in(rng, 3), *heavy), -reach, reach).astype(kind)


def setup_inputs(seed: int = 0) -> dict:
    seeds = jax.random.split(jax.random.key(seed), 14)
    tokens = noise_with(seeds[0], (TOKENS, D), 1.0, 6.0, ((0, 32),), (0, 1, 32, 2.75))
    doc_ids = draw_doc_ids(jax.random.fold_in(seeds[13], 71), 0)
    cotangent = noise_with(seeds[2], (TOKENS, D), 1.0, 6.0, ((0, 32),), (0, 1, 32, 2.75))
    w_qkv = noise(seeds[3], (D, 3 * D), (D // 2) ** -0.5, 0.3125, ((0, 32),))
    bias_qv = noise(seeds[4], (2, D), 0.5, 3.0, ((1, 32),))
    w_o = noise(seeds[5], (D, D), (D // 16) ** -0.5, 0.875, ((0, 32),))
    bias_o = noise(seeds[6], (D,), 0.3, 2.0, ((0, 32),))
    ln_gain = jnp.clip(1.0 + 0.15 * jax.random.normal(seeds[7], (2, D), jnp.float32), 0.25, 1.75).astype(jnp.bfloat16)
    ln_bias = noise(seeds[8], (2, D), 0.3, 2.0, ((1, 32),))
    w_in = noise(seeds[9], (D, FF), D ** -0.5, 0.21875, ((0, 32),))
    bias_in = noise(seeds[10], (FF,), 0.5, 3.0, ((0, 32),))
    w_out = noise(seeds[11], (FF, D), FF ** -0.5, 0.109375, ((0, 32),))
    bias_out = noise(seeds[12], (D,), 0.3, 2.0, ((0, 32),))
    return dict(tokens=tokens, doc_ids=doc_ids, cotangent=cotangent, w_qkv=w_qkv, bias_qv=bias_qv, w_o=w_o, bias_o=bias_o, ln_gain=ln_gain, ln_bias=ln_bias, w_in=w_in, bias_in=bias_in, w_out=w_out, bias_out=bias_out)


@jax.custom_vjp
def low(v):
    return lax.optimization_barrier(v.astype(jnp.bfloat16)).astype(jnp.float32)

@jax.custom_vjp
def low_back(v):
    return v

def low_keep(v):
    return (low(v), None)

def low_pass(kept, grad):
    return (grad,)

def back_keep(v):
    return (v, None)

def back_low(kept, grad):
    return (low(grad),)
low.defvjp(low_keep, low_pass)
low_back.defvjp(back_keep, back_low)
EPSILON = 1e-12
NEG_LARGE = -1e+30

def matmul(left, right):
    return jnp.dot(left, right, precision=lax.Precision.HIGHEST, preferred_element_type=jnp.float32)

def layer_norm(resid, gain, shift):
    center = resid - lax.optimization_barrier(jnp.mean(resid, axis=-1, keepdims=True))
    spread = lax.optimization_barrier(jnp.mean(center * center, axis=-1, keepdims=True))
    return center * lax.rsqrt(spread + EPSILON) * gain + shift

def attention(queries, keys, values, doc):
    length = queries.shape[0]
    rows = math.gcd(length, 512)
    blocks = jnp.arange(length, dtype=jnp.int32) // BLK
    key_heads = keys.reshape(length, HEADS, HDIM)
    value_heads = values.reshape(length, HEADS, HDIM)

    @jax.checkpoint
    def one_block(items):
        query_part, doc_part, block_part = items
        raw = jnp.einsum('qhd,khd->hqk', query_part, key_heads, precision=lax.Precision.HIGHEST)
        scores = low_back(raw) * 0.125
        allowed = (doc_part[:, None] == doc[None, :]) & (blocks[None, :] <= block_part[:, None])
        masked = jnp.where(allowed[None], scores, NEG_LARGE)
        top = lax.optimization_barrier(jnp.max(masked, axis=-1, keepdims=True))
        expd = jnp.exp(masked - top)
        probs = low(expd / lax.optimization_barrier(jnp.sum(expd, axis=-1, keepdims=True)))
        mixed = jnp.einsum('hqk,khd->qhd', probs, value_heads, precision=lax.Precision.HIGHEST)
        return mixed.reshape(rows, D)
    result = lax.map(one_block, (queries.reshape(length // rows, rows, HEADS, HDIM), doc.reshape(length // rows, rows), blocks.reshape(length // rows, rows)))
    return result.reshape(length, D)

def forward(params, inputs, doc):
    w_qkv, bias_qv, w_o, bias_o, ln_gain, ln_bias, w_in, bias_in, w_out, bias_out = params
    bias_three = jnp.concatenate([bias_qv[0], jnp.zeros((D,), jnp.float32), bias_qv[1]])
    projected = low(low_back(matmul(inputs, w_qkv)) + bias_three)
    attended = attention(projected[:, :D], projected[:, D:2 * D], projected[:, 2 * D:], doc)
    attended_low = low(low_back(attended))
    resid_one = inputs + low_back(matmul(attended_low, w_o)) + bias_o
    hidden_one = layer_norm(resid_one, ln_gain[0], ln_bias[0])
    pre_act = low_back(matmul(low(hidden_one), w_in)) + bias_in
    act_low = low(jax.nn.gelu(pre_act, approximate=False))
    resid_two = hidden_one + low_back(matmul(act_low, w_out)) + bias_out
    return layer_norm(resid_two, ln_gain[1], ln_bias[1])

def reference(tokens, doc_ids, cotangent, w_qkv, bias_qv, w_o, bias_o, ln_gain, ln_bias, w_in, bias_in, w_out, bias_out):
    params = tuple((a.astype(jnp.float32) for a in (w_qkv, bias_qv, w_o, bias_o, ln_gain, ln_bias, w_in, bias_in, w_out, bias_out)))
    streams = tokens.astype(jnp.float32).reshape(N_DP, STREAM, D)
    docs = doc_ids.reshape(N_DP, STREAM)
    grads_in = cotangent.astype(jnp.float32).reshape(N_DP, STREAM, D)

    def one_stream(totals, items):
        inputs, doc, grad_out = items
        result, pull = jax.vjp(lambda p, x: forward(p, x, doc), params, inputs)
        grad_params, grad_inputs = pull(grad_out)
        totals = jax.tree.map(lambda a, b: a + b, totals, grad_params)
        return (totals, (result, grad_inputs))
    start_totals = jax.tree.map(jnp.zeros_like, params)
    totals, (results, grad_inputs) = lax.scan(one_stream, start_totals, (streams, docs, grads_in))
    return (results.reshape(TOKENS, D).astype(jnp.bfloat16), grad_inputs.reshape(TOKENS, D), totals[0], totals[1], totals[2], totals[3], totals[4], totals[5], totals[6], totals[7], totals[8], totals[9])
```

```python
import math

import jax
import jax.numpy as jnp
from jax import lax
from jax.experimental import pallas as pl
from jax.experimental.pallas import tpu as pltpu
from jax.sharding import PartitionSpec as P

HEADS = 12
HDIM = 64
BLK = 256


EPSILON = 1e-12
NEG_LARGE = -1e30

F32 = jnp.float32
BF16 = jnp.bfloat16
LOG2E = 1.4426950408889634
NT = (((1,), (1,)), ((), ()))
TN = (((0,), (0,)), ((), ()))
NN = (((1,), (0,)), ((), ()))


def dot(left, right, dims=NN):
    return lax.dot_general(left, right, dims, preferred_element_type=F32)


def sds(shape, dtype):
    return jax.ShapeDtypeStruct(shape, dtype)


def call(kernel, args, outs, scratch=(), smem_in=(0,), smem_out=(), flops=0, name=None):
    space = lambda inside: pl.BlockSpec(memory_space=pltpu.SMEM if inside else pltpu.VMEM)
    nbytes = sum(math.prod(a.shape) * a.dtype.itemsize for a in tuple(args) + tuple(outs))
    return pl.pallas_call(
        kernel,
        out_shape=tuple(outs),
        in_specs=[space(i in smem_in) for i in range(len(args))],
        out_specs=tuple(space(i in smem_out) for i in range(len(outs))),
        scratch_shapes=list(scratch),
        compiler_params=pltpu.CompilerParams(vmem_limit_bytes=60 * 1024 * 1024),
        cost_estimate=pl.CostEstimate(
            flops=int(flops), transcendentals=0, bytes_accessed=int(nbytes)
        ),
        name=name,
    )(*args)


def place(pos):
    d = pos[0]
    return d >> 3, (d >> 1) & 3, d & 1


def row_of(start, size=8):
    return pl.multiple_of(start, size)


def pack_kernel(pos, wqkv, win, wout, smalls, p0, p1, p2, p3, wx):
    z, p, c = place(pos)
    rows = lax.broadcasted_iota(jnp.int32, (96, 96), 0)
    cols = lax.broadcasted_iota(jnp.int32, (96, 96), 1)
    eye = (rows == cols).astype(BF16)
    side = dot(eye, smalls[...], NT).astype(BF16)
    wx[...] = jnp.concatenate([wout[...], side, jnp.zeros((96, 112), BF16)], axis=1)
    small = jnp.concatenate([side[:24], jnp.zeros((24, 48), BF16)], axis=1)

    def piece(chip):
        parts = [wqkv[:, 768 * i + 192 * chip : 768 * i + 192 * chip + 192] for i in range(3)]
        parts.append(small)
        parts += [win[:, 768 * i + 192 * chip : 768 * i + 192 * chip + 192] for i in range(4)]
        return jnp.concatenate(parts, axis=1)

    for own in range(4):

        @pl.when(p == own)
        def _(own=own):
            for k, out in enumerate((p0, p1, p2, p3)):
                out[...] = piece(own ^ k)


def interleave(pos, mine, other, lanes, out, order):
    z, p, c = place(pos)

    def run(first, second):
        for j in range(4):
            for k in range(4):
                at = (j, slice(24 * k, 24 * k + 24), lanes) if order == "jk" else (
                    k, slice(24 * j, 24 * j + 24), lanes)
                block = jnp.concatenate([first[at], second[at]], axis=0)
                start = ((z ^ j) * 4 + (p ^ k)) * 48
                out[pl.ds(row_of(start, 16), 48), :] = block

    @pl.when(c == 0)
    def _():
        run(mine, other)

    @pl.when(c == 1)
    def _():
        run(other, mine)


def qkv_kernel(pos, am, ao, x0, x1, x2, x3, q, kv, wq, vecs, nb, bias):
    z, p, c = place(pos)
    interleave(pos, am, ao, slice(None), wq, "jk")
    flipped = jnp.transpose(wq[:, 512:640].astype(F32))
    vecs[...] = flipped[64:80]
    for own in range(4):

        @pl.when(p == own)
        def _(own=own):
            at = slice(192 * own, 192 * own + 192)
            bias[0:1, :] = jnp.concatenate(
                [vecs[0:1, at], jnp.zeros((1, 192), F32), vecs[1:2, at], jnp.zeros((1, 64), F32)],
                axis=1,
            )

    lane = lax.broadcasted_iota(jnp.int32, (1, 768), 1)
    mask = (lane >= 192 * z) & (lane < 192 * z + 192) & (lane % 24 == 0)
    second = jnp.sum(jnp.where(mask, vecs[8:9, :], 0.0))
    nb[0] = 8 - second.astype(jnp.int32)
    for k, x in enumerate((x0, x1, x2, x3)):
        got = (dot(x[...], wq[...]) + bias[0:1, :]).astype(BF16)
        q[k] = got[:, :192]
        kv[k] = got[:, 192:576]


def weights_kernel(pos, mm, mo, wi, wx, bin_):
    z, p, c = place(pos)
    interleave(pos, mm, mo, slice(0, 768), wi, "jk")
    for j in range(4):
        base = (z ^ j) * 192
        wx[pl.ds(row_of(base + c * 96, 32), 96), :] = mm[j, :, 768:1664]
        wx[pl.ds(row_of(base + (1 - c) * 96, 32), 96), :] = mo[j, :, 768:1664]
    flipped = jnp.transpose(wx[:, 768:896].astype(F32))
    bin_[...] = flipped[8:16]


def wo_kernel(pos, om, oo, wo):
    interleave(pos, om, oo, slice(None), wo, "kj")


def absolute_kv(pos, mine, other, kv):
    z, p, c = place(pos)
    for k in range(4):
        first = 2 * (p ^ k)
        kv[first + c] = mine[k]
        kv[first + 1 - c] = other[k]


def key_range(pos, nb, k):
    z, p, c = place(pos)
    block = 2 * (p ^ k) + c
    return jnp.where(block < nb[0], 0, nb[0]), block + 1


def attention_kernel(pos, nb, q, mine, other, a0, a1, a2, a3, ot, lse, kv):
    scale = 0.125 * LOG2E
    absolute_kv(pos, mine, other, kv)
    for k, out in enumerate((a0, a1, a2, a3)):
        low, high = key_range(pos, nb, k)
        heads = [q[k, :, 64 * h : 64 * h + 64] for h in range(3)]

        def step(kb, state):
            new = []
            for h in range(3):
                top, total, acc = state[h]
                keys = kv[kb, :, 64 * h : 64 * h + 64]
                values = kv[kb, :, 192 + 64 * h : 256 + 64 * h]
                scores = dot(keys, heads[h], NT)
                next_top = jnp.maximum(top, jnp.max(scores, axis=0, keepdims=True))
                weights = jnp.exp2((scores - next_top) * scale)
                factor = jnp.exp2((top - next_top) * scale)
                total = total * factor + jnp.sum(weights, axis=0, keepdims=True)
                acc = acc * factor + dot(values, weights.astype(BF16), TN)
                new.append((next_top, total, acc))
            return tuple(new)

        start = tuple(
            (jnp.full((1, BLK), NEG_LARGE, F32), jnp.zeros((1, BLK), F32), jnp.zeros((HDIM, BLK), F32))
            for _ in range(3)
        )
        state = lax.fori_loop(low, high, step, start)
        done = []
        for h in range(3):
            top, total, acc = state[h]
            mixed = acc / total
            ot[k, 64 * h : 64 * h + 64, :] = mixed
            lse[k, h : h + 1, :] = top * scale + jnp.log(total) * LOG2E
            done.append(mixed)
        out[...] = jnp.transpose(jnp.concatenate(done, axis=0)).astype(BF16)


def attention_back_kernel(
    pos, nb, q, mine, other, g0, g1, g2, g3, ot, lse, dq, dmine, dother, kv, dkv
):
    z, p, c = place(pos)
    scale = 0.125 * LOG2E
    absolute_kv(pos, mine, other, kv)
    dkv[...] = jnp.zeros(dkv.shape, F32)
    for k, grad in enumerate((g0, g1, g2, g3)):
        low, high = key_range(pos, nb, k)
        heads = [q[k, :, 64 * h : 64 * h + 64] for h in range(3)]
        grads = [grad[:, 64 * h : 64 * h + 64] for h in range(3)]
        flipped = jnp.transpose(grad[...].astype(F32))
        product = flipped * ot[k]
        deltas = [
            jnp.sum(product[64 * h : 64 * h + 64], axis=0, keepdims=True) for h in range(3)
        ]
        logs = [lse[k, h : h + 1, :] for h in range(3)]

        def step(kb, state):
            new = []
            for h in range(3):
                keys = kv[kb, :, 64 * h : 64 * h + 64]
                values = kv[kb, :, 192 + 64 * h : 256 + 64 * h]
                probs = jnp.exp2(dot(keys, heads[h], NT) * scale - logs[h])
                dprobs = dot(values, grads[h], NT)
                low_scores = (probs * (dprobs - deltas[h]) * 0.125).astype(BF16)
                dkv[h, kb] += dot(low_scores, heads[h])
                dkv[3 + h, kb] += dot(probs.astype(BF16), grads[h])
                new.append(state[h] + dot(keys, low_scores, TN))
            return tuple(new)

        state = lax.fori_loop(
            low, high, step, tuple(jnp.zeros((HDIM, BLK), F32) for _ in range(3))
        )
        dq[k] = jnp.transpose(jnp.concatenate(state, axis=0))
    for k in range(4):
        first = 2 * (p ^ k)
        dmine[k] = jnp.concatenate([dkv[i, first + c] for i in range(6)], axis=1)
        dother[k] = jnp.concatenate([dkv[i, first + 1 - c] for i in range(6)], axis=1).astype(BF16)


def norm_kernel(pos, tokens, a0, a1, a2, a3, wo, vecs, low, xhat, rstd):
    z, p, c = place(pos)
    resid = tokens[...].astype(F32) + vecs[2:3, :]
    for k, a in enumerate((a0, a1, a2, a3)):
        start = (p ^ k) * 192
        resid += dot(a[...], wo[pl.ds(row_of(start, 64), 192), :])
    center = resid - jnp.mean(resid, axis=-1, keepdims=True)
    scale = lax.rsqrt(jnp.mean(center * center, axis=-1, keepdims=True) + EPSILON)
    hat = center * scale
    xhat[...] = hat
    rstd[...] = scale
    low[...] = (hat * vecs[3:4, :] + vecs[5:6, :]).astype(BF16)


def norm_grad(grad, gain, hat, scale):
    e = grad * gain
    mean_e = jnp.mean(e, axis=-1, keepdims=True)
    mean_x = jnp.mean(e * hat, axis=-1, keepdims=True)
    return scale * (e - mean_e - hat * mean_x)


def total(values):
    return jnp.sum(values, axis=0, keepdims=True)


def norm_two_kernel(vecs, xhat, own, r1, r2, r3, cot, block_out, low, grad_two, sums):
    acc = [jnp.zeros((1, 768), F32) for _ in range(3)]
    for i in range(8):
        at = slice(32 * i, 32 * i + 32)
        hidden = xhat[at, :] * vecs[3:4, :] + vecs[5:6, :]
        resid = hidden + own[at, :] + vecs[7:8, :]
        for r in (r1, r2, r3):
            resid += r[at, :].astype(F32)
        center = resid - jnp.mean(resid, axis=-1, keepdims=True)
        scale = lax.rsqrt(jnp.mean(center * center, axis=-1, keepdims=True) + EPSILON)
        hat = center * scale
        block_out[at, :] = (hat * vecs[4:5, :] + vecs[6:7, :]).astype(BF16)
        grad = cot[at, :].astype(F32)
        back = norm_grad(grad, vecs[4:5, :], hat, scale)
        grad_two[at, :] = back
        low[at, :] = back.astype(BF16)
        acc = [acc[0] + total(grad * hat), acc[1] + total(grad), acc[2] + total(back)]
    sums[...] = jnp.concatenate(acc + [jnp.zeros((5, 768), F32)], axis=0)


def norm_one_kernel(
    pos, own, r1, r2, r3, grad_two, xhat, rstd, vecs, wo, o0, o1, o2, o3, low, grad_one, sums
):
    z, p, c = place(pos)
    acc = [jnp.zeros((1, 768), F32) for _ in range(3)]
    for i in range(8):
        at = slice(32 * i, 32 * i + 32)
        grad = own[at, :] + grad_two[at, :]
        for r in (r1, r2, r3):
            grad += r[at, :].astype(F32)
        hat = xhat[at, :]
        back = norm_grad(grad, vecs[3:4, :], hat, rstd[at, :])
        grad_one[at, :] = back
        low[at, :] = back.astype(BF16)
        acc = [acc[0] + total(grad * hat), acc[1] + total(grad), acc[2] + total(back)]
    sums[...] = jnp.concatenate(acc + [jnp.zeros((5, 768), F32)], axis=0)
    for k, out in enumerate((o0, o1, o2, o3)):
        start = (p ^ k) * 192
        out[...] = dot(low[...], wo[pl.ds(row_of(start, 64), 192), :], NT).astype(BF16)


def ff_kernel(count):
    def kernel(*refs):
        hs = refs[:count]
        wi, wx, bias = refs[count : count + 3]
        outs = refs[count + 3 :]
        for i, h in enumerate(hs):
            part, act, slope = outs[3 * i : 3 * i + 3]
            acc = jnp.zeros((256, 768), F32)
            for f in range(3):
                at = slice(256 * f, 256 * f + 256)
                u = dot(h[...], wi[:, at]) + bias[1:2, at]
                cdf = 0.5 * (1.0 + lax.erf(u * 0.7071067811865476))
                low = (u * cdf).astype(BF16)
                act[:, at] = low
                slope[:, at] = cdf + u * jnp.exp2(u * u * (-0.5 * LOG2E)) * 0.3989422804014327
                acc += dot(low, wx[at, :768])
            part[...] = acc.astype(part.dtype)

    return kernel


def ff_back_kernel(count):
    def kernel(*refs):
        gs = refs[:count]
        slopes = refs[count : 2 * count]
        wi, wx = refs[2 * count : 2 * count + 2]
        sums = refs[2 * count + 2]
        outs = refs[2 * count + 3 :]
        for f in range(3):
            at = slice(256 * f, 256 * f + 256)
            acc = jnp.zeros((1, 256), F32)
            for i in range(count):
                pre = dot(gs[i][...], wx[at, :768], NT) * slopes[i][:, at]
                outs[2 * i + 1][:, at] = pre.astype(BF16)
                acc += total(pre)
            sums[:, at] = jnp.broadcast_to(acc, (8, 256))
        for i in range(count):
            back = dot(outs[2 * i + 1][...], wi[...], NT)
            outs[2 * i][...] = back.astype(outs[2 * i].dtype)

    return kernel


def column_of(row):
    n = row.shape[1]
    first = lax.broadcasted_iota(jnp.int32, (128, n), 0) == 0
    return jnp.transpose(jnp.where(first, jnp.broadcast_to(row, (128, n)), 0.0))


def ff_grad_kernel(*refs):
    pos = refs[0]
    hs, pres, acts, gs = refs[1:5], refs[5:9], refs[9:13], refs[13:17]
    sum_a, sum_b = refs[17:19]
    keep, send, gi, go = refs[19:]
    z, p, c = place(pos)
    gi[...] = sum(dot(hs[k][...], pres[k][...], TN) for k in range(4))
    go[:, :768] = sum(dot(acts[k][...], gs[k][...], TN) for k in range(4))
    go[:, 768:] = column_of(sum_a[0:1, :] + sum_b[0:1, :])
    for j in range(4):
        for out, core in ((keep, c), (send, 1 - c)):
            for k in range(4):
                start = ((z ^ j) * 4 + (p ^ k)) * 48 + core * 24
                out[j, 24 * k : 24 * k + 24, 0:768] = gi[pl.ds(row_of(start), 24), :].astype(BF16)
            start = (z ^ j) * 192 + core * 96
            out[j, :, 768:1664] = go[pl.ds(row_of(start), 96), :].astype(BF16)


def wo_grad_kernel(pos, a0, a1, a2, a3, low, sum_one, sum_two, keep, send, acc):
    z, p, c = place(pos)
    for k, a in enumerate((a0, a1, a2, a3)):
        start = (p ^ k) * 192
        acc[pl.ds(row_of(start), 192), 0:768] = dot(a[...], low[...], TN)
    rows = jnp.concatenate(
        [
            sum_one[2:3, :],
            sum_one[0:1, :],
            sum_two[0:1, :],
            sum_one[1:2, :],
            sum_two[1:2, :],
            sum_two[2:3, :],
            jnp.zeros((122, 768), F32),
        ],
        axis=0,
    )
    acc[:, 768:896] = jnp.transpose(rows)
    for k in range(4):
        for j in range(4):
            for out, core in ((keep, c), (send, 1 - c)):
                start = ((z ^ j) * 4 + (p ^ k)) * 48 + core * 24
                out[k, 24 * j : 24 * j + 24, :] = acc[pl.ds(row_of(start), 24), :].astype(BF16)


def qkv_back_kernel(dq, dmine, dother, wq, i0, i1, i2, i3, low, sums):
    bias_q = jnp.zeros((1, 192), F32)
    bias_v = jnp.zeros((1, 192), F32)
    for k, out in enumerate((i0, i1, i2, i3)):
        grad_q = dq[k]
        grad_kv = dmine[k] + dother[k].astype(F32)
        bias_q += total(grad_q)
        bias_v += total(grad_kv[:, 192:])
        whole = jnp.concatenate([grad_q, grad_kv, jnp.zeros((256, 64), F32)], axis=1).astype(BF16)
        low[k] = whole
        out[...] = dot(whole, wq[...], NT).astype(out.dtype)
    sums[...] = jnp.concatenate(
        [
            jnp.concatenate([bias_q, jnp.zeros((1, 64), F32)], axis=1),
            jnp.concatenate([bias_v, jnp.zeros((1, 64), F32)], axis=1),
            jnp.zeros((6, 256), F32),
        ],
        axis=0,
    )


def qkv_grad_kernel(pos, x0, x1, x2, x3, low, sums, keep, send, acc):
    z, p, c = place(pos)
    acc[...] = sum(dot(x[...], low[k], TN) for k, x in enumerate((x0, x1, x2, x3)))
    rows = jnp.concatenate(
        [jnp.zeros((64, 256), F32), sums[...], jnp.zeros((56, 256), F32)], axis=0
    )
    extra = jnp.transpose(rows)[:192]
    for i in range(4):
        acc[192 * i : 192 * i + 192, 512:640] += extra
    for j in range(4):
        for k in range(4):
            for out, core in ((keep, c), (send, 1 - c)):
                start = ((z ^ j) * 4 + (p ^ k)) * 48 + core * 24
                out[j, 24 * k : 24 * k + 24, :] = acc[pl.ds(row_of(start), 24), :].astype(BF16)


def turned(block):
    n = block.shape[0]
    return jnp.transpose(jnp.concatenate([block, jnp.zeros((128 - n, 128), F32)], axis=0))


def finish_kernel(
    pos, tq, tm, f1, f2, f3, uo, gqkv, gbqv, gwo, gbo, gain, shift, gwin, gbin, gwout, gbout
):
    z, p, c = place(pos)
    gwout[...] = tm[:, 768:1536]
    gbin[...] = turned(tm[:, 1536:1664])[0:1, 0:96]
    gwo[...] = uo[:, 0:768]
    side = turned(uo[:, 768:896])
    gbo[...] = side[0:1, 0:24]
    gain[...] = side[1:3, 0:24]
    shift[...] = side[3:5, 0:24]
    gbout[...] = side[5:6, 0:24]
    for own in range(4):

        @pl.when(p == own)
        def _(own=own):
            biases = jnp.zeros((24, 128), F32)
            for k in range(4):
                chip = own ^ k
                if k == 0:
                    qkv, win = tq[0:24, :], tm[0:24, 0:768]
                else:
                    got = (f1, f2, f3)[k - 1][...].astype(F32)
                    qkv, win = got[:, 0:640], got[:, 640:1408]
                for i in range(3):
                    gqkv[:, 768 * i + 192 * chip : 768 * i + 192 * chip + 192] = qkv[
                        :, 192 * i : 192 * i + 192
                    ]
                for i in range(4):
                    gwin[:, 768 * i + 192 * chip : 768 * i + 192 * chip + 192] = win[
                        :, 192 * i : 192 * i + 192
                    ]
                biases += jnp.where(z == chip, qkv[:, 512:640], 0.0)
            gbqv[...] = turned(biases)[64:66, 0:24]


def chip_swap(value, k):
    return lax.ppermute(value, "seq", [(s, s ^ (2 * k)) for s in range(8)])


def core_swap(value):
    return lax.ppermute(value, "seq", [(s, s ^ 1) for s in range(8)])


def z_swap(value, j):
    return lax.ppermute(value, "dp", [(s, s ^ j) for s in range(4)])


def low_add(*terms):
    return sum(t.astype(F32) for t in terms)


def fast_device(
    tokens,
    doc_ids,
    cotangent,
    w_qkv,
    bias_qv,
    w_o,
    bias_o,
    ln_gain,
    ln_bias,
    w_in,
    bias_in,
    w_out,
    bias_out,
):
    pos = lax.axis_index(("dp", "seq")).astype(jnp.int32).reshape(1)
    others = (1, 2, 3)
    narrow = jnp.concatenate(
        [
            bias_qv,
            bias_o[None],
            ln_gain,
            ln_bias,
            bias_out[None],
            doc_ids[None, :24].astype(BF16),
        ],
        axis=0,
    )
    smalls = jnp.concatenate(
        [
            jnp.pad(narrow, ((0, 0), (0, 72))),
            bias_in[None],
            jnp.zeros((6, 96), BF16),
        ],
        axis=0,
    )
    p0, p1, p2, p3, wx_own = call(
        pack_kernel,
        (pos, w_qkv, w_in, w_out, smalls),
        [sds((24, 1408), BF16)] * 4 + [sds((96, 896), BF16)],
        name="pack",
    )
    got = [p0] + [chip_swap(v, k) for v, k in zip((p1, p2, p3), others)]
    xs = [tokens] + [chip_swap(tokens, k) for k in others]
    first = jnp.concatenate([g[:, :640] for g in got], axis=0)
    first_all = jnp.stack([first] + [z_swap(first, j) for j in others])
    first_other = core_swap(first_all)
    wo_z = jnp.concatenate([w_o] + [z_swap(w_o, j) for j in others], axis=0)
    bulk = jnp.concatenate(
        [jnp.concatenate([g[:, 640:] for g in got], axis=0), wx_own], axis=1
    )
    bulk_all = jnp.stack([bulk] + [z_swap(bulk, j) for j in others])
    bulk_other = core_swap(bulk_all)
    wo_all = jnp.stack([wo_z] + [chip_swap(wo_z, k) for k in others])
    wo_other = core_swap(wo_all)

    q, kv, wq, vecs, nb = call(
        qkv_kernel,
        (pos, first_all, first_other, *xs),
        [
            sds((4, 256, 192), BF16),
            sds((4, 256, 384), BF16),
            sds((768, 640), BF16),
            sds((16, 768), F32),
            sds((1,), jnp.int32),
        ],
        scratch=[pltpu.VMEM((8, 640), F32)],
        smem_out=(4,),
        flops=2 * 1024 * 768 * 640,
        name="qkv",
    )
    kv_other = core_swap(kv)
    *attended, ot, lse = call(
        attention_kernel,
        (pos, nb, q, kv, kv_other),
        [sds((256, 192), BF16)] * 4 + [sds((4, 192, 256), F32), sds((4, 8, 256), F32)],
        scratch=[pltpu.VMEM((8, 256, 384), BF16)],
        smem_in=(0, 1),
        flops=6e9,
        name="attention",
    )
    pieces = [attended[0]] + [chip_swap(attended[k], k) for k in others]
    (wo,) = call(wo_kernel, (pos, wo_all, wo_other), [sds((768, 768), BF16)], name="join_wo")
    hidden, xhat, rstd = call(
        norm_kernel,
        (pos, tokens, *pieces, wo, vecs),
        [sds((256, 768), BF16), sds((256, 768), F32), sds((256, 1), F32)],
        flops=2 * 256 * 768 * 768,
        name="norm_one",
    )
    hs = [hidden] + [chip_swap(hidden, k) for k in others]
    wi, wx, bin_ = call(
        weights_kernel,
        (pos, bulk_all, bulk_other),
        [sds((768, 768), BF16), sds((768, 896), BF16), sds((8, 768), F32)],
        name="join_ff",
    )

    def ff(blocks, dtype):
        per = [sds((256, 768), dtype), sds((256, 768), BF16), sds((256, 768), F32)]
        out = call(
            ff_kernel(len(blocks)),
            (*blocks, wi, wx, bin_),
            per * len(blocks),
            smem_in=(),
            flops=len(blocks) * 4 * 256 * 768 * 768,
            name="ff",
        )
        return [out[3 * i : 3 * i + 3] for i in range(len(blocks))]

    made = ff(hs[:1], F32) + ff(hs[1:], BF16)
    parts = [made[0][0]] + [chip_swap(made[k][0], k) for k in others]
    block_out, grad_two_low, grad_two, sums_two = call(
        norm_two_kernel,
        (vecs, xhat, *parts, cotangent),
        [sds((256, 768), BF16), sds((256, 768), BF16), sds((256, 768), F32), sds((8, 768), F32)],
        smem_in=(),
        flops=1e7,
        name="norm_two",
    )
    gs = [grad_two_low] + [chip_swap(grad_two_low, k) for k in others]

    def ff_back(blocks, slopes, dtype):
        n = len(blocks)
        out = call(
            ff_back_kernel(n),
            (*blocks, *slopes, wi, wx),
            [sds((8, 768), F32)] + [sds((256, 768), dtype), sds((256, 768), BF16)] * n,
            smem_in=(),
            flops=n * 4 * 256 * 768 * 768,
            name="ff_back",
        )
        return out[0], [out[1 + 2 * i : 3 + 2 * i] for i in range(n)]

    sum_a, back_a = ff_back(gs[:1], [made[0][2]], F32)
    sum_b, back_b = ff_back(gs[1:], [m[2] for m in made[1:]], BF16)
    backs = back_a + back_b
    grad_parts = [backs[0][0]] + [chip_swap(backs[k][0], k) for k in others]
    ff_keep, ff_send = call(
        ff_grad_kernel,
        (pos, *hs, *[b[1] for b in backs], *[m[1] for m in made], *gs, sum_a, sum_b),
        [sds((4, 96, 1664), BF16)] * 2,
        scratch=[pltpu.VMEM((768, 768), F32), pltpu.VMEM((768, 896), F32)],
        flops=16 * 256 * 768 * 768,
        name="ff_grad",
    )
    ff_got = core_swap(ff_send)
    ff_sum = [low_add(ff_keep[j], ff_got[j]) for j in range(4)]
    ff_z = [z_swap(ff_sum[j].astype(BF16), j) for j in others]
    tm = low_add(ff_sum[0], *ff_z)

    *grad_att, low_one, grad_one, sums_one = call(
        norm_one_kernel,
        (pos, *grad_parts, grad_two, xhat, rstd, vecs, wo),
        [sds((256, 192), BF16)] * 4
        + [sds((256, 768), BF16), sds((256, 768), F32), sds((8, 768), F32)],
        flops=2 * 256 * 768 * 768,
        name="norm_one_back",
    )
    grad_pieces = [grad_att[0]] + [chip_swap(grad_att[k], k) for k in others]
    wo_keep, wo_send = call(
        wo_grad_kernel,
        (pos, *pieces, low_one, sums_one, sums_two),
        [sds((4, 96, 896), BF16)] * 2,
        scratch=[pltpu.VMEM((768, 896), F32)],
        flops=2 * 256 * 768 * 768,
        name="wo_grad",
    )
    wo_got = core_swap(wo_send)
    wo_sum = [low_add(wo_keep[k], wo_got[k]) for k in range(4)]
    to = low_add(wo_sum[0], *[chip_swap(wo_sum[k].astype(BF16), k) for k in others])
    uo = low_add(
        to[:24], *[z_swap(to[24 * j : 24 * j + 24].astype(BF16), j) for j in others]
    )

    dq, dmine, dother = call(
        attention_back_kernel,
        (pos, nb, q, kv, kv_other, *grad_pieces, ot, lse),
        [sds((4, 256, 192), F32), sds((4, 256, 384), F32), sds((4, 256, 384), BF16)],
        scratch=[pltpu.VMEM((8, 256, 384), BF16), pltpu.VMEM((6, 8, 256, 64), F32)],
        smem_in=(0, 1),
        flops=15e9,
        name="attention_back",
    )
    dgot = core_swap(dother)
    *in_parts, low, sums_qv = call(
        qkv_back_kernel,
        (dq, dmine, dgot, wq),
        [sds((256, 768), F32)]
        + [sds((256, 768), BF16)] * 3
        + [sds((4, 256, 640), BF16), sds((8, 256), F32)],
        smem_in=(),
        flops=2 * 1024 * 768 * 640,
        name="qkv_back",
    )
    in_got = [chip_swap(in_parts[k], k) for k in others]
    input_grad = low_add(in_parts[0], grad_one, *in_got)
    q_keep, q_send = call(
        qkv_grad_kernel,
        (pos, *xs, low, sums_qv),
        [sds((4, 96, 640), BF16)] * 2,
        scratch=[pltpu.VMEM((768, 640), F32)],
        flops=2 * 1024 * 768 * 640,
        name="qkv_grad",
    )
    q_got = core_swap(q_send)
    q_sum = [low_add(q_keep[j], q_got[j]) for j in range(4)]
    tq = low_add(q_sum[0], *[z_swap(q_sum[j].astype(BF16), j) for j in others])
    final = [
        chip_swap(
            jnp.concatenate(
                [tq[24 * k : 24 * k + 24], tm[24 * k : 24 * k + 24, :768]], axis=1
            ).astype(BF16),
            k,
        )
        for k in others
    ]
    gqkv, gbqv, gwo, gbo, gain, shift, gwin, gbin, gwout, gbout = call(
        finish_kernel,
        (pos, tq, tm, *final, uo),
        [
            sds((24, 2304), F32),
            sds((2, 24), F32),
            sds((24, 768), F32),
            sds((1, 24), F32),
            sds((2, 24), F32),
            sds((2, 24), F32),
            sds((24, 3072), F32),
            sds((1, 96), F32),
            sds((96, 768), F32),
            sds((1, 24), F32),
        ],
        name="finish",
    )
    return (
        block_out,
        input_grad,
        gqkv,
        gbqv,
        gwo,
        gbo.reshape(24),
        gain,
        shift,
        gwin,
        gbin.reshape(96),
        gwout,
        gbout.reshape(24),
    )


def layer_norm(resid, gain, shift):
    center = resid - jnp.mean(resid, axis=-1, keepdims=True)
    spread = jnp.mean(center * center, axis=-1, keepdims=True)
    return center * lax.rsqrt(spread + EPSILON) * gain + shift


def exact_gelu(value):
    return jax.nn.gelu(value, approximate=False)


def split_heads(matrix):
    return matrix.reshape(matrix.shape[0], HEADS, HDIM)


def allowed_pairs(query_doc, query_block, key_doc, key_block):
    return (query_doc[:, None] == key_doc[None, :]) & (key_block[None, :] <= query_block[:, None])


def over_parts(carry, arrays, update):
    count = arrays[0].shape[0]
    span = math.gcd(count, 1024)
    steps = count // span
    offsets = jnp.arange(steps, dtype=jnp.int32) * span
    parts = tuple((a.reshape((steps, span) + a.shape[1:]) for a in arrays))

    def inner(state, items):
        return (update(state, items[:-1], items[-1]), None)

    carry, unused = lax.scan(inner, carry, parts + (offsets,))
    return carry


def score_grads(query_heads, grad_heads, log_total, delta, allowed, key_heads, value_heads):
    raw = (
        jnp.einsum("qhd,khd->hqk", query_heads, key_heads, preferred_element_type=jnp.float32)
        * 0.125
    )
    probs = jnp.where(allowed[None], jnp.exp(raw - log_total[:, :, None]), 0.0)
    grad_probs = jnp.einsum(
        "qhd,khd->hqk", grad_heads, value_heads, preferred_element_type=jnp.float32
    )
    grad_scores = (probs * (grad_probs - delta[:, :, None]) * 0.125).astype(jnp.bfloat16)
    grad_query = jnp.einsum(
        "hqk,khd->qhd", grad_scores, key_heads, preferred_element_type=jnp.float32
    )
    grad_key = jnp.einsum(
        "hqk,qhd->khd", grad_scores, query_heads, preferred_element_type=jnp.float32
    )
    grad_value = jnp.einsum(
        "hqk,qhd->khd", probs.astype(jnp.bfloat16), grad_heads, preferred_element_type=jnp.float32
    )
    return (grad_query, grad_key, grad_value)


def on_device(
    tokens,
    doc_ids,
    cotangent,
    w_qkv,
    bias_qv,
    w_o,
    bias_o,
    ln_gain,
    ln_bias,
    w_in,
    bias_in,
    w_out,
    bias_out,
):
    rows = tokens.shape[0]
    width = tokens.shape[1]
    full = (
        lax.all_gather(w_qkv, ("dp", "seq"), axis=0, tiled=True),
        lax.all_gather(bias_qv, ("dp", "seq"), axis=1, tiled=True),
        lax.all_gather(w_o, ("dp", "seq"), axis=0, tiled=True),
        lax.all_gather(bias_o, ("dp", "seq"), axis=0, tiled=True),
        lax.all_gather(ln_gain, ("dp", "seq"), axis=1, tiled=True),
        lax.all_gather(ln_bias, ("dp", "seq"), axis=1, tiled=True),
        lax.all_gather(w_in, ("dp", "seq"), axis=0, tiled=True),
        lax.all_gather(bias_in, ("dp", "seq"), axis=0, tiled=True),
        lax.all_gather(w_out, ("dp", "seq"), axis=0, tiled=True),
        lax.all_gather(bias_out, ("dp", "seq"), axis=0, tiled=True),
    )
    (
        full_qkv,
        full_bias_qv,
        full_o,
        full_bias_o,
        full_gain,
        full_shift,
        full_in,
        full_bias_in,
        full_out,
        full_bias_out,
    ) = full
    positions = lax.axis_index("seq") * rows + jnp.arange(rows, dtype=jnp.int32)
    query_block = positions // BLK
    bias_three = jnp.concatenate(
        [
            full_bias_qv[0].astype(jnp.float32),
            jnp.zeros((width,), jnp.float32),
            full_bias_qv[1].astype(jnp.float32),
        ]
    )
    projected = (jnp.dot(tokens, full_qkv, preferred_element_type=jnp.float32) + bias_three).astype(
        jnp.bfloat16
    )
    queries = projected[:, :width]
    keys = projected[:, width : 2 * width]
    values = projected[:, 2 * width :]
    query_heads = split_heads(queries)

    def forward_update(state, parts, first):
        key_rows, value_rows, key_doc = parts
        count = key_rows.shape[0]
        key_block = (first + jnp.arange(count, dtype=jnp.int32)) // BLK
        allowed = allowed_pairs(doc_ids, query_block, key_doc, key_block)
        raw = (
            jnp.einsum(
                "qhd,khd->hqk",
                query_heads,
                split_heads(key_rows),
                preferred_element_type=jnp.float32,
            )
            * 0.125
        )
        masked = jnp.where(allowed[None], raw, NEG_LARGE)
        top, total, summed = state
        new_top = jnp.maximum(top, jnp.max(masked, axis=-1))
        weights = jnp.where(allowed[None], jnp.exp(masked - new_top[:, :, None]), 0.0)
        factor = jnp.exp(top - new_top)
        total = total * factor + jnp.sum(weights, axis=-1)
        summed = summed * factor[:, :, None] + jnp.einsum(
            "hqk,khd->hqd",
            weights.astype(jnp.bfloat16),
            split_heads(value_rows),
            preferred_element_type=jnp.float32,
        )
        return (new_top, total, summed)

    start_state = (
        jnp.full((HEADS, rows), NEG_LARGE, jnp.float32),
        jnp.zeros((HEADS, rows), jnp.float32),
        jnp.zeros((HEADS, rows, HDIM), jnp.float32),
    )
    top, total, summed = over_parts(
        start_state,
        (
            lax.all_gather(keys, "seq", axis=0, tiled=True),
            lax.all_gather(values, "seq", axis=0, tiled=True),
            lax.all_gather(doc_ids, "seq", axis=0, tiled=True),
        ),
        forward_update,
    )
    attn_heads = summed / total[:, :, None]
    log_total = top + jnp.log(total)
    attended_low = attn_heads.transpose(1, 0, 2).reshape(rows, width).astype(jnp.bfloat16)
    resid_one = (
        tokens.astype(jnp.float32)
        + jnp.dot(attended_low, full_o, preferred_element_type=jnp.float32)
        + full_bias_o.astype(jnp.float32)
    )
    hidden_one, norm_one_pull = jax.vjp(
        layer_norm, resid_one, full_gain[0].astype(jnp.float32), full_shift[0].astype(jnp.float32)
    )
    hidden_low = hidden_one.astype(jnp.bfloat16)
    pre_act = jnp.dot(
        hidden_low, full_in, preferred_element_type=jnp.float32
    ) + full_bias_in.astype(jnp.float32)
    activated, gelu_pull = jax.vjp(exact_gelu, pre_act)
    act_low = activated.astype(jnp.bfloat16)
    resid_two = (
        hidden_one
        + jnp.dot(act_low, full_out, preferred_element_type=jnp.float32)
        + full_bias_out.astype(jnp.float32)
    )
    normed, norm_two_pull = jax.vjp(
        layer_norm, resid_two, full_gain[1].astype(jnp.float32), full_shift[1].astype(jnp.float32)
    )
    block_out = normed.astype(jnp.bfloat16)
    again = (
        lax.all_gather(w_qkv, ("dp", "seq"), axis=0, tiled=True),
        lax.all_gather(bias_qv, ("dp", "seq"), axis=1, tiled=True),
        lax.all_gather(w_o, ("dp", "seq"), axis=0, tiled=True),
        lax.all_gather(bias_o, ("dp", "seq"), axis=0, tiled=True),
        lax.all_gather(ln_gain, ("dp", "seq"), axis=1, tiled=True),
        lax.all_gather(ln_bias, ("dp", "seq"), axis=1, tiled=True),
        lax.all_gather(w_in, ("dp", "seq"), axis=0, tiled=True),
        lax.all_gather(bias_in, ("dp", "seq"), axis=0, tiled=True),
        lax.all_gather(w_out, ("dp", "seq"), axis=0, tiled=True),
        lax.all_gather(bias_out, ("dp", "seq"), axis=0, tiled=True),
    )
    back_qkv = again[0]
    back_o = again[2]
    back_in = again[6]
    back_out = again[8]
    grad_resid_two, grad_gain_two, grad_shift_two = norm_two_pull(cotangent.astype(jnp.float32))
    grad_two_low = grad_resid_two.astype(jnp.bfloat16)
    grad_w_out = jnp.einsum("tf,td->fd", act_low, grad_two_low, preferred_element_type=jnp.float32)
    grad_bias_out = jnp.sum(grad_resid_two, axis=0)
    grad_act = jnp.einsum("td,fd->tf", grad_two_low, back_out, preferred_element_type=jnp.float32)
    (grad_pre,) = gelu_pull(grad_act)
    grad_pre_low = grad_pre.astype(jnp.bfloat16)
    grad_w_in = jnp.einsum(
        "td,tf->df", hidden_low, grad_pre_low, preferred_element_type=jnp.float32
    )
    grad_bias_in = jnp.sum(grad_pre, axis=0)
    grad_hidden = (
        jnp.einsum("tf,df->td", grad_pre_low, back_in, preferred_element_type=jnp.float32)
        + grad_resid_two
    )
    grad_resid_one, grad_gain_one, grad_shift_one = norm_one_pull(grad_hidden)
    grad_one_low = grad_resid_one.astype(jnp.bfloat16)
    grad_w_o = jnp.einsum(
        "te,td->ed", attended_low, grad_one_low, preferred_element_type=jnp.float32
    )
    grad_bias_o = jnp.sum(grad_resid_one, axis=0)
    grad_attn_low = jnp.einsum(
        "td,ed->te", grad_one_low, back_o, preferred_element_type=jnp.float32
    ).astype(jnp.bfloat16)
    grad_heads = split_heads(grad_attn_low)
    delta = jnp.sum(grad_heads.astype(jnp.float32).transpose(1, 0, 2) * attn_heads, axis=-1)
    keys_all, values_all, docs_all = (
        lax.all_gather(keys, "seq", axis=0, tiled=True),
        lax.all_gather(values, "seq", axis=0, tiled=True),
        lax.all_gather(doc_ids, "seq", axis=0, tiled=True),
    )
    length = keys_all.shape[0]
    span = math.gcd(length, 1024)
    steps = length // span
    offsets = jnp.arange(steps, dtype=jnp.int32) * span

    def back_step(grad_query, items):
        key_rows, value_rows, key_doc, first = items
        key_block = (first + jnp.arange(span, dtype=jnp.int32)) // BLK
        allowed = allowed_pairs(doc_ids, query_block, key_doc, key_block)
        part_query, part_key, part_value = score_grads(
            query_heads,
            grad_heads,
            log_total,
            delta,
            allowed,
            split_heads(key_rows),
            split_heads(value_rows),
        )
        return (
            grad_query + part_query,
            (part_key.reshape(span, width), part_value.reshape(span, width)),
        )

    grad_query, (key_terms, value_terms) = lax.scan(
        back_step,
        jnp.zeros((rows, HEADS, HDIM), jnp.float32),
        (
            keys_all.reshape(steps, span, width),
            values_all.reshape(steps, span, width),
            docs_all.reshape(steps, span),
            offsets,
        ),
    )
    grad_keys, grad_values = (
        lax.psum_scatter(
            key_terms.reshape(length, width).astype(jnp.bfloat16),
            "seq",
            scatter_dimension=0,
            tiled=True,
        ).astype(jnp.float32),
        lax.psum_scatter(
            value_terms.reshape(length, width).astype(jnp.bfloat16),
            "seq",
            scatter_dimension=0,
            tiled=True,
        ).astype(jnp.float32),
    )
    grad_queries = grad_query.reshape(rows, width)
    grad_qkv_low = jnp.concatenate([grad_queries, grad_keys, grad_values], axis=1).astype(
        jnp.bfloat16
    )
    grad_w_qkv = jnp.einsum("td,te->de", tokens, grad_qkv_low, preferred_element_type=jnp.float32)
    grad_bias_qv = jnp.stack([jnp.sum(grad_queries, axis=0), jnp.sum(grad_values, axis=0)])
    input_grad = (
        jnp.einsum("te,de->td", grad_qkv_low, back_qkv, preferred_element_type=jnp.float32)
        + grad_resid_one
    )
    grad_gain = jnp.stack([grad_gain_one, grad_gain_two])
    grad_shift = jnp.stack([grad_shift_one, grad_shift_two])
    owned = (
        lax.psum_scatter(grad_w_qkv, ("dp", "seq"), scatter_dimension=0, tiled=True),
        lax.psum_scatter(grad_bias_qv, ("dp", "seq"), scatter_dimension=1, tiled=True),
        lax.psum_scatter(grad_w_o, ("dp", "seq"), scatter_dimension=0, tiled=True),
        lax.psum_scatter(grad_bias_o, ("dp", "seq"), scatter_dimension=0, tiled=True),
        lax.psum_scatter(grad_gain, ("dp", "seq"), scatter_dimension=1, tiled=True),
        lax.psum_scatter(grad_shift, ("dp", "seq"), scatter_dimension=1, tiled=True),
        lax.psum_scatter(grad_w_in, ("dp", "seq"), scatter_dimension=0, tiled=True),
        lax.psum_scatter(grad_bias_in, ("dp", "seq"), scatter_dimension=0, tiled=True),
        lax.psum_scatter(grad_w_out, ("dp", "seq"), scatter_dimension=0, tiled=True),
        lax.psum_scatter(grad_bias_out, ("dp", "seq"), scatter_dimension=0, tiled=True),
    )
    return (
        block_out,
        input_grad,
        owned[0],
        owned[1],
        owned[2],
        owned[3],
        owned[4],
        owned[5],
        owned[6],
        owned[7],
        owned[8],
        owned[9],
    )


def solution(mesh):
    placed = (
        P(("dp", "seq"), None),
        P(("dp", "seq")),
        P(("dp", "seq"), None),
        P(("dp", "seq"), None),
        P(None, ("dp", "seq")),
        P(("dp", "seq"), None),
        P(("dp", "seq")),
        P(None, ("dp", "seq")),
        P(None, ("dp", "seq")),
        P(("dp", "seq"), None),
        P(("dp", "seq")),
        P(("dp", "seq"), None),
        P(("dp", "seq")),
    )
    sizes = dict(mesh.shape)
    fast = sizes["dp"] == 4 and sizes["seq"] == 8
    return jax.shard_map(
        fast_device if fast else on_device,
        mesh=mesh,
        in_specs=placed,
        out_specs=(
            P(("dp", "seq"), None),
            P(("dp", "seq"), None),
            P(("dp", "seq"), None),
            P(None, ("dp", "seq")),
            P(("dp", "seq"), None),
            P(("dp", "seq")),
            P(None, ("dp", "seq")),
            P(None, ("dp", "seq")),
            P(("dp", "seq"), None),
            P(("dp", "seq")),
            P(("dp", "seq"), None),
            P(("dp", "seq")),
        ),
        check_vma=False,
    )
```

```python
import math

import jax
import jax.numpy as jnp
from jax import lax
from jax.experimental import pallas as pl
from jax.experimental.pallas import tpu as pltpu
from jax.sharding import PartitionSpec as P

HEADS = 12
HDIM = 64
BLK = 256


EPSILON = 1e-12
NEG_LARGE = -1e30

F32 = jnp.float32
BF16 = jnp.bfloat16
LOG2E = 1.4426950408889634
NT = (((1,), (1,)), ((), ()))
TN = (((0,), (0,)), ((), ()))
NN = (((1,), (0,)), ((), ()))


def dot(left, right, dims=NN):
    return lax.dot_general(left, right, dims, preferred_element_type=F32)


def sds(shape, dtype):
    return jax.ShapeDtypeStruct(shape, dtype)


def call(kernel, args, outs, scratch=(), smem_in=(0,), smem_out=(), flops=0, name=None):
    space = lambda inside: pl.BlockSpec(memory_space=pltpu.SMEM if inside else pltpu.VMEM)
    nbytes = sum(math.prod(a.shape) * a.dtype.itemsize for a in tuple(args) + tuple(outs))
    return pl.pallas_call(
        kernel,
        out_shape=tuple(outs),
        in_specs=[space(i in smem_in) for i in range(len(args))],
        out_specs=tuple(space(i in smem_out) for i in range(len(outs))),
        scratch_shapes=list(scratch),
        compiler_params=pltpu.CompilerParams(vmem_limit_bytes=16 * 1024 * 1024),
        cost_estimate=pl.CostEstimate(
            flops=int(flops), transcendentals=0, bytes_accessed=int(nbytes)
        ),
        name=name,
    )(*args)


def place(pos):
    d = pos[0]
    return d >> 3, (d >> 1) & 3, d & 1


def row_of(start, size=8):
    return pl.multiple_of(start, size)


def pack_kernel(pos, wqkv, win, wout, smalls, p0, p1, p2, p3, wx):
    z, p, c = place(pos)
    rows = lax.broadcasted_iota(jnp.int32, (96, 96), 0)
    cols = lax.broadcasted_iota(jnp.int32, (96, 96), 1)
    eye = (rows == cols).astype(BF16)
    side = dot(eye, smalls[...], NT).astype(BF16)
    wx[...] = jnp.concatenate([wout[...], side, jnp.zeros((96, 112), BF16)], axis=1)
    small = jnp.concatenate([side[:24], jnp.zeros((24, 48), BF16)], axis=1)

    def piece(chip):
        parts = [wqkv[:, 768 * i + 192 * chip : 768 * i + 192 * chip + 192] for i in range(3)]
        parts.append(small)
        parts += [win[:, 768 * i + 192 * chip : 768 * i + 192 * chip + 192] for i in range(4)]
        return jnp.concatenate(parts, axis=1)

    for own in range(4):

        @pl.when(p == own)
        def _(own=own):
            for k, out in enumerate((p0, p1, p2, p3)):
                out[...] = piece(own ^ k)


def interleave(pos, mine, other, lanes, out, order):
    z, p, c = place(pos)

    def run(first, second):
        for j in range(4):
            for k in range(4):
                at = (j, slice(24 * k, 24 * k + 24), lanes) if order == "jk" else (
                    k, slice(24 * j, 24 * j + 24), lanes)
                block = jnp.concatenate([first[at], second[at]], axis=0)
                start = ((z ^ j) * 4 + (p ^ k)) * 48
                out[pl.ds(row_of(start, 16), 48), :] = block

    @pl.when(c == 0)
    def _():
        run(mine, other)

    @pl.when(c == 1)
    def _():
        run(other, mine)


def qkv_kernel(pos, am, ao, x0, x1, x2, x3, q, kv, wq, vecs, nb, bias):
    z, p, c = place(pos)
    interleave(pos, am, ao, slice(None), wq, "jk")
    flipped = jnp.transpose(wq[:, 512:640].astype(F32))
    vecs[...] = flipped[64:80]
    for own in range(4):

        @pl.when(p == own)
        def _(own=own):
            at = slice(192 * own, 192 * own + 192)
            bias[0:1, :] = jnp.concatenate(
                [vecs[0:1, at], jnp.zeros((1, 192), F32), vecs[1:2, at], jnp.zeros((1, 64), F32)],
                axis=1,
            )

    lane = lax.broadcasted_iota(jnp.int32, (1, 768), 1)
    mask = (lane >= 192 * z) & (lane < 192 * z + 192) & (lane % 24 == 0)
    second = jnp.sum(jnp.where(mask, vecs[8:9, :], 0.0))
    nb[0] = 8 - second.astype(jnp.int32)
    for k, x in enumerate((x0, x1, x2, x3)):
        got = (dot(x[...], wq[...]) + bias[0:1, :]).astype(BF16)
        q[k] = got[:, :192]
        kv[k] = got[:, 192:576]


def weights_kernel(pos, mm, mo, wi, wx, bin_):
    z, p, c = place(pos)
    interleave(pos, mm, mo, slice(0, 768), wi, "jk")
    for j in range(4):
        base = (z ^ j) * 192
        wx[pl.ds(row_of(base + c * 96, 32), 96), :] = mm[j, :, 768:1664]
        wx[pl.ds(row_of(base + (1 - c) * 96, 32), 96), :] = mo[j, :, 768:1664]
    flipped = jnp.transpose(wx[:, 768:896].astype(F32))
    bin_[...] = flipped[8:16]


def wo_kernel(pos, om, oo, wo):
    interleave(pos, om, oo, slice(None), wo, "kj")


def absolute_kv(pos, mine, other, kv):
    z, p, c = place(pos)
    for k in range(4):
        first = 2 * (p ^ k)
        kv[first + c] = mine[k]
        kv[first + 1 - c] = other[k]


def key_range(pos, nb, k):
    z, p, c = place(pos)
    block = 2 * (p ^ k) + c
    return jnp.where(block < nb[0], 0, nb[0]), block + 1


def attention_kernel(pos, nb, q, mine, other, a0, a1, a2, a3, ot, lse, kv):
    scale = 0.125 * LOG2E
    absolute_kv(pos, mine, other, kv)
    for k, out in enumerate((a0, a1, a2, a3)):
        low, high = key_range(pos, nb, k)
        heads = [q[k, :, 64 * h : 64 * h + 64] for h in range(3)]

        def step(kb, state):
            new = []
            for h in range(3):
                top, total, acc = state[h]
                keys = kv[kb, :, 64 * h : 64 * h + 64]
                values = kv[kb, :, 192 + 64 * h : 256 + 64 * h]
                scores = dot(keys, heads[h], NT)
                next_top = jnp.maximum(top, jnp.max(scores, axis=0, keepdims=True))
                weights = jnp.exp2((scores - next_top) * scale)
                factor = jnp.exp2((top - next_top) * scale)
                total = total * factor + jnp.sum(weights, axis=0, keepdims=True)
                acc = acc * factor + dot(values, weights.astype(BF16), TN)
                new.append((next_top, total, acc))
            return tuple(new)

        start = tuple(
            (jnp.full((1, BLK), NEG_LARGE, F32), jnp.zeros((1, BLK), F32), jnp.zeros((HDIM, BLK), F32))
            for _ in range(3)
        )
        state = lax.fori_loop(low, high, step, start)
        done = []
        for h in range(3):
            top, total, acc = state[h]
            mixed = acc / total
            ot[k, 64 * h : 64 * h + 64, :] = mixed
            lse[k, h : h + 1, :] = top * scale + jnp.log(total) * LOG2E
            done.append(mixed)
        out[...] = jnp.transpose(jnp.concatenate(done, axis=0)).astype(BF16)


def attention_back_kernel(
    pos, nb, q, mine, other, g0, g1, g2, g3, ot, lse, dq, dmine, dother, kv, dkv
):
    z, p, c = place(pos)
    scale = 0.125 * LOG2E
    absolute_kv(pos, mine, other, kv)
    dkv[...] = jnp.zeros(dkv.shape, F32)
    for k, grad in enumerate((g0, g1, g2, g3)):
        low, high = key_range(pos, nb, k)
        heads = [q[k, :, 64 * h : 64 * h + 64] for h in range(3)]
        grads = [grad[:, 64 * h : 64 * h + 64] for h in range(3)]
        flipped = jnp.transpose(grad[...].astype(F32))
        product = flipped * ot[k]
        deltas = [
            jnp.sum(product[64 * h : 64 * h + 64], axis=0, keepdims=True) for h in range(3)
        ]
        logs = [lse[k, h : h + 1, :] for h in range(3)]

        def step(kb, state):
            new = []
            for h in range(3):
                keys = kv[kb, :, 64 * h : 64 * h + 64]
                values = kv[kb, :, 192 + 64 * h : 256 + 64 * h]
                probs = jnp.exp2(dot(keys, heads[h], NT) * scale - logs[h])
                dprobs = dot(values, grads[h], NT)
                low_scores = (probs * (dprobs - deltas[h]) * 0.125).astype(BF16)
                dkv[h, kb] += dot(low_scores, heads[h])
                dkv[3 + h, kb] += dot(probs.astype(BF16), grads[h])
                new.append(state[h] + dot(keys, low_scores, TN))
            return tuple(new)

        state = lax.fori_loop(
            low, high, step, tuple(jnp.zeros((HDIM, BLK), F32) for _ in range(3))
        )
        dq[k] = jnp.transpose(jnp.concatenate(state, axis=0))
    for k in range(4):
        first = 2 * (p ^ k)
        dmine[k] = jnp.concatenate([dkv[i, first + c] for i in range(6)], axis=1)
        dother[k] = jnp.concatenate([dkv[i, first + 1 - c] for i in range(6)], axis=1).astype(BF16)


def norm_kernel(pos, tokens, a0, a1, a2, a3, wo, vecs, low, xhat, rstd):
    z, p, c = place(pos)
    resid = tokens[...].astype(F32) + vecs[2:3, :]
    for k, a in enumerate((a0, a1, a2, a3)):
        start = (p ^ k) * 192
        resid += dot(a[...], wo[pl.ds(row_of(start, 64), 192), :])
    center = resid - jnp.mean(resid, axis=-1, keepdims=True)
    scale = lax.rsqrt(jnp.mean(center * center, axis=-1, keepdims=True) + EPSILON)
    hat = center * scale
    xhat[...] = hat
    rstd[...] = scale
    low[...] = (hat * vecs[3:4, :] + vecs[5:6, :]).astype(BF16)


def norm_grad(grad, gain, hat, scale):
    e = grad * gain
    mean_e = jnp.mean(e, axis=-1, keepdims=True)
    mean_x = jnp.mean(e * hat, axis=-1, keepdims=True)
    return scale * (e - mean_e - hat * mean_x)


def total(values):
    return jnp.sum(values, axis=0, keepdims=True)


def norm_two_kernel(vecs, xhat, own, r1, r2, r3, cot, block_out, low, grad_two, sums):
    acc = [jnp.zeros((1, 768), F32) for _ in range(3)]
    for i in range(8):
        at = slice(32 * i, 32 * i + 32)
        hidden = xhat[at, :] * vecs[3:4, :] + vecs[5:6, :]
        resid = hidden + own[at, :] + vecs[7:8, :]
        for r in (r1, r2, r3):
            resid += r[at, :].astype(F32)
        center = resid - jnp.mean(resid, axis=-1, keepdims=True)
        scale = lax.rsqrt(jnp.mean(center * center, axis=-1, keepdims=True) + EPSILON)
        hat = center * scale
        block_out[at, :] = (hat * vecs[4:5, :] + vecs[6:7, :]).astype(BF16)
        grad = cot[at, :].astype(F32)
        back = norm_grad(grad, vecs[4:5, :], hat, scale)
        grad_two[at, :] = back
        low[at, :] = back.astype(BF16)
        acc = [acc[0] + total(grad * hat), acc[1] + total(grad), acc[2] + total(back)]
    sums[...] = jnp.concatenate(acc + [jnp.zeros((5, 768), F32)], axis=0)


def norm_one_kernel(
    pos, own, r1, r2, r3, grad_two, xhat, rstd, vecs, wo, o0, o1, o2, o3, low, grad_one, sums
):
    z, p, c = place(pos)
    acc = [jnp.zeros((1, 768), F32) for _ in range(3)]
    for i in range(8):
        at = slice(32 * i, 32 * i + 32)
        grad = own[at, :] + grad_two[at, :]
        for r in (r1, r2, r3):
            grad += r[at, :].astype(F32)
        hat = xhat[at, :]
        back = norm_grad(grad, vecs[3:4, :], hat, rstd[at, :])
        grad_one[at, :] = back
        low[at, :] = back.astype(BF16)
        acc = [acc[0] + total(grad * hat), acc[1] + total(grad), acc[2] + total(back)]
    sums[...] = jnp.concatenate(acc + [jnp.zeros((5, 768), F32)], axis=0)
    for k, out in enumerate((o0, o1, o2, o3)):
        start = (p ^ k) * 192
        out[...] = dot(low[...], wo[pl.ds(row_of(start, 64), 192), :], NT).astype(BF16)


def ff_kernel(count):
    def kernel(*refs):
        hs = refs[:count]
        wi, wx, bias = refs[count : count + 3]
        outs = refs[count + 3 :]
        for i, h in enumerate(hs):
            part, act, slope = outs[3 * i : 3 * i + 3]
            acc = jnp.zeros((256, 768), F32)
            for f in range(3):
                at = slice(256 * f, 256 * f + 256)
                u = dot(h[...], wi[:, at]) + bias[1:2, at]
                cdf = 0.5 * (1.0 + lax.erf(u * 0.7071067811865476))
                low = (u * cdf).astype(BF16)
                act[:, at] = low
                slope[:, at] = cdf + u * jnp.exp2(u * u * (-0.5 * LOG2E)) * 0.3989422804014327
                acc += dot(low, wx[at, :768])
            part[...] = acc.astype(part.dtype)

    return kernel


def ff_back_kernel(count):
    def kernel(*refs):
        gs = refs[:count]
        slopes = refs[count : 2 * count]
        wi, wx = refs[2 * count : 2 * count + 2]
        sums = refs[2 * count + 2]
        outs = refs[2 * count + 3 :]
        for f in range(3):
            at = slice(256 * f, 256 * f + 256)
            acc = jnp.zeros((1, 256), F32)
            for i in range(count):
                pre = dot(gs[i][...], wx[at, :768], NT) * slopes[i][:, at]
                outs[2 * i + 1][:, at] = pre.astype(BF16)
                acc += total(pre)
            sums[:, at] = jnp.broadcast_to(acc, (8, 256))
        for i in range(count):
            back = dot(outs[2 * i + 1][...], wi[...], NT)
            outs[2 * i][...] = back.astype(outs[2 * i].dtype)

    return kernel


def column_of(row):
    n = row.shape[1]
    first = lax.broadcasted_iota(jnp.int32, (128, n), 0) == 0
    return jnp.transpose(jnp.where(first, jnp.broadcast_to(row, (128, n)), 0.0))


def ff_grad_kernel(*refs):
    pos = refs[0]
    hs, pres, acts, gs = refs[1:5], refs[5:9], refs[9:13], refs[13:17]
    sum_a, sum_b = refs[17:19]
    keep, send, gi, go = refs[19:]
    z, p, c = place(pos)
    gi[...] = sum(dot(hs[k][...], pres[k][...], TN) for k in range(4))
    go[:, :768] = sum(dot(acts[k][...], gs[k][...], TN) for k in range(4))
    go[:, 768:] = column_of(sum_a[0:1, :] + sum_b[0:1, :])
    for j in range(4):
        for out, core in ((keep, c), (send, 1 - c)):
            for k in range(4):
                start = ((z ^ j) * 4 + (p ^ k)) * 48 + core * 24
                out[j, 24 * k : 24 * k + 24, 0:768] = gi[pl.ds(row_of(start), 24), :].astype(BF16)
            start = (z ^ j) * 192 + core * 96
            out[j, :, 768:1664] = go[pl.ds(row_of(start), 96), :].astype(BF16)


def wo_grad_kernel(pos, a0, a1, a2, a3, low, sum_one, sum_two, keep, send, acc):
    z, p, c = place(pos)
    for k, a in enumerate((a0, a1, a2, a3)):
        start = (p ^ k) * 192
        acc[pl.ds(row_of(start), 192), 0:768] = dot(a[...], low[...], TN)
    rows = jnp.concatenate(
        [
            sum_one[2:3, :],
            sum_one[0:1, :],
            sum_two[0:1, :],
            sum_one[1:2, :],
            sum_two[1:2, :],
            sum_two[2:3, :],
            jnp.zeros((122, 768), F32),
        ],
        axis=0,
    )
    acc[:, 768:896] = jnp.transpose(rows)
    for k in range(4):
        for j in range(4):
            for out, core in ((keep, c), (send, 1 - c)):
                start = ((z ^ j) * 4 + (p ^ k)) * 48 + core * 24
                out[k, 24 * j : 24 * j + 24, :] = acc[pl.ds(row_of(start), 24), :].astype(BF16)


def qkv_back_kernel(dq, dmine, dother, wq, i0, i1, i2, i3, low, sums):
    bias_q = jnp.zeros((1, 192), F32)
    bias_v = jnp.zeros((1, 192), F32)
    for k, out in enumerate((i0, i1, i2, i3)):
        grad_q = dq[k]
        grad_kv = dmine[k] + dother[k].astype(F32)
        bias_q += total(grad_q)
        bias_v += total(grad_kv[:, 192:])
        whole = jnp.concatenate([grad_q, grad_kv, jnp.zeros((256, 64), F32)], axis=1).astype(BF16)
        low[k] = whole
        out[...] = dot(whole, wq[...], NT).astype(out.dtype)
    sums[...] = jnp.concatenate(
        [
            jnp.concatenate([bias_q, jnp.zeros((1, 64), F32)], axis=1),
            jnp.concatenate([bias_v, jnp.zeros((1, 64), F32)], axis=1),
            jnp.zeros((6, 256), F32),
        ],
        axis=0,
    )


def qkv_grad_kernel(pos, x0, x1, x2, x3, low, sums, keep, send, acc):
    z, p, c = place(pos)
    acc[...] = sum(dot(x[...], low[k], TN) for k, x in enumerate((x0, x1, x2, x3)))
    rows = jnp.concatenate(
        [jnp.zeros((64, 256), F32), sums[...], jnp.zeros((56, 256), F32)], axis=0
    )
    extra = jnp.transpose(rows)[:192]
    for i in range(4):
        acc[192 * i : 192 * i + 192, 512:640] += extra
    for j in range(4):
        for k in range(4):
            for out, core in ((keep, c), (send, 1 - c)):
                start = ((z ^ j) * 4 + (p ^ k)) * 48 + core * 24
                out[j, 24 * k : 24 * k + 24, :] = acc[pl.ds(row_of(start), 24), :].astype(BF16)


def turned(block):
    n = block.shape[0]
    return jnp.transpose(jnp.concatenate([block, jnp.zeros((128 - n, 128), F32)], axis=0))


def finish_kernel(
    pos, tq, tm, f1, f2, f3, uo, gqkv, gbqv, gwo, gbo, gain, shift, gwin, gbin, gwout, gbout
):
    z, p, c = place(pos)
    gwout[...] = tm[:, 768:1536]
    gbin[...] = turned(tm[:, 1536:1664])[0:1, 0:96]
    gwo[...] = uo[:, 0:768]
    side = turned(uo[:, 768:896])
    gbo[...] = side[0:1, 0:24]
    gain[...] = side[1:3, 0:24]
    shift[...] = side[3:5, 0:24]
    gbout[...] = side[5:6, 0:24]
    for own in range(4):

        @pl.when(p == own)
        def _(own=own):
            biases = jnp.zeros((24, 128), F32)
            for k in range(4):
                chip = own ^ k
                if k == 0:
                    qkv, win = tq[0:24, :], tm[0:24, 0:768]
                else:
                    got = (f1, f2, f3)[k - 1][...].astype(F32)
                    qkv, win = got[:, 0:640], got[:, 640:1408]
                for i in range(3):
                    gqkv[:, 768 * i + 192 * chip : 768 * i + 192 * chip + 192] = qkv[
                        :, 192 * i : 192 * i + 192
                    ]
                for i in range(4):
                    gwin[:, 768 * i + 192 * chip : 768 * i + 192 * chip + 192] = win[
                        :, 192 * i : 192 * i + 192
                    ]
                biases += jnp.where(z == chip, qkv[:, 512:640], 0.0)
            gbqv[...] = turned(biases)[64:66, 0:24]


def chip_swap(value, k):
    return lax.ppermute(value, "seq", [(s, s ^ (2 * k)) for s in range(8)])


def core_swap(value):
    return lax.ppermute(value, "seq", [(s, s ^ 1) for s in range(8)])


def z_swap(value, j):
    return lax.ppermute(value, "dp", [(s, s ^ j) for s in range(4)])


def low_add(*terms):
    return sum(t.astype(F32) for t in terms)


def fast_device(
    tokens,
    doc_ids,
    cotangent,
    w_qkv,
    bias_qv,
    w_o,
    bias_o,
    ln_gain,
    ln_bias,
    w_in,
    bias_in,
    w_out,
    bias_out,
):
    pos = lax.axis_index(("dp", "seq")).astype(jnp.int32).reshape(1)
    others = (1, 2, 3)
    narrow = jnp.concatenate(
        [
            bias_qv,
            bias_o[None],
            ln_gain,
            ln_bias,
            bias_out[None],
            doc_ids[None, :24].astype(BF16),
        ],
        axis=0,
    )
    smalls = jnp.concatenate(
        [
            jnp.pad(narrow, ((0, 0), (0, 72))),
            bias_in[None],
            jnp.zeros((6, 96), BF16),
        ],
        axis=0,
    )
    p0, p1, p2, p3, wx_own = call(
        pack_kernel,
        (pos, w_qkv, w_in, w_out, smalls),
        [sds((24, 1408), BF16)] * 4 + [sds((96, 896), BF16)],
        name="pack",
    )
    got = [p0] + [chip_swap(v, k) for v, k in zip((p1, p2, p3), others)]
    xs = [tokens] + [chip_swap(tokens, k) for k in others]
    first = jnp.concatenate([g[:, :640] for g in got], axis=0)
    first_all = jnp.stack([first] + [z_swap(first, j) for j in others])
    first_other = core_swap(first_all)
    wo_z = jnp.concatenate([w_o] + [z_swap(w_o, j) for j in others], axis=0)
    bulk = jnp.concatenate(
        [jnp.concatenate([g[:, 640:] for g in got], axis=0), wx_own], axis=1
    )
    bulk_all = jnp.stack([bulk] + [z_swap(bulk, j) for j in others])
    bulk_other = core_swap(bulk_all)
    wo_all = jnp.stack([wo_z] + [chip_swap(wo_z, k) for k in others])
    wo_other = core_swap(wo_all)

    q, kv, wq, vecs, nb = call(
        qkv_kernel,
        (pos, first_all, first_other, *xs),
        [
            sds((4, 256, 192), BF16),
            sds((4, 256, 384), BF16),
            sds((768, 640), BF16),
            sds((16, 768), F32),
            sds((1,), jnp.int32),
        ],
        scratch=[pltpu.VMEM((8, 640), F32)],
        smem_out=(4,),
        flops=2 * 1024 * 768 * 640,
        name="qkv",
    )
    kv_other = core_swap(kv)
    *attended, ot, lse = call(
        attention_kernel,
        (pos, nb, q, kv, kv_other),
        [sds((256, 192), BF16)] * 4 + [sds((4, 192, 256), F32), sds((4, 8, 256), F32)],
        scratch=[pltpu.VMEM((8, 256, 384), BF16)],
        smem_in=(0, 1),
        flops=6e9,
        name="attention",
    )
    pieces = [attended[0]] + [chip_swap(attended[k], k) for k in others]
    (wo,) = call(wo_kernel, (pos, wo_all, wo_other), [sds((768, 768), BF16)], name="join_wo")
    hidden, xhat, rstd = call(
        norm_kernel,
        (pos, tokens, *pieces, wo, vecs),
        [sds((256, 768), BF16), sds((256, 768), F32), sds((256, 1), F32)],
        flops=2 * 256 * 768 * 768,
        name="norm_one",
    )
    hs = [hidden] + [chip_swap(hidden, k) for k in others]
    wi, wx, bin_ = call(
        weights_kernel,
        (pos, bulk_all, bulk_other),
        [sds((768, 768), BF16), sds((768, 896), BF16), sds((8, 768), F32)],
        name="join_ff",
    )

    def ff(blocks, dtype):
        per = [sds((256, 768), dtype), sds((256, 768), BF16), sds((256, 768), F32)]
        out = call(
            ff_kernel(len(blocks)),
            (*blocks, wi, wx, bin_),
            per * len(blocks),
            smem_in=(),
            flops=len(blocks) * 4 * 256 * 768 * 768,
            name="ff",
        )
        return [out[3 * i : 3 * i + 3] for i in range(len(blocks))]

    made = ff(hs[:1], F32) + ff(hs[1:], BF16)
    parts = [made[0][0]] + [chip_swap(made[k][0], k) for k in others]
    block_out, grad_two_low, grad_two, sums_two = call(
        norm_two_kernel,
        (vecs, xhat, *parts, cotangent),
        [sds((256, 768), BF16), sds((256, 768), BF16), sds((256, 768), F32), sds((8, 768), F32)],
        smem_in=(),
        flops=1e7,
        name="norm_two",
    )
    gs = [grad_two_low] + [chip_swap(grad_two_low, k) for k in others]

    def ff_back(blocks, slopes, dtype):
        n = len(blocks)
        out = call(
            ff_back_kernel(n),
            (*blocks, *slopes, wi, wx),
            [sds((8, 768), F32)] + [sds((256, 768), dtype), sds((256, 768), BF16)] * n,
            smem_in=(),
            flops=n * 4 * 256 * 768 * 768,
            name="ff_back",
        )
        return out[0], [out[1 + 2 * i : 3 + 2 * i] for i in range(n)]

    sum_a, back_a = ff_back(gs[:1], [made[0][2]], F32)
    sum_b, back_b = ff_back(gs[1:], [m[2] for m in made[1:]], BF16)
    backs = back_a + back_b
    grad_parts = [backs[0][0]] + [chip_swap(backs[k][0], k) for k in others]
    ff_keep, ff_send = call(
        ff_grad_kernel,
        (pos, *hs, *[b[1] for b in backs], *[m[1] for m in made], *gs, sum_a, sum_b),
        [sds((4, 96, 1664), BF16)] * 2,
        scratch=[pltpu.VMEM((768, 768), F32), pltpu.VMEM((768, 896), F32)],
        flops=16 * 256 * 768 * 768,
        name="ff_grad",
    )
    ff_got = core_swap(ff_send)
    ff_sum = [low_add(ff_keep[j], ff_got[j]) for j in range(4)]
    ff_z = [z_swap(ff_sum[j].astype(BF16), j) for j in others]
    tm = low_add(ff_sum[0], *ff_z)

    *grad_att, low_one, grad_one, sums_one = call(
        norm_one_kernel,
        (pos, *grad_parts, grad_two, xhat, rstd, vecs, wo),
        [sds((256, 192), BF16)] * 4
        + [sds((256, 768), BF16), sds((256, 768), F32), sds((8, 768), F32)],
        flops=2 * 256 * 768 * 768,
        name="norm_one_back",
    )
    grad_pieces = [grad_att[0]] + [chip_swap(grad_att[k], k) for k in others]
    wo_keep, wo_send = call(
        wo_grad_kernel,
        (pos, *pieces, low_one, sums_one, sums_two),
        [sds((4, 96, 896), BF16)] * 2,
        scratch=[pltpu.VMEM((768, 896), F32)],
        flops=2 * 256 * 768 * 768,
        name="wo_grad",
    )
    wo_got = core_swap(wo_send)
    wo_sum = [low_add(wo_keep[k], wo_got[k]) for k in range(4)]
    to = low_add(wo_sum[0], *[chip_swap(wo_sum[k].astype(BF16), k) for k in others])
    uo = low_add(
        to[:24], *[z_swap(to[24 * j : 24 * j + 24].astype(BF16), j) for j in others]
    )

    dq, dmine, dother = call(
        attention_back_kernel,
        (pos, nb, q, kv, kv_other, *grad_pieces, ot, lse),
        [sds((4, 256, 192), F32), sds((4, 256, 384), F32), sds((4, 256, 384), BF16)],
        scratch=[pltpu.VMEM((8, 256, 384), BF16), pltpu.VMEM((6, 8, 256, 64), F32)],
        smem_in=(0, 1),
        flops=15e9,
        name="attention_back",
    )
    dgot = core_swap(dother)
    *in_parts, low, sums_qv = call(
        qkv_back_kernel,
        (dq, dmine, dgot, wq),
        [sds((256, 768), F32)]
        + [sds((256, 768), BF16)] * 3
        + [sds((4, 256, 640), BF16), sds((8, 256), F32)],
        smem_in=(),
        flops=2 * 1024 * 768 * 640,
        name="qkv_back",
    )
    in_got = [chip_swap(in_parts[k], k) for k in others]
    input_grad = low_add(in_parts[0], grad_one, *in_got)
    q_keep, q_send = call(
        qkv_grad_kernel,
        (pos, *xs, low, sums_qv),
        [sds((4, 96, 640), BF16)] * 2,
        scratch=[pltpu.VMEM((768, 640), F32)],
        flops=2 * 1024 * 768 * 640,
        name="qkv_grad",
    )
    q_got = core_swap(q_send)
    q_sum = [low_add(q_keep[j], q_got[j]) for j in range(4)]
    tq = low_add(q_sum[0], *[z_swap(q_sum[j].astype(BF16), j) for j in others])
    final = [
        chip_swap(
            jnp.concatenate(
                [tq[24 * k : 24 * k + 24], tm[24 * k : 24 * k + 24, :768]], axis=1
            ).astype(BF16),
            k,
        )
        for k in others
    ]
    gqkv, gbqv, gwo, gbo, gain, shift, gwin, gbin, gwout, gbout = call(
        finish_kernel,
        (pos, tq, tm, *final, uo),
        [
            sds((24, 2304), F32),
            sds((2, 24), F32),
            sds((24, 768), F32),
            sds((1, 24), F32),
            sds((2, 24), F32),
            sds((2, 24), F32),
            sds((24, 3072), F32),
            sds((1, 96), F32),
            sds((96, 768), F32),
            sds((1, 24), F32),
        ],
        name="finish",
    )
    return (
        block_out,
        input_grad,
        gqkv,
        gbqv,
        gwo,
        gbo.reshape(24),
        gain,
        shift,
        gwin,
        gbin.reshape(96),
        gwout,
        gbout.reshape(24),
    )


def layer_norm(resid, gain, shift):
    center = resid - jnp.mean(resid, axis=-1, keepdims=True)
    spread = jnp.mean(center * center, axis=-1, keepdims=True)
    return center * lax.rsqrt(spread + EPSILON) * gain + shift


def exact_gelu(value):
    return jax.nn.gelu(value, approximate=False)


def split_heads(matrix):
    return matrix.reshape(matrix.shape[0], HEADS, HDIM)


def allowed_pairs(query_doc, query_block, key_doc, key_block):
    return (query_doc[:, None] == key_doc[None, :]) & (key_block[None, :] <= query_block[:, None])


def over_parts(carry, arrays, update):
    count = arrays[0].shape[0]
    span = math.gcd(count, 1024)
    steps = count // span
    offsets = jnp.arange(steps, dtype=jnp.int32) * span
    parts = tuple((a.reshape((steps, span) + a.shape[1:]) for a in arrays))

    def inner(state, items):
        return (update(state, items[:-1], items[-1]), None)

    carry, unused = lax.scan(inner, carry, parts + (offsets,))
    return carry


def score_grads(query_heads, grad_heads, log_total, delta, allowed, key_heads, value_heads):
    raw = (
        jnp.einsum("qhd,khd->hqk", query_heads, key_heads, preferred_element_type=jnp.float32)
        * 0.125
    )
    probs = jnp.where(allowed[None], jnp.exp(raw - log_total[:, :, None]), 0.0)
    grad_probs = jnp.einsum(
        "qhd,khd->hqk", grad_heads, value_heads, preferred_element_type=jnp.float32
    )
    grad_scores = (probs * (grad_probs - delta[:, :, None]) * 0.125).astype(jnp.bfloat16)
    grad_query = jnp.einsum(
        "hqk,khd->qhd", grad_scores, key_heads, preferred_element_type=jnp.float32
    )
    grad_key = jnp.einsum(
        "hqk,qhd->khd", grad_scores, query_heads, preferred_element_type=jnp.float32
    )
    grad_value = jnp.einsum(
        "hqk,qhd->khd", probs.astype(jnp.bfloat16), grad_heads, preferred_element_type=jnp.float32
    )
    return (grad_query, grad_key, grad_value)


def on_device(
    tokens,
    doc_ids,
    cotangent,
    w_qkv,
    bias_qv,
    w_o,
    bias_o,
    ln_gain,
    ln_bias,
    w_in,
    bias_in,
    w_out,
    bias_out,
):
    rows = tokens.shape[0]
    width = tokens.shape[1]
    full = (
        lax.all_gather(w_qkv, ("dp", "seq"), axis=0, tiled=True),
        lax.all_gather(bias_qv, ("dp", "seq"), axis=1, tiled=True),
        lax.all_gather(w_o, ("dp", "seq"), axis=0, tiled=True),
        lax.all_gather(bias_o, ("dp", "seq"), axis=0, tiled=True),
        lax.all_gather(ln_gain, ("dp", "seq"), axis=1, tiled=True),
        lax.all_gather(ln_bias, ("dp", "seq"), axis=1, tiled=True),
        lax.all_gather(w_in, ("dp", "seq"), axis=0, tiled=True),
        lax.all_gather(bias_in, ("dp", "seq"), axis=0, tiled=True),
        lax.all_gather(w_out, ("dp", "seq"), axis=0, tiled=True),
        lax.all_gather(bias_out, ("dp", "seq"), axis=0, tiled=True),
    )
    (
        full_qkv,
        full_bias_qv,
        full_o,
        full_bias_o,
        full_gain,
        full_shift,
        full_in,
        full_bias_in,
        full_out,
        full_bias_out,
    ) = full
    positions = lax.axis_index("seq") * rows + jnp.arange(rows, dtype=jnp.int32)
    query_block = positions // BLK
    bias_three = jnp.concatenate(
        [
            full_bias_qv[0].astype(jnp.float32),
            jnp.zeros((width,), jnp.float32),
            full_bias_qv[1].astype(jnp.float32),
        ]
    )
    projected = (jnp.dot(tokens, full_qkv, preferred_element_type=jnp.float32) + bias_three).astype(
        jnp.bfloat16
    )
    queries = projected[:, :width]
    keys = projected[:, width : 2 * width]
    values = projected[:, 2 * width :]
    query_heads = split_heads(queries)

    def forward_update(state, parts, first):
        key_rows, value_rows, key_doc = parts
        count = key_rows.shape[0]
        key_block = (first + jnp.arange(count, dtype=jnp.int32)) // BLK
        allowed = allowed_pairs(doc_ids, query_block, key_doc, key_block)
        raw = (
            jnp.einsum(
                "qhd,khd->hqk",
                query_heads,
                split_heads(key_rows),
                preferred_element_type=jnp.float32,
            )
            * 0.125
        )
        masked = jnp.where(allowed[None], raw, NEG_LARGE)
        top, total, summed = state
        new_top = jnp.maximum(top, jnp.max(masked, axis=-1))
        weights = jnp.where(allowed[None], jnp.exp(masked - new_top[:, :, None]), 0.0)
        factor = jnp.exp(top - new_top)
        total = total * factor + jnp.sum(weights, axis=-1)
        summed = summed * factor[:, :, None] + jnp.einsum(
            "hqk,khd->hqd",
            weights.astype(jnp.bfloat16),
            split_heads(value_rows),
            preferred_element_type=jnp.float32,
        )
        return (new_top, total, summed)

    start_state = (
        jnp.full((HEADS, rows), NEG_LARGE, jnp.float32),
        jnp.zeros((HEADS, rows), jnp.float32),
        jnp.zeros((HEADS, rows, HDIM), jnp.float32),
    )
    top, total, summed = over_parts(
        start_state,
        (
            lax.all_gather(keys, "seq", axis=0, tiled=True),
            lax.all_gather(values, "seq", axis=0, tiled=True),
            lax.all_gather(doc_ids, "seq", axis=0, tiled=True),
        ),
        forward_update,
    )
    attn_heads = summed / total[:, :, None]
    log_total = top + jnp.log(total)
    attended_low = attn_heads.transpose(1, 0, 2).reshape(rows, width).astype(jnp.bfloat16)
    resid_one = (
        tokens.astype(jnp.float32)
        + jnp.dot(attended_low, full_o, preferred_element_type=jnp.float32)
        + full_bias_o.astype(jnp.float32)
    )
    hidden_one, norm_one_pull = jax.vjp(
        layer_norm, resid_one, full_gain[0].astype(jnp.float32), full_shift[0].astype(jnp.float32)
    )
    hidden_low = hidden_one.astype(jnp.bfloat16)
    pre_act = jnp.dot(
        hidden_low, full_in, preferred_element_type=jnp.float32
    ) + full_bias_in.astype(jnp.float32)
    activated, gelu_pull = jax.vjp(exact_gelu, pre_act)
    act_low = activated.astype(jnp.bfloat16)
    resid_two = (
        hidden_one
        + jnp.dot(act_low, full_out, preferred_element_type=jnp.float32)
        + full_bias_out.astype(jnp.float32)
    )
    normed, norm_two_pull = jax.vjp(
        layer_norm, resid_two, full_gain[1].astype(jnp.float32), full_shift[1].astype(jnp.float32)
    )
    block_out = normed.astype(jnp.bfloat16)
    again = (
        lax.all_gather(w_qkv, ("dp", "seq"), axis=0, tiled=True),
        lax.all_gather(bias_qv, ("dp", "seq"), axis=1, tiled=True),
        lax.all_gather(w_o, ("dp", "seq"), axis=0, tiled=True),
        lax.all_gather(bias_o, ("dp", "seq"), axis=0, tiled=True),
        lax.all_gather(ln_gain, ("dp", "seq"), axis=1, tiled=True),
        lax.all_gather(ln_bias, ("dp", "seq"), axis=1, tiled=True),
        lax.all_gather(w_in, ("dp", "seq"), axis=0, tiled=True),
        lax.all_gather(bias_in, ("dp", "seq"), axis=0, tiled=True),
        lax.all_gather(w_out, ("dp", "seq"), axis=0, tiled=True),
        lax.all_gather(bias_out, ("dp", "seq"), axis=0, tiled=True),
    )
    back_qkv = again[0]
    back_o = again[2]
    back_in = again[6]
    back_out = again[8]
    grad_resid_two, grad_gain_two, grad_shift_two = norm_two_pull(cotangent.astype(jnp.float32))
    grad_two_low = grad_resid_two.astype(jnp.bfloat16)
    grad_w_out = jnp.einsum("tf,td->fd", act_low, grad_two_low, preferred_element_type=jnp.float32)
    grad_bias_out = jnp.sum(grad_resid_two, axis=0)
    grad_act = jnp.einsum("td,fd->tf", grad_two_low, back_out, preferred_element_type=jnp.float32)
    (grad_pre,) = gelu_pull(grad_act)
    grad_pre_low = grad_pre.astype(jnp.bfloat16)
    grad_w_in = jnp.einsum(
        "td,tf->df", hidden_low, grad_pre_low, preferred_element_type=jnp.float32
    )
    grad_bias_in = jnp.sum(grad_pre, axis=0)
    grad_hidden = (
        jnp.einsum("tf,df->td", grad_pre_low, back_in, preferred_element_type=jnp.float32)
        + grad_resid_two
    )
    grad_resid_one, grad_gain_one, grad_shift_one = norm_one_pull(grad_hidden)
    grad_one_low = grad_resid_one.astype(jnp.bfloat16)
    grad_w_o = jnp.einsum(
        "te,td->ed", attended_low, grad_one_low, preferred_element_type=jnp.float32
    )
    grad_bias_o = jnp.sum(grad_resid_one, axis=0)
    grad_attn_low = jnp.einsum(
        "td,ed->te", grad_one_low, back_o, preferred_element_type=jnp.float32
    ).astype(jnp.bfloat16)
    grad_heads = split_heads(grad_attn_low)
    delta = jnp.sum(grad_heads.astype(jnp.float32).transpose(1, 0, 2) * attn_heads, axis=-1)
    keys_all, values_all, docs_all = (
        lax.all_gather(keys, "seq", axis=0, tiled=True),
        lax.all_gather(values, "seq", axis=0, tiled=True),
        lax.all_gather(doc_ids, "seq", axis=0, tiled=True),
    )
    length = keys_all.shape[0]
    span = math.gcd(length, 1024)
    steps = length // span
    offsets = jnp.arange(steps, dtype=jnp.int32) * span

    def back_step(grad_query, items):
        key_rows, value_rows, key_doc, first = items
        key_block = (first + jnp.arange(span, dtype=jnp.int32)) // BLK
        allowed = allowed_pairs(doc_ids, query_block, key_doc, key_block)
        part_query, part_key, part_value = score_grads(
            query_heads,
            grad_heads,
            log_total,
            delta,
            allowed,
            split_heads(key_rows),
            split_heads(value_rows),
        )
        return (
            grad_query + part_query,
            (part_key.reshape(span, width), part_value.reshape(span, width)),
        )

    grad_query, (key_terms, value_terms) = lax.scan(
        back_step,
        jnp.zeros((rows, HEADS, HDIM), jnp.float32),
        (
            keys_all.reshape(steps, span, width),
            values_all.reshape(steps, span, width),
            docs_all.reshape(steps, span),
            offsets,
        ),
    )
    grad_keys, grad_values = (
        lax.psum_scatter(
            key_terms.reshape(length, width).astype(jnp.bfloat16),
            "seq",
            scatter_dimension=0,
            tiled=True,
        ).astype(jnp.float32),
        lax.psum_scatter(
            value_terms.reshape(length, width).astype(jnp.bfloat16),
            "seq",
            scatter_dimension=0,
            tiled=True,
        ).astype(jnp.float32),
    )
    grad_queries = grad_query.reshape(rows, width)
    grad_qkv_low = jnp.concatenate([grad_queries, grad_keys, grad_values], axis=1).astype(
        jnp.bfloat16
    )
    grad_w_qkv = jnp.einsum("td,te->de", tokens, grad_qkv_low, preferred_element_type=jnp.float32)
    grad_bias_qv = jnp.stack([jnp.sum(grad_queries, axis=0), jnp.sum(grad_values, axis=0)])
    input_grad = (
        jnp.einsum("te,de->td", grad_qkv_low, back_qkv, preferred_element_type=jnp.float32)
        + grad_resid_one
    )
    grad_gain = jnp.stack([grad_gain_one, grad_gain_two])
    grad_shift = jnp.stack([grad_shift_one, grad_shift_two])
    owned = (
        lax.psum_scatter(grad_w_qkv, ("dp", "seq"), scatter_dimension=0, tiled=True),
        lax.psum_scatter(grad_bias_qv, ("dp", "seq"), scatter_dimension=1, tiled=True),
        lax.psum_scatter(grad_w_o, ("dp", "seq"), scatter_dimension=0, tiled=True),
        lax.psum_scatter(grad_bias_o, ("dp", "seq"), scatter_dimension=0, tiled=True),
        lax.psum_scatter(grad_gain, ("dp", "seq"), scatter_dimension=1, tiled=True),
        lax.psum_scatter(grad_shift, ("dp", "seq"), scatter_dimension=1, tiled=True),
        lax.psum_scatter(grad_w_in, ("dp", "seq"), scatter_dimension=0, tiled=True),
        lax.psum_scatter(grad_bias_in, ("dp", "seq"), scatter_dimension=0, tiled=True),
        lax.psum_scatter(grad_w_out, ("dp", "seq"), scatter_dimension=0, tiled=True),
        lax.psum_scatter(grad_bias_out, ("dp", "seq"), scatter_dimension=0, tiled=True),
    )
    return (
        block_out,
        input_grad,
        owned[0],
        owned[1],
        owned[2],
        owned[3],
        owned[4],
        owned[5],
        owned[6],
        owned[7],
        owned[8],
        owned[9],
    )


def solution(mesh):
    placed = (
        P(("dp", "seq"), None),
        P(("dp", "seq")),
        P(("dp", "seq"), None),
        P(("dp", "seq"), None),
        P(None, ("dp", "seq")),
        P(("dp", "seq"), None),
        P(("dp", "seq")),
        P(None, ("dp", "seq")),
        P(None, ("dp", "seq")),
        P(("dp", "seq"), None),
        P(("dp", "seq")),
        P(("dp", "seq"), None),
        P(("dp", "seq")),
    )
    sizes = dict(mesh.shape)
    fast = sizes["dp"] == 4 and sizes["seq"] == 8
    return jax.shard_map(
        fast_device if fast else on_device,
        mesh=mesh,
        in_specs=placed,
        out_specs=(
            P(("dp", "seq"), None),
            P(("dp", "seq"), None),
            P(("dp", "seq"), None),
            P(None, ("dp", "seq")),
            P(("dp", "seq"), None),
            P(("dp", "seq")),
            P(None, ("dp", "seq")),
            P(None, ("dp", "seq")),
            P(("dp", "seq"), None),
            P(("dp", "seq")),
            P(("dp", "seq"), None),
            P(("dp", "seq")),
        ),
        check_vma=False,
    )
```

```python
import math

import jax
import jax.numpy as jnp
from jax import lax
from jax.experimental import pallas as pl
from jax.experimental.pallas import tpu as pltpu
from jax.sharding import PartitionSpec as P

HEADS = 12
HDIM = 64
BLK = 256


EPSILON = 1e-12
NEG_LARGE = -1e30

F32 = jnp.float32
BF16 = jnp.bfloat16
LOG2E = 1.4426950408889634
NT = (((1,), (1,)), ((), ()))
TN = (((0,), (0,)), ((), ()))
NN = (((1,), (0,)), ((), ()))


def dot(left, right, dims=NN):
    return lax.dot_general(left, right, dims, preferred_element_type=F32)


def sds(shape, dtype):
    return jax.ShapeDtypeStruct(shape, dtype)


def call(kernel, args, outs, scratch=(), smem_in=(0,), smem_out=(), flops=1, name=None):
    space = lambda inside: pl.BlockSpec(memory_space=pltpu.SMEM if inside else pltpu.VMEM)
    return pl.pallas_call(
        kernel,
        out_shape=tuple(outs),
        in_specs=[space(i in smem_in) for i in range(len(args))],
        out_specs=tuple(space(i in smem_out) for i in range(len(outs))),
        scratch_shapes=list(scratch),
        compiler_params=pltpu.CompilerParams(vmem_limit_bytes=16 * 1024 * 1024),
        cost_estimate=pl.CostEstimate(flops=int(flops), transcendentals=0, bytes_accessed=1),
        name=name,
    )(*args)


def place(pos):
    d = pos[0]
    return d >> 3, (d >> 1) & 3, d & 1


def row_of(start, size=8):
    return pl.multiple_of(start, size)


def pack_kernel(wqkv, wo, wout, smalls, zq, zw):
    rows = lax.broadcasted_iota(jnp.int32, (96, 96), 0)
    cols = lax.broadcasted_iota(jnp.int32, (96, 96), 1)
    eye = (rows == cols).astype(BF16)
    side = dot(eye, smalls[...], NT).astype(BF16)
    side = jnp.concatenate([side, jnp.zeros((96, 112), BF16)], axis=1)
    zw[:, 0:768] = wout[...]
    zw[:, 768:896] = side
    zq[:, 0:2304] = wqkv[...]
    zq[:, 2304:3072] = wo[...]
    zq[:, 3072:3200] = side[:24]


def each_chip(p, run):
    for own in range(4):

        @pl.when(p == own)
        def _(own=own):
            run(own)


def split_qkv_kernel(pos, z0, z1, z2, z3, p0, p1, p2, p3, wo):
    z, p, c = place(pos)
    for i, zq in enumerate((z0, z1, z2, z3)):
        wo[24 * i : 24 * i + 24, :] = zq[:, 2304:3072]

    def run(own):
        for k, out in enumerate((p0, p1, p2, p3)):
            at = 192 * (own ^ k)
            for i, zq in enumerate((z0, z1, z2, z3)):
                parts = [zq[:, 768 * t + at : 768 * t + at + 192] for t in range(3)]
                parts.append(zq[:, 3072:3136])
                out[24 * i : 24 * i + 24, :] = jnp.concatenate(parts, axis=1)

    each_chip(p, run)


def split_in_kernel(pos, z0, z1, mine, theirs):
    z, p, c = place(pos)
    for side in range(2):

        @pl.when((z & 1) == side)
        def _(side=side):
            for out, g in ((mine, side), (theirs, 1 - side)):
                for i, zi in enumerate((z0, z1)):
                    at = slice(24 * i, 24 * i + 24)
                    out[at, 0:768] = zi[:, 768 * g : 768 * g + 768]
                    out[at, 768:1536] = zi[:, 768 * g + 1536 : 768 * g + 2304]


SLOTS = (0, 2, 1, 3)


def interleave(pos, mine, other, out, slots):
    z, p, c = place(pos)

    def run(first, second):
        for k in range(4):
            for i in range(4):
                at = (k, slice(24 * i, 24 * i + 24), slice(None))
                block = jnp.concatenate([first[at], second[at]], axis=0)
                plane = z ^ slots[i]
                out[pl.ds(row_of((4 * plane + (p ^ k)) * 48, 16), 48), :] = block

    @pl.when(c == 0)
    def _():
        run(mine, other)

    @pl.when(c == 1)
    def _():
        run(other, mine)


def qkv_kernel(pos, am, ao, x0, x1, x2, x3, q, kv, wq, vecs, nb, bias):
    z, p, c = place(pos)
    interleave(pos, am, ao, wq, (0, 1, 2, 3))
    flipped = jnp.transpose(wq[:, 512:640].astype(F32))
    vecs[...] = flipped[64:80]

    def run(own):
        at = slice(192 * own, 192 * own + 192)
        bias[0:1, :] = jnp.concatenate(
            [vecs[0:1, at], jnp.zeros((1, 192), F32), vecs[1:2, at], jnp.zeros((1, 64), F32)],
            axis=1,
        )

    each_chip(p, run)
    lane = lax.broadcasted_iota(jnp.int32, (1, 768), 1)
    mask = (lane >= 192 * z) & (lane < 192 * z + 192) & (lane % 24 == 0)
    second = jnp.sum(jnp.where(mask, vecs[8:9, :], 0.0))
    nb[0] = 8 - second.astype(jnp.int32)
    for k, x in enumerate((x0, x1, x2, x3)):
        got = (dot(x[...], wq[...]) + bias[0:1, :]).astype(BF16)
        pad = jnp.zeros((got.shape[0], 64), BF16)
        q[k] = jnp.concatenate([got[:, :192], pad], axis=1)
        kv[k] = jnp.concatenate([got[:, 192:384], pad, got[:, 384:576], pad], axis=1)


def join_in_kernel(pos, im, io, wi):
    interleave(pos, im, io, wi, SLOTS)


def join_wo_kernel(pos, om, oo, wo):
    interleave(pos, om, oo, wo, (0, 1, 2, 3))


def join_out_kernel(pos, wm, wo_, wx, bin_):
    z, p, c = place(pos)
    for k in range(4):
        for i in range(2):
            start = (((z ^ (2 * i)) >> 1) * 4 + (p ^ SLOTS[k])) * 192
            at = (k, slice(96 * i, 96 * i + 96), slice(None))
            wx[pl.ds(row_of(start + c * 96, 32), 96), :] = wm[at]
            wx[pl.ds(row_of(start + (1 - c) * 96, 32), 96), :] = wo_[at]
    flipped = jnp.transpose(wx[:, 768:896].astype(F32))
    bin_[...] = flipped[8:16]


def key_range(pos, nb, k):
    z, p, c = place(pos)
    block = 2 * (p ^ k) + c
    return jnp.where(block < nb[0], 0, nb[0]), block + 1


def absolute_keys(pos, mine, other, keys, values, key_t, value_t):
    z, p, c = place(pos)
    for k in range(4):
        for ref, core in ((mine, c), (other, 1 - c)):
            at = 2 * (p ^ k) + core
            keys[at] = ref[k, :, 0:256]
            values[at] = ref[k, :, 256:512]
            if key_t is not None:
                key_t[at] = jnp.transpose(ref[k, :, 0:256])[:192] * 0.125
            if value_t is not None:
                value_t[at] = jnp.transpose(ref[k, :, 256:512])[:192]


def masked_heads(block):
    lane = lax.broadcasted_iota(jnp.int32, (256, 128), 1)
    zero = jnp.zeros((256, 128), block.dtype)
    return (
        jnp.where(lane < 64, block[:, 0:128], zero),
        jnp.where(lane >= 64, block[:, 0:128], zero),
        block[:, 128:256],
    )


GROUPS = (slice(0, 128), slice(0, 128), slice(128, 256))


def attention_kernel(pos, nb, q, mine, other, a0, a1, a2, a3, ot, lse, keys, values, value_t):
    scale = 0.125 * LOG2E
    absolute_keys(pos, mine, other, keys, values, None, value_t)
    for k, out in enumerate((a0, a1, a2, a3)):
        low, high = key_range(pos, nb, k)
        heads = masked_heads(q[k])

        def step(i, state):
            kb = low + 2 * i
            more = jnp.minimum(kb + 1, 7)
            valid = kb + 1 < high
            new = []
            scores = []
            for h in range(3):
                one = dot(keys[kb, :, GROUPS[h]], heads[h], NT)
                two = dot(keys[more, :, GROUPS[h]], heads[h], NT)
                scores.append((one, jnp.where(valid, two, NEG_LARGE)))
            for h in range(3):
                top, total, acc = state[h]
                one, two = scores[h]
                peak = jnp.max(jnp.maximum(one, two), axis=0, keepdims=True)
                next_top = jnp.maximum(top, peak * scale)
                one = jnp.exp2(one * scale - next_top)
                two = jnp.exp2(two * scale - next_top)
                factor = jnp.exp2(top - next_top)
                total = total * factor + jnp.sum(one + two, axis=0, keepdims=True)
                at = slice(64 * h, 64 * h + 64)
                acc = acc * factor + (
                    dot(value_t[kb, at, :], one.astype(BF16))
                    + dot(value_t[more, at, :], two.astype(BF16))
                )
                new.append((next_top, total, acc))
            return tuple(new)

        start = tuple(
            (jnp.full((1, BLK), NEG_LARGE, F32), jnp.zeros((1, BLK), F32), jnp.zeros((HDIM, BLK), F32))
            for _ in range(3)
        )
        state = lax.fori_loop(0, (high - low + 1) >> 1, step, start)
        done = []
        for h in range(3):
            top, total, acc = state[h]
            mixed = acc / total
            ot[k, 64 * h : 64 * h + 64, :] = mixed
            lse[k, h : h + 1, :] = top + jnp.log(total) * LOG2E
            done.append(mixed)
        out[...] = jnp.transpose(jnp.concatenate(done, axis=0)).astype(BF16)


def attention_back_kernel(
    pos, nb, q, mine, other, g0, g1, g2, g3, ot, lse, dq, dmine, dother, keys, values, key_t, dk, dv
):
    z, p, c = place(pos)
    scale = 0.125 * LOG2E
    absolute_keys(pos, mine, other, keys, values, key_t, None)
    dk[...] = jnp.zeros(dk.shape, F32)
    dv[...] = jnp.zeros(dv.shape, F32)
    for k, grad in enumerate((g0, g1, g2, g3)):
        low, high = key_range(pos, nb, k)
        heads = masked_heads(q[k])
        padded = jnp.concatenate([grad[...], jnp.zeros((256, 64), BF16)], axis=1)
        grads = masked_heads(padded)
        flipped = jnp.transpose(grad[...].astype(F32))
        product = flipped * ot[k]
        deltas = [
            jnp.sum(product[64 * h : 64 * h + 64], axis=0, keepdims=True) for h in range(3)
        ]
        logs = [lse[k, h : h + 1, :] for h in range(3)]
        pair_q = jnp.concatenate([heads[0], heads[1]], axis=0) * 0.125
        small_q = heads[2] * 0.125
        pair_g = jnp.concatenate([grads[0], grads[1]], axis=0)

        def step(kb, state):
            new, probs_low, scores_low = [], [], []
            for h in range(3):
                probs = jnp.exp2(dot(keys[kb, :, GROUPS[h]], heads[h], NT) * scale - logs[h])
                dprobs = dot(values[kb, :, GROUPS[h]], grads[h], NT)
                probs_low.append(probs.astype(BF16))
                scores_low.append((probs * (dprobs - deltas[h])).astype(BF16))
            for h in range(3):
                new.append(state[h] + dot(key_t[kb, 64 * h : 64 * h + 64, :], scores_low[h]))
            for ref, lows, pair, one in (
                (dk, scores_low, pair_q, small_q),
                (dv, probs_low, pair_g, grads[2]),
            ):
                ref[kb, :, 0:128] += dot(jnp.concatenate(lows[:2], axis=1), pair)
                ref[kb, :, 128:256] += dot(lows[2], one)
            return tuple(new)

        state = lax.fori_loop(
            low, high, step, tuple(jnp.zeros((HDIM, BLK), F32) for _ in range(3))
        )
        dq[k] = jnp.transpose(jnp.concatenate(state, axis=0))
    for k in range(4):
        at = 2 * (p ^ k)
        dmine[k] = jnp.concatenate([dk[at + c], dv[at + c]], axis=1)
        dother[k] = jnp.concatenate([dk[at + 1 - c], dv[at + 1 - c]], axis=1).astype(BF16)


def norm_kernel(pos, tokens, a0, a1, a2, a3, wo, vecs, low, xhat, rstd):
    z, p, c = place(pos)
    resid = tokens[...].astype(F32) + vecs[2:3, :]
    for k, a in enumerate((a0, a1, a2, a3)):
        start = (p ^ k) * 192
        resid += dot(a[...], wo[pl.ds(row_of(start, 64), 192), :])
    center = resid - jnp.mean(resid, axis=-1, keepdims=True)
    scale = lax.rsqrt(jnp.mean(center * center, axis=-1, keepdims=True) + EPSILON)
    hat = center * scale
    xhat[...] = hat
    rstd[...] = scale
    low[...] = (hat * vecs[3:4, :] + vecs[5:6, :]).astype(BF16)


def norm_grad(grad, gain, hat, scale):
    e = grad * gain
    mean_e = jnp.mean(e, axis=-1, keepdims=True)
    mean_x = jnp.mean(e * hat, axis=-1, keepdims=True)
    return scale * (e - mean_e - hat * mean_x)


def total(values):
    return jnp.sum(values, axis=0, keepdims=True)


def norm_two_kernel(vecs, xhat, own, r1, cot, block_out, low, grad_two, sums):
    acc = [jnp.zeros((1, 768), F32) for _ in range(3)]
    for i in range(8):
        at = slice(32 * i, 32 * i + 32)
        hidden = xhat[at, :] * vecs[3:4, :] + vecs[5:6, :]
        resid = hidden + own[at, :] + r1[at, :].astype(F32) + vecs[7:8, :]
        center = resid - jnp.mean(resid, axis=-1, keepdims=True)
        scale = lax.rsqrt(jnp.mean(center * center, axis=-1, keepdims=True) + EPSILON)
        hat = center * scale
        block_out[at, :] = (hat * vecs[4:5, :] + vecs[6:7, :]).astype(BF16)
        grad = cot[at, :].astype(F32)
        back = norm_grad(grad, vecs[4:5, :], hat, scale)
        grad_two[at, :] = back
        low[at, :] = back.astype(BF16)
        acc = [acc[0] + total(grad * hat), acc[1] + total(grad), acc[2] + total(back)]
    sums[...] = jnp.concatenate(acc + [jnp.zeros((5, 768), F32)], axis=0)


def norm_one_kernel(
    pos, own, r1, grad_two, xhat, rstd, vecs, wo, o0, o1, o2, o3, low, grad_one, sums
):
    z, p, c = place(pos)
    acc = [jnp.zeros((1, 768), F32) for _ in range(3)]
    for i in range(8):
        at = slice(32 * i, 32 * i + 32)
        grad = own[at, :] + grad_two[at, :] + r1[at, :].astype(F32)
        hat = xhat[at, :]
        back = norm_grad(grad, vecs[3:4, :], hat, rstd[at, :])
        grad_one[at, :] = back
        low[at, :] = back.astype(BF16)
        acc = [acc[0] + total(grad * hat), acc[1] + total(grad), acc[2] + total(back)]
    sums[...] = jnp.concatenate(acc + [jnp.zeros((5, 768), F32)], axis=0)
    for k, out in enumerate((o0, o1, o2, o3)):
        start = (p ^ k) * 192
        out[...] = dot(low[...], wo[pl.ds(row_of(start, 64), 192), :], NT).astype(BF16)


def ff_kernel(h, wi, wx, bias, part, act, slope):
    acc = jnp.zeros((256, 768), F32)
    for f in range(6):
        at = slice(256 * f, 256 * f + 256)
        u = dot(h[...], wi[:, at]) + bias[1:2, at]
        cdf = 0.5 * (1.0 + lax.erf(u * 0.7071067811865476))
        low = (u * cdf).astype(BF16)
        act[:, at] = low
        slope[:, at] = cdf + u * jnp.exp2(u * u * (-0.5 * LOG2E)) * 0.3989422804014327
        acc += dot(low, wx[at, :768])
    part[...] = acc.astype(part.dtype)


def ff_back_kernel(g, slope, wi, wx, back, pre_low, sums):
    acc = jnp.zeros((256, 768), F32)
    for f in range(6):
        at = slice(256 * f, 256 * f + 256)
        pre = dot(g[...], wx[at, :768], NT) * slope[:, at]
        low = pre.astype(BF16)
        pre_low[:, at] = low
        sums[:, at] = jnp.broadcast_to(total(pre), (8, 256))
        acc += dot(low, wi[:, at], NT)
    back[...] = acc.astype(back.dtype)


def column_of(row):
    n = row.shape[1]
    first = lax.broadcasted_iota(jnp.int32, (128, n), 0) == 0
    return jnp.transpose(jnp.where(first, jnp.broadcast_to(row, (128, n)), 0.0))


def ff_grad_out_kernel(pos, a0, a1, g0, g1, sum_a, sum_b, keep, send, go):
    z, p, c = place(pos)
    go[:, :768] = dot(a0[...], g0[...], TN) + dot(a1[...], g1[...], TN)
    go[:, 768:] = column_of(sum_a[0:1, :] + sum_b[0:1, :])
    for k in range(4):
        for i in range(2):
            for out, core in ((keep, c), (send, 1 - c)):
                start = (((z ^ (2 * i)) >> 1) * 4 + (p ^ k)) * 192 + core * 96
                out[k, 96 * i : 96 * i + 96, :] = go[pl.ds(row_of(start), 96), :].astype(BF16)


def ff_grad_in_kernel(pos, h0, h1, b0, b1, keep, send, gi):
    z, p, c = place(pos)
    gi[...] = dot(h0[...], b0[...], TN) + dot(h1[...], b1[...], TN)
    for k in range(4):
        for i in range(4):
            for out, core in ((keep, c), (send, 1 - c)):
                start = (4 * (z ^ SLOTS[i]) + (p ^ k)) * 48 + core * 24
                out[k, 24 * i : 24 * i + 24, :] = gi[pl.ds(row_of(start), 24), :].astype(BF16)


def wo_grad_kernel(pos, a0, a1, a2, a3, low, sum_one, sum_two, keep, send, acc):
    z, p, c = place(pos)
    for k, a in enumerate((a0, a1, a2, a3)):
        start = (p ^ k) * 192
        acc[pl.ds(row_of(start), 192), 0:768] = dot(a[...], low[...], TN)
    rows = jnp.concatenate(
        [
            sum_one[2:3, :],
            sum_one[0:1, :],
            sum_two[0:1, :],
            sum_one[1:2, :],
            sum_two[1:2, :],
            sum_two[2:3, :],
            jnp.zeros((122, 768), F32),
        ],
        axis=0,
    )
    acc[:, 768:896] = jnp.transpose(rows)
    for k in range(4):
        for j in range(4):
            for out, core in ((keep, c), (send, 1 - c)):
                start = (4 * (z ^ SLOTS[j]) + (p ^ k)) * 48 + core * 24
                out[k, 24 * j : 24 * j + 24, :] = acc[pl.ds(row_of(start), 24), :].astype(BF16)


def qkv_back_kernel(dq, dmine, dother, wq, i0, mx, my, rest, low, sums):
    bias_q = jnp.zeros((1, 192), F32)
    bias_v = jnp.zeros((1, 192), F32)
    for k in range(4):
        grad_q = dq[k]
        grad_kv = dmine[k] + dother[k].astype(F32)
        grad_v = grad_kv[:, 256:448]
        bias_q += total(grad_q)
        bias_v += total(grad_v)
        parts = [grad_q, grad_kv[:, :192], grad_v, jnp.zeros((256, 64), F32)]
        whole = jnp.concatenate(parts, axis=1).astype(BF16)
        low[k] = whole
        part = dot(whole, wq[...], NT)
        if k == 0:
            i0[...] = part
        elif k == 1:
            mx[0:128, :] = part[:128].astype(BF16)
            rest[1] = part[128:].astype(BF16)
        elif k == 2:
            my[0:128, :] = part[128:].astype(BF16)
            rest[0] = part[:128].astype(BF16)
        else:
            mx[128:256, :] = part[:128].astype(BF16)
            my[128:256, :] = part[128:].astype(BF16)
    sums[...] = jnp.concatenate(
        [
            jnp.concatenate([bias_q, jnp.zeros((1, 64), F32)], axis=1),
            jnp.concatenate([bias_v, jnp.zeros((1, 64), F32)], axis=1),
            jnp.zeros((6, 256), F32),
        ],
        axis=0,
    )


def qkv_grad_kernel(pos, x0, x1, x2, x3, low, sums, keep, send, acc):
    z, p, c = place(pos)
    acc[...] = sum(dot(x[...], low[k], TN) for k, x in enumerate((x0, x1, x2, x3)))
    rows = jnp.concatenate(
        [jnp.zeros((64, 256), F32), sums[...], jnp.zeros((56, 256), F32)], axis=0
    )
    extra = jnp.transpose(rows)[:192]
    for i in range(4):
        acc[192 * i : 192 * i + 192, 512:640] += extra
    for j in range(4):
        for k in range(4):
            for out, core in ((keep, c), (send, 1 - c)):
                start = (4 * (z ^ j) + (p ^ k)) * 48 + core * 24
                out[j, 24 * k : 24 * k + 24, :] = acc[pl.ds(row_of(start), 24), :].astype(BF16)


def turned(block):
    n = block.shape[0]
    return jnp.transpose(jnp.concatenate([block, jnp.zeros((128 - n, 128), F32)], axis=0))


def finish_kernel(
    pos, tq, f1, f2, f3, ti, tw, gqkv, gbqv, gwo, gbo, gain, shift, gwin, gbin, gwout, gbout
):
    z, p, c = place(pos)
    gwout[...] = tw[:, 0:768]
    gbin[...] = turned(tw[:, 768:896])[0:1, 0:96]
    gwo[...] = ti[:, 3072:3840]
    side = turned(ti[:, 3840:3968])
    gbo[...] = side[0:1, 0:24]
    gain[...] = side[1:3, 0:24]
    shift[...] = side[3:5, 0:24]
    gbout[...] = side[5:6, 0:24]

    def run(own):
        biases = jnp.zeros((24, 128), F32)
        for k in range(4):
            chip = own ^ k
            qkv = tq[0:24, :] if k == 0 else (f1, f2, f3)[k - 1][...].astype(F32)
            for i in range(3):
                at = 768 * i + 192 * chip
                gqkv[:, at : at + 192] = qkv[:, 192 * i : 192 * i + 192]
            biases += jnp.where(z == chip, qkv[:, 512:640], 0.0)
        gbqv[...] = turned(biases)[64:66, 0:24]

    each_chip(p, run)
    for side in range(2):

        @pl.when((z & 1) == side)
        def _(side=side):
            for t in range(2):
                for i in range(2):
                    at = 768 * (side ^ t) + 1536 * i
                    gwin[:, at : at + 768] = ti[:, 1536 * t + 768 * i : 1536 * t + 768 * i + 768]


def chip_swap(value, k):
    return lax.ppermute(value, "seq", [(s, s ^ (2 * k)) for s in range(8)])


def core_swap(value):
    return lax.ppermute(value, "seq", [(s, s ^ 1) for s in range(8)])


def z_trade(value):
    return lax.all_to_all(value, "dp", 0, 0, tiled=True)


def z_swap(value, j):
    return lax.ppermute(value, "dp", [(i, i ^ j) for i in range(4)])


def after(value, *others):
    return lax.optimization_barrier((value, *others))[0]


def low_add(*terms):
    return sum(t.astype(F32) for t in terms)


def fast_device(
    tokens,
    doc_ids,
    cotangent,
    w_qkv,
    bias_qv,
    w_o,
    bias_o,
    ln_gain,
    ln_bias,
    w_in,
    bias_in,
    w_out,
    bias_out,
):
    pos = lax.axis_index(("dp", "seq")).astype(jnp.int32).reshape(1)
    others = (1, 2, 3)
    smalls = sum(
        jnp.pad(v, ((at, 16 - at - v.shape[0]), (0, 96 - v.shape[1])))
        for v, at in (
            (bias_qv, 0),
            (bias_o[None], 2),
            (ln_gain, 3),
            (ln_bias, 5),
            (bias_out[None], 7),
            (doc_ids[None, :24].astype(BF16), 8),
            (bias_in[None], 9),
        )
    )
    x1, x2, x3 = (chip_swap(tokens, k) for k in others)
    zq, zw = call(
        pack_kernel,
        (w_qkv, w_o, w_out, smalls),
        [sds((24, 3200), BF16), sds((96, 896), BF16)],
        smem_in=(),
        name="pack",
    )
    zqs = (zq,) + lax.optimization_barrier((*[z_swap(zq, j) for j in others], x1, x2))[:3]
    xs = (tokens, x1, x2, x3)
    *pieces_q, wo_z = call(
        split_qkv_kernel,
        (pos, *zqs),
        [sds((96, 640), BF16)] * 4 + [sds((96, 768), BF16)],
        name="split_qkv",
    )
    first_all = jnp.stack([pieces_q[0]] + [chip_swap(pieces_q[k], k) for k in others])
    first_other = core_swap(after(first_all, x3))
    zi_one = z_swap(after(w_in, *zqs[1:]), 2)
    zw_one = z_swap(after(zw, *zqs[1:]), 2)
    zi_mine, zi_theirs = call(
        split_in_kernel, (pos, w_in, zi_one), [sds((48, 1536), BF16)] * 2, name="split_in"
    )
    zi_two = z_swap(zi_theirs, 1)
    zw_pair = jnp.concatenate([zw, zw_one], axis=0)
    wo_z = after(wo_z, first_all)
    wo_all = jnp.stack([wo_z] + [chip_swap(wo_z, k) for k in others])
    wo_other = core_swap(wo_all)

    q, kv, wq, vecs, nb = call(
        qkv_kernel,
        (pos, first_all, first_other, *xs),
        [
            sds((4, 256, 256), BF16),
            sds((4, 256, 512), BF16),
            sds((768, 640), BF16),
            sds((16, 768), F32),
            sds((1,), jnp.int32),
        ],
        scratch=[pltpu.VMEM((8, 640), F32)],
        smem_out=(4,),
        name="qkv",
    )
    kv_other = after(core_swap(kv), zw_pair, zi_theirs)
    out_two = chip_swap(zw_pair, 2)
    *attended, ot, lse = call(
        attention_kernel,
        (pos, nb, q, kv, kv_other),
        [sds((256, 192), BF16)] * 4 + [sds((4, 192, 256), F32), sds((4, 8, 256), F32)],
        scratch=[pltpu.VMEM((8, 256, 256), BF16)] * 2 + [pltpu.VMEM((8, 192, 256), BF16)],
        smem_in=(0, 1),
        flops=1e10,
        name="attention",
    )
    attended = lax.optimization_barrier((*attended, wo_other, zi_two))[:4]
    pieces = [attended[0]] + [chip_swap(attended[k], k) for k in others]
    (wo,) = call(join_wo_kernel, (pos, wo_all, wo_other), [sds((768, 768), BF16)], name="join_wo")
    hidden, xhat, rstd = call(
        norm_kernel,
        (pos, tokens, *pieces, wo, vecs),
        [sds((256, 768), BF16), sds((256, 768), F32), sds((256, 1), F32)],
        name="norm_one",
    )
    hs = (hidden, z_swap(hidden, 1))
    out_half = after(jnp.stack([zw_pair, out_two]), pieces[1])
    out_all = jnp.concatenate([out_half, chip_swap(out_half, 1)])
    out_other = core_swap(out_all)
    in_one = after(jnp.concatenate([zi_mine, zi_two], axis=0), pieces[1])
    in_half = jnp.stack([in_one, chip_swap(in_one, 1)])
    in_all = jnp.concatenate([in_half, chip_swap(in_half, 2)])
    in_other = core_swap(in_all)
    (wi,) = call(join_in_kernel, (pos, in_all, in_other), [sds((768, 1536), BF16)], name="join_in")
    wx, bin_ = call(
        join_out_kernel,
        (pos, out_all, out_other),
        [sds((1536, 896), BF16), sds((8, 1536), F32)],
        name="join_out",
    )

    def ff(block, dtype):
        return call(
            ff_kernel,
            (block, wi, wx, bin_),
            [sds((256, 768), dtype), sds((256, 1536), BF16), sds((256, 1536), F32)],
            smem_in=(),
                name="ff",
        )

    part_own, act_own, slope_own = ff(hs[0], F32)
    part_far, act_far, slope_far = ff(after(hs[1], part_own), BF16)
    block_out, grad_two_low, grad_two, sums_two = call(
        norm_two_kernel,
        (vecs, xhat, part_own, z_swap(part_far, 1), cotangent),
        [sds((256, 768), BF16), sds((256, 768), BF16), sds((256, 768), F32), sds((8, 768), F32)],
        smem_in=(),
        name="norm_two",
    )
    gs = (grad_two_low, z_swap(grad_two_low, 1))

    def ff_back(block, slope, dtype):
        return call(
            ff_back_kernel,
            (block, slope, wi, wx),
            [sds((256, 768), dtype), sds((256, 1536), BF16), sds((8, 1536), F32)],
            smem_in=(),
                name="ff_back",
        )

    back_own, pre_own, sum_own = ff_back(gs[0], slope_own, F32)
    back_far, pre_far, sum_far = ff_back(after(gs[1], back_own), slope_far, BF16)
    back_got = z_swap(back_far, 1)
    out_keep, out_send = call(
        ff_grad_out_kernel,
        (pos, act_own, act_far, *gs, sum_own, sum_far),
        [sds((4, 192, 896), BF16)] * 2,
        scratch=[pltpu.VMEM((1536, 896), F32)],
        name="ff_grad_out",
    )
    in_keep, in_send = call(
        ff_grad_in_kernel,
        (pos, *hs, pre_own, pre_far),
        [sds((4, 96, 1536), BF16)] * 2,
        scratch=[pltpu.VMEM((768, 1536), F32)],
        name="ff_grad_in",
    )
    out_got, in_got = core_swap(out_send), core_swap(in_send)
    out_sum = low_add(out_keep, out_got)
    out_send = out_sum[1::2].astype(BF16)
    out_part = chip_swap(out_send, 1)
    out_left = low_add(out_sum[2], out_part[1]).astype(BF16)
    out_mine = low_add(out_sum[0], out_part[0], chip_swap(out_left, 2))
    tw = low_add(out_mine[:96], z_swap(out_mine[96:].astype(BF16), 2))
    in_sum = low_add(in_keep, in_got)
    in_send_two = in_sum[2:].astype(BF16)
    in_part = chip_swap(in_send_two, 2)
    in_left = low_add(in_sum[1], in_part[1]).astype(BF16)
    in_mine = low_add(in_sum[0], in_part[0], chip_swap(in_left, 1))
    back_got = after(back_got, out_send, in_send_two)

    *grad_att, low_one, grad_one, sums_one = call(
        norm_one_kernel,
        (pos, back_own, back_got, grad_two, xhat, rstd, vecs, wo),
        [sds((256, 192), BF16)] * 4
        + [sds((256, 768), BF16), sds((256, 768), F32), sds((8, 768), F32)],
        name="norm_one_back",
    )
    grad_pieces = [grad_att[0]] + [chip_swap(grad_att[k], k) for k in others]
    wo_keep, wo_send = call(
        wo_grad_kernel,
        (pos, *pieces, low_one, sums_one, sums_two),
        [sds((4, 96, 896), BF16)] * 2,
        scratch=[pltpu.VMEM((768, 896), F32)],
        name="wo_grad",
    )
    wo_got = core_swap(wo_send)
    wo_sum = low_add(wo_keep, wo_got)
    wo_low = [wo_sum[k].astype(BF16) for k in others]
    wo_part = [chip_swap(v, k) for v, k in zip(wo_low, others)]
    zi_sum = jnp.concatenate([in_mine, low_add(wo_sum[0], *wo_part)], axis=1)
    zi_got = z_swap(zi_sum[48:].astype(BF16), 1)
    zi_half = jnp.concatenate(
        [
            zi_sum[:48, :1536],
            zi_got[:, :1536].astype(F32),
            low_add(zi_sum[:48, 1536:], zi_got[:, 1536:]),
        ],
        axis=1,
    )
    ti = low_add(zi_half[:24], z_swap(zi_half[24:].astype(BF16), 2))
    grad_pieces = lax.optimization_barrier((*grad_pieces, *wo_low, out_left, in_left))[:4]

    dq, dmine, dother = call(
        attention_back_kernel,
        (pos, nb, q, kv, kv_other, *grad_pieces, ot, lse),
        [sds((4, 256, 192), F32), sds((4, 256, 512), F32), sds((4, 256, 512), BF16)],
        scratch=[pltpu.VMEM((8, 256, 256), BF16)] * 2
        + [pltpu.VMEM((8, 192, 256), BF16)]
        + [pltpu.VMEM((8, 256, 256), F32)] * 2,
        smem_in=(0, 1),
        flops=1e10,
        name="attention_back",
    )
    dgot = core_swap(dother)
    in_own, in_x, in_y, in_rest, low, sums_qv = call(
        qkv_back_kernel,
        (dq, dmine, dgot, wq),
        [sds((256, 768), F32)]
        + [sds((256, 768), BF16)] * 2
        + [sds((2, 128, 768), BF16), sds((4, 256, 640), BF16), sds((8, 256), F32)],
        smem_in=(),
        name="qkv_back",
    )
    q_keep, q_send = call(
        qkv_grad_kernel,
        (pos, *xs, low, sums_qv),
        [sds((4, 96, 640), BF16)] * 2,
        scratch=[pltpu.VMEM((768, 640), F32)],
        name="qkv_grad",
    )
    q_got = core_swap(q_send)
    q_sum = [low_add(q_keep[i], q_got[i]) for i in range(4)]
    tq = low_add(q_sum[0], *[z_swap(q_sum[j].astype(BF16), j) for j in others])
    got_x, got_y = chip_swap(in_x, 1), chip_swap(in_y, 2)
    last_y = chip_swap(low_add(in_rest[0], got_x[128:]).astype(BF16), 2)
    last_x = chip_swap(low_add(in_rest[1], got_y[128:]).astype(BF16), 1)
    input_grad = low_add(
        in_own,
        grad_one,
        jnp.concatenate([got_x[:128], got_y[:128]], axis=0),
        jnp.concatenate([last_y, last_x], axis=0),
    )
    final = [chip_swap(tq[24 * k : 24 * k + 24].astype(BF16), k) for k in others]
    gqkv, gbqv, gwo, gbo, gain, shift, gwin, gbin, gwout, gbout = call(
        finish_kernel,
        (pos, tq, *final, ti, tw),
        [
            sds((24, 2304), F32),
            sds((2, 24), F32),
            sds((24, 768), F32),
            sds((1, 24), F32),
            sds((2, 24), F32),
            sds((2, 24), F32),
            sds((24, 3072), F32),
            sds((1, 96), F32),
            sds((96, 768), F32),
            sds((1, 24), F32),
        ],
        name="finish",
    )
    return (
        block_out,
        input_grad,
        gqkv,
        gbqv,
        gwo,
        gbo.reshape(24),
        gain,
        shift,
        gwin,
        gbin.reshape(96),
        gwout,
        gbout.reshape(24),
    )


def layer_norm(resid, gain, shift):
    center = resid - jnp.mean(resid, axis=-1, keepdims=True)
    spread = jnp.mean(center * center, axis=-1, keepdims=True)
    return center * lax.rsqrt(spread + EPSILON) * gain + shift


def exact_gelu(value):
    return jax.nn.gelu(value, approximate=False)


def split_heads(matrix):
    return matrix.reshape(matrix.shape[0], HEADS, HDIM)


def allowed_pairs(query_doc, query_block, key_doc, key_block):
    return (query_doc[:, None] == key_doc[None, :]) & (key_block[None, :] <= query_block[:, None])


def over_parts(carry, arrays, update):
    count = arrays[0].shape[0]
    span = math.gcd(count, 1024)
    steps = count // span
    offsets = jnp.arange(steps, dtype=jnp.int32) * span
    parts = tuple((a.reshape((steps, span) + a.shape[1:]) for a in arrays))

    def inner(state, items):
        return (update(state, items[:-1], items[-1]), None)

    carry, unused = lax.scan(inner, carry, parts + (offsets,))
    return carry


def score_grads(query_heads, grad_heads, log_total, delta, allowed, key_heads, value_heads):
    raw = (
        jnp.einsum("qhd,khd->hqk", query_heads, key_heads, preferred_element_type=jnp.float32)
        * 0.125
    )
    probs = jnp.where(allowed[None], jnp.exp(raw - log_total[:, :, None]), 0.0)
    grad_probs = jnp.einsum(
        "qhd,khd->hqk", grad_heads, value_heads, preferred_element_type=jnp.float32
    )
    grad_scores = (probs * (grad_probs - delta[:, :, None]) * 0.125).astype(jnp.bfloat16)
    grad_query = jnp.einsum(
        "hqk,khd->qhd", grad_scores, key_heads, preferred_element_type=jnp.float32
    )
    grad_key = jnp.einsum(
        "hqk,qhd->khd", grad_scores, query_heads, preferred_element_type=jnp.float32
    )
    grad_value = jnp.einsum(
        "hqk,qhd->khd", probs.astype(jnp.bfloat16), grad_heads, preferred_element_type=jnp.float32
    )
    return (grad_query, grad_key, grad_value)


def on_device(
    tokens,
    doc_ids,
    cotangent,
    w_qkv,
    bias_qv,
    w_o,
    bias_o,
    ln_gain,
    ln_bias,
    w_in,
    bias_in,
    w_out,
    bias_out,
):
    rows = tokens.shape[0]
    width = tokens.shape[1]
    full = (
        lax.all_gather(w_qkv, ("dp", "seq"), axis=0, tiled=True),
        lax.all_gather(bias_qv, ("dp", "seq"), axis=1, tiled=True),
        lax.all_gather(w_o, ("dp", "seq"), axis=0, tiled=True),
        lax.all_gather(bias_o, ("dp", "seq"), axis=0, tiled=True),
        lax.all_gather(ln_gain, ("dp", "seq"), axis=1, tiled=True),
        lax.all_gather(ln_bias, ("dp", "seq"), axis=1, tiled=True),
        lax.all_gather(w_in, ("dp", "seq"), axis=0, tiled=True),
        lax.all_gather(bias_in, ("dp", "seq"), axis=0, tiled=True),
        lax.all_gather(w_out, ("dp", "seq"), axis=0, tiled=True),
        lax.all_gather(bias_out, ("dp", "seq"), axis=0, tiled=True),
    )
    (
        full_qkv,
        full_bias_qv,
        full_o,
        full_bias_o,
        full_gain,
        full_shift,
        full_in,
        full_bias_in,
        full_out,
        full_bias_out,
    ) = full
    positions = lax.axis_index("seq") * rows + jnp.arange(rows, dtype=jnp.int32)
    query_block = positions // BLK
    bias_three = jnp.concatenate(
        [
            full_bias_qv[0].astype(jnp.float32),
            jnp.zeros((width,), jnp.float32),
            full_bias_qv[1].astype(jnp.float32),
        ]
    )
    projected = (jnp.dot(tokens, full_qkv, preferred_element_type=jnp.float32) + bias_three).astype(
        jnp.bfloat16
    )
    queries = projected[:, :width]
    keys = projected[:, width : 2 * width]
    values = projected[:, 2 * width :]
    query_heads = split_heads(queries)

    def forward_update(state, parts, first):
        key_rows, value_rows, key_doc = parts
        count = key_rows.shape[0]
        key_block = (first + jnp.arange(count, dtype=jnp.int32)) // BLK
        allowed = allowed_pairs(doc_ids, query_block, key_doc, key_block)
        raw = (
            jnp.einsum(
                "qhd,khd->hqk",
                query_heads,
                split_heads(key_rows),
                preferred_element_type=jnp.float32,
            )
            * 0.125
        )
        masked = jnp.where(allowed[None], raw, NEG_LARGE)
        top, total, summed = state
        new_top = jnp.maximum(top, jnp.max(masked, axis=-1))
        weights = jnp.where(allowed[None], jnp.exp(masked - new_top[:, :, None]), 0.0)
        factor = jnp.exp(top - new_top)
        total = total * factor + jnp.sum(weights, axis=-1)
        summed = summed * factor[:, :, None] + jnp.einsum(
            "hqk,khd->hqd",
            weights.astype(jnp.bfloat16),
            split_heads(value_rows),
            preferred_element_type=jnp.float32,
        )
        return (new_top, total, summed)

    start_state = (
        jnp.full((HEADS, rows), NEG_LARGE, jnp.float32),
        jnp.zeros((HEADS, rows), jnp.float32),
        jnp.zeros((HEADS, rows, HDIM), jnp.float32),
    )
    top, total, summed = over_parts(
        start_state,
        (
            lax.all_gather(keys, "seq", axis=0, tiled=True),
            lax.all_gather(values, "seq", axis=0, tiled=True),
            lax.all_gather(doc_ids, "seq", axis=0, tiled=True),
        ),
        forward_update,
    )
    attn_heads = summed / total[:, :, None]
    log_total = top + jnp.log(total)
    attended_low = attn_heads.transpose(1, 0, 2).reshape(rows, width).astype(jnp.bfloat16)
    resid_one = (
        tokens.astype(jnp.float32)
        + jnp.dot(attended_low, full_o, preferred_element_type=jnp.float32)
        + full_bias_o.astype(jnp.float32)
    )
    hidden_one, norm_one_pull = jax.vjp(
        layer_norm, resid_one, full_gain[0].astype(jnp.float32), full_shift[0].astype(jnp.float32)
    )
    hidden_low = hidden_one.astype(jnp.bfloat16)
    pre_act = jnp.dot(
        hidden_low, full_in, preferred_element_type=jnp.float32
    ) + full_bias_in.astype(jnp.float32)
    activated, gelu_pull = jax.vjp(exact_gelu, pre_act)
    act_low = activated.astype(jnp.bfloat16)
    resid_two = (
        hidden_one
        + jnp.dot(act_low, full_out, preferred_element_type=jnp.float32)
        + full_bias_out.astype(jnp.float32)
    )
    normed, norm_two_pull = jax.vjp(
        layer_norm, resid_two, full_gain[1].astype(jnp.float32), full_shift[1].astype(jnp.float32)
    )
    block_out = normed.astype(jnp.bfloat16)
    again = (
        lax.all_gather(w_qkv, ("dp", "seq"), axis=0, tiled=True),
        lax.all_gather(bias_qv, ("dp", "seq"), axis=1, tiled=True),
        lax.all_gather(w_o, ("dp", "seq"), axis=0, tiled=True),
        lax.all_gather(bias_o, ("dp", "seq"), axis=0, tiled=True),
        lax.all_gather(ln_gain, ("dp", "seq"), axis=1, tiled=True),
        lax.all_gather(ln_bias, ("dp", "seq"), axis=1, tiled=True),
        lax.all_gather(w_in, ("dp", "seq"), axis=0, tiled=True),
        lax.all_gather(bias_in, ("dp", "seq"), axis=0, tiled=True),
        lax.all_gather(w_out, ("dp", "seq"), axis=0, tiled=True),
        lax.all_gather(bias_out, ("dp", "seq"), axis=0, tiled=True),
    )
    back_qkv = again[0]
    back_o = again[2]
    back_in = again[6]
    back_out = again[8]
    grad_resid_two, grad_gain_two, grad_shift_two = norm_two_pull(cotangent.astype(jnp.float32))
    grad_two_low = grad_resid_two.astype(jnp.bfloat16)
    grad_w_out = jnp.einsum("tf,td->fd", act_low, grad_two_low, preferred_element_type=jnp.float32)
    grad_bias_out = jnp.sum(grad_resid_two, axis=0)
    grad_act = jnp.einsum("td,fd->tf", grad_two_low, back_out, preferred_element_type=jnp.float32)
    (grad_pre,) = gelu_pull(grad_act)
    grad_pre_low = grad_pre.astype(jnp.bfloat16)
    grad_w_in = jnp.einsum(
        "td,tf->df", hidden_low, grad_pre_low, preferred_element_type=jnp.float32
    )
    grad_bias_in = jnp.sum(grad_pre, axis=0)
    grad_hidden = (
        jnp.einsum("tf,df->td", grad_pre_low, back_in, preferred_element_type=jnp.float32)
        + grad_resid_two
    )
    grad_resid_one, grad_gain_one, grad_shift_one = norm_one_pull(grad_hidden)
    grad_one_low = grad_resid_one.astype(jnp.bfloat16)
    grad_w_o = jnp.einsum(
        "te,td->ed", attended_low, grad_one_low, preferred_element_type=jnp.float32
    )
    grad_bias_o = jnp.sum(grad_resid_one, axis=0)
    grad_attn_low = jnp.einsum(
        "td,ed->te", grad_one_low, back_o, preferred_element_type=jnp.float32
    ).astype(jnp.bfloat16)
    grad_heads = split_heads(grad_attn_low)
    delta = jnp.sum(grad_heads.astype(jnp.float32).transpose(1, 0, 2) * attn_heads, axis=-1)
    keys_all, values_all, docs_all = (
        lax.all_gather(keys, "seq", axis=0, tiled=True),
        lax.all_gather(values, "seq", axis=0, tiled=True),
        lax.all_gather(doc_ids, "seq", axis=0, tiled=True),
    )
    length = keys_all.shape[0]
    span = math.gcd(length, 1024)
    steps = length // span
    offsets = jnp.arange(steps, dtype=jnp.int32) * span

    def back_step(grad_query, items):
        key_rows, value_rows, key_doc, first = items
        key_block = (first + jnp.arange(span, dtype=jnp.int32)) // BLK
        allowed = allowed_pairs(doc_ids, query_block, key_doc, key_block)
        part_query, part_key, part_value = score_grads(
            query_heads,
            grad_heads,
            log_total,
            delta,
            allowed,
            split_heads(key_rows),
            split_heads(value_rows),
        )
        return (
            grad_query + part_query,
            (part_key.reshape(span, width), part_value.reshape(span, width)),
        )

    grad_query, (key_terms, value_terms) = lax.scan(
        back_step,
        jnp.zeros((rows, HEADS, HDIM), jnp.float32),
        (
            keys_all.reshape(steps, span, width),
            values_all.reshape(steps, span, width),
            docs_all.reshape(steps, span),
            offsets,
        ),
    )
    grad_keys, grad_values = (
        lax.psum_scatter(
            key_terms.reshape(length, width).astype(jnp.bfloat16),
            "seq",
            scatter_dimension=0,
            tiled=True,
        ).astype(jnp.float32),
        lax.psum_scatter(
            value_terms.reshape(length, width).astype(jnp.bfloat16),
            "seq",
            scatter_dimension=0,
            tiled=True,
        ).astype(jnp.float32),
    )
    grad_queries = grad_query.reshape(rows, width)
    grad_qkv_low = jnp.concatenate([grad_queries, grad_keys, grad_values], axis=1).astype(
        jnp.bfloat16
    )
    grad_w_qkv = jnp.einsum("td,te->de", tokens, grad_qkv_low, preferred_element_type=jnp.float32)
    grad_bias_qv = jnp.stack([jnp.sum(grad_queries, axis=0), jnp.sum(grad_values, axis=0)])
    input_grad = (
        jnp.einsum("te,de->td", grad_qkv_low, back_qkv, preferred_element_type=jnp.float32)
        + grad_resid_one
    )
    grad_gain = jnp.stack([grad_gain_one, grad_gain_two])
    grad_shift = jnp.stack([grad_shift_one, grad_shift_two])
    owned = (
        lax.psum_scatter(grad_w_qkv, ("dp", "seq"), scatter_dimension=0, tiled=True),
        lax.psum_scatter(grad_bias_qv, ("dp", "seq"), scatter_dimension=1, tiled=True),
        lax.psum_scatter(grad_w_o, ("dp", "seq"), scatter_dimension=0, tiled=True),
        lax.psum_scatter(grad_bias_o, ("dp", "seq"), scatter_dimension=0, tiled=True),
        lax.psum_scatter(grad_gain, ("dp", "seq"), scatter_dimension=1, tiled=True),
        lax.psum_scatter(grad_shift, ("dp", "seq"), scatter_dimension=1, tiled=True),
        lax.psum_scatter(grad_w_in, ("dp", "seq"), scatter_dimension=0, tiled=True),
        lax.psum_scatter(grad_bias_in, ("dp", "seq"), scatter_dimension=0, tiled=True),
        lax.psum_scatter(grad_w_out, ("dp", "seq"), scatter_dimension=0, tiled=True),
        lax.psum_scatter(grad_bias_out, ("dp", "seq"), scatter_dimension=0, tiled=True),
    )
    return (
        block_out,
        input_grad,
        owned[0],
        owned[1],
        owned[2],
        owned[3],
        owned[4],
        owned[5],
        owned[6],
        owned[7],
        owned[8],
        owned[9],
    )


def solution(mesh):
    placed = (
        P(("dp", "seq"), None),
        P(("dp", "seq")),
        P(("dp", "seq"), None),
        P(("dp", "seq"), None),
        P(None, ("dp", "seq")),
        P(("dp", "seq"), None),
        P(("dp", "seq")),
        P(None, ("dp", "seq")),
        P(None, ("dp", "seq")),
        P(("dp", "seq"), None),
        P(("dp", "seq")),
        P(("dp", "seq"), None),
        P(("dp", "seq")),
    )
    sizes = dict(mesh.shape)
    fast = sizes["dp"] == 4 and sizes["seq"] == 8
    return jax.shard_map(
        fast_device if fast else on_device,
        mesh=mesh,
        in_specs=placed,
        out_specs=(
            P(("dp", "seq"), None),
            P(("dp", "seq"), None),
            P(("dp", "seq"), None),
            P(None, ("dp", "seq")),
            P(("dp", "seq"), None),
            P(("dp", "seq")),
            P(None, ("dp", "seq")),
            P(None, ("dp", "seq")),
            P(("dp", "seq"), None),
            P(("dp", "seq")),
            P(("dp", "seq"), None),
            P(("dp", "seq")),
        ),
        check_vma=False,
    )
```

```python
import math

import jax
import jax.numpy as jnp
from jax import lax
from jax.experimental import pallas as pl
from jax.experimental.pallas import tpu as pltpu
from jax.sharding import PartitionSpec as P

HEADS = 12
HDIM = 64
BLK = 256


EPSILON = 1e-12
NEG_LARGE = -1e30

F32 = jnp.float32
BF16 = jnp.bfloat16
LOG2E = 1.4426950408889634
NT = (((1,), (1,)), ((), ()))
TN = (((0,), (0,)), ((), ()))
NN = (((1,), (0,)), ((), ()))


def dot(left, right, dims=NN):
    return lax.dot_general(left, right, dims, preferred_element_type=F32)


def sds(shape, dtype):
    return jax.ShapeDtypeStruct(shape, dtype)


def call(kernel, args, outs, scratch=(), smem_in=(0,), smem_out=(), flops=1, name=None):
    space = lambda inside: pl.BlockSpec(memory_space=pltpu.SMEM if inside else pltpu.VMEM)
    return pl.pallas_call(
        kernel,
        out_shape=tuple(outs),
        in_specs=[space(i in smem_in) for i in range(len(args))],
        out_specs=tuple(space(i in smem_out) for i in range(len(outs))),
        scratch_shapes=list(scratch),
        compiler_params=pltpu.CompilerParams(vmem_limit_bytes=16 * 1024 * 1024),
        cost_estimate=pl.CostEstimate(flops=int(flops), transcendentals=0, bytes_accessed=1),
        name=name,
    )(*args)


def place(pos):
    d = pos[0]
    return d >> 3, (d >> 1) & 3, d & 1


def row_of(start, size=8):
    return pl.multiple_of(start, size)


def each_chip(p, run):
    for own in range(4):

        @pl.when(p == own)
        def _(own=own):
            run(own)


def pack_kernel(pos, wqkv, win, wout, smalls, p0, p1, p2, p3, wx):
    z, p, c = place(pos)
    rows = lax.broadcasted_iota(jnp.int32, (96, 96), 0)
    cols = lax.broadcasted_iota(jnp.int32, (96, 96), 1)
    eye = (rows == cols).astype(BF16)
    side = dot(eye, smalls[...], NT).astype(BF16)
    wx[...] = jnp.concatenate([wout[...], side, jnp.zeros((96, 112), BF16)], axis=1)
    small = jnp.concatenate([side[:24], jnp.zeros((24, 48), BF16)], axis=1)

    def run(own):
        for k, out in enumerate((p0, p1, p2, p3)):
            at = 192 * (own ^ k)
            parts = [wqkv[:, 768 * i + at : 768 * i + at + 192] for i in range(3)]
            parts.append(small)
            parts += [win[:, 768 * i + at : 768 * i + at + 192] for i in range(4)]
            out[...] = jnp.concatenate(parts, axis=1)

    each_chip(p, run)


SLOTS = (0, 2, 1, 3)


def interleave(pos, mine, other, out, at, slots):
    z, p, c = place(pos)

    def run(first, second):
        for k in range(4):
            for i in range(4):
                block = jnp.concatenate([first[at(i, k)], second[at(i, k)]], axis=0)
                start = (4 * (z ^ slots[i]) + (p ^ k)) * 48
                out[pl.ds(row_of(start, 16), 48), :] = block

    @pl.when(c == 0)
    def _():
        run(mine, other)

    @pl.when(c == 1)
    def _():
        run(other, mine)


def qkv_kernel(pos, am, ao, x0, x1, x2, x3, q, kv, wq, vecs, nb, bias):
    z, p, c = place(pos)
    everything = slice(None)
    interleave(
        pos, am, ao, wq, lambda i, k: (i, slice(24 * k, 24 * k + 24), everything), (0, 1, 2, 3)
    )
    flipped = jnp.transpose(wq[:, 512:640].astype(F32))
    vecs[...] = flipped[64:80]

    def run(own):
        at = slice(192 * own, 192 * own + 192)
        bias[0:1, :] = jnp.concatenate(
            [vecs[0:1, at], jnp.zeros((1, 192), F32), vecs[1:2, at], jnp.zeros((1, 64), F32)],
            axis=1,
        )

    each_chip(p, run)
    lane = lax.broadcasted_iota(jnp.int32, (1, 768), 1)
    mask = (lane >= 192 * z) & (lane < 192 * z + 192) & (lane % 24 == 0)
    second = jnp.sum(jnp.where(mask, vecs[8:9, :], 0.0))
    nb[0] = 8 - second.astype(jnp.int32)
    for k, x in enumerate((x0, x1, x2, x3)):
        got = (dot(x[...], wq[...]) + bias[0:1, :]).astype(BF16)
        pad = jnp.zeros((got.shape[0], 64), BF16)
        q[k] = jnp.concatenate([got[:, :192], pad], axis=1)
        kv[k] = jnp.concatenate([got[:, 192:384], pad, got[:, 384:576], pad], axis=1)


def join_ff_kernel(pos, mm, mo, wi, wx, bin_):
    z, p, c = place(pos)
    interleave(
        pos, mm, mo, wi, lambda i, k: (i, slice(24 * k, 24 * k + 24), slice(0, 768)), SLOTS
    )
    for i in range(4):
        base = (z ^ SLOTS[i]) * 192
        wx[pl.ds(row_of(base + c * 96, 32), 96), :] = mm[i, :, 768:1664]
        wx[pl.ds(row_of(base + (1 - c) * 96, 32), 96), :] = mo[i, :, 768:1664]
    flipped = jnp.transpose(wx[:, 768:896].astype(F32))
    bin_[...] = flipped[8:16]


def join_wo_kernel(pos, om, oo, wo):
    everything = slice(None)
    interleave(pos, om, oo, wo, lambda i, k: (k, slice(24 * i, 24 * i + 24), everything), SLOTS)


def key_range(pos, nb, k):
    z, p, c = place(pos)
    block = 2 * (p ^ k) + c
    return jnp.where(block < nb[0], 0, nb[0]), block + 1


def absolute_keys(pos, mine, other, keys, values, key_t, value_t):
    z, p, c = place(pos)
    for k in range(4):
        for ref, core in ((mine, c), (other, 1 - c)):
            at = 2 * (p ^ k) + core
            keys[at] = ref[k, :, 0:256]
            values[at] = ref[k, :, 256:512]
            if key_t is not None:
                key_t[at] = jnp.transpose(ref[k, :, 0:256])[:192] * 0.125
            if value_t is not None:
                value_t[at] = jnp.transpose(ref[k, :, 256:512])[:192]


def masked_heads(block):
    lane = lax.broadcasted_iota(jnp.int32, (256, 128), 1)
    zero = jnp.zeros((256, 128), block.dtype)
    return (
        jnp.where(lane < 64, block[:, 0:128], zero),
        jnp.where(lane >= 64, block[:, 0:128], zero),
        block[:, 128:256],
    )


GROUPS = (slice(0, 128), slice(0, 128), slice(128, 256))


def attention_kernel(pos, nb, q, mine, other, a0, a1, a2, a3, ot, lse, keys, values, value_t):
    scale = 0.125 * LOG2E
    absolute_keys(pos, mine, other, keys, values, None, value_t)
    for k, out in enumerate((a0, a1, a2, a3)):
        low, high = key_range(pos, nb, k)
        heads = masked_heads(q[k])

        def step(i, state):
            kb = low + 2 * i
            more = jnp.minimum(kb + 1, 7)
            valid = kb + 1 < high
            new = []
            scores = []
            for h in range(3):
                one = dot(keys[kb, :, GROUPS[h]], heads[h], NT)
                two = dot(keys[more, :, GROUPS[h]], heads[h], NT)
                scores.append((one, jnp.where(valid, two, NEG_LARGE)))
            for h in range(3):
                top, total, acc = state[h]
                one, two = scores[h]
                peak = jnp.max(jnp.maximum(one, two), axis=0, keepdims=True)
                next_top = jnp.maximum(top, peak * scale)
                one = jnp.exp2(one * scale - next_top)
                two = jnp.exp2(two * scale - next_top)
                factor = jnp.exp2(top - next_top)
                total = total * factor + jnp.sum(one + two, axis=0, keepdims=True)
                at = slice(64 * h, 64 * h + 64)
                acc = acc * factor + (
                    dot(value_t[kb, at, :], one.astype(BF16))
                    + dot(value_t[more, at, :], two.astype(BF16))
                )
                new.append((next_top, total, acc))
            return tuple(new)

        start = tuple(
            (jnp.full((1, BLK), NEG_LARGE, F32), jnp.zeros((1, BLK), F32), jnp.zeros((HDIM, BLK), F32))
            for _ in range(3)
        )
        state = lax.fori_loop(0, (high - low + 1) >> 1, step, start)
        done = []
        for h in range(3):
            top, total, acc = state[h]
            mixed = acc / total
            ot[k, 64 * h : 64 * h + 64, :] = mixed
            lse[k, h : h + 1, :] = top + jnp.log(total) * LOG2E
            done.append(mixed)
        out[...] = jnp.transpose(jnp.concatenate(done, axis=0)).astype(BF16)


def attention_back_kernel(
    pos, nb, q, mine, other, g0, g1, g2, g3, ot, lse, dq, dmine, dother, keys, values, key_t, dk, dv
):
    z, p, c = place(pos)
    scale = 0.125 * LOG2E
    absolute_keys(pos, mine, other, keys, values, key_t, None)
    dk[...] = jnp.zeros(dk.shape, F32)
    dv[...] = jnp.zeros(dv.shape, F32)
    for k, grad in enumerate((g0, g1, g2, g3)):
        low, high = key_range(pos, nb, k)
        heads = masked_heads(q[k])
        padded = jnp.concatenate([grad[...], jnp.zeros((256, 64), BF16)], axis=1)
        grads = masked_heads(padded)
        flipped = jnp.transpose(grad[...].astype(F32))
        product = flipped * ot[k]
        deltas = [
            jnp.sum(product[64 * h : 64 * h + 64], axis=0, keepdims=True) for h in range(3)
        ]
        logs = [lse[k, h : h + 1, :] for h in range(3)]
        pair_q = jnp.concatenate([heads[0], heads[1]], axis=0) * 0.125
        small_q = heads[2] * 0.125
        pair_g = jnp.concatenate([grads[0], grads[1]], axis=0)

        def step(kb, state):
            new, probs_low, scores_low = [], [], []
            for h in range(3):
                probs = jnp.exp2(dot(keys[kb, :, GROUPS[h]], heads[h], NT) * scale - logs[h])
                dprobs = dot(values[kb, :, GROUPS[h]], grads[h], NT)
                probs_low.append(probs.astype(BF16))
                scores_low.append((probs * (dprobs - deltas[h])).astype(BF16))
            for h in range(3):
                new.append(state[h] + dot(key_t[kb, 64 * h : 64 * h + 64, :], scores_low[h]))
            for ref, lows, pair, one in (
                (dk, scores_low, pair_q, small_q),
                (dv, probs_low, pair_g, grads[2]),
            ):
                ref[kb, :, 0:128] += dot(jnp.concatenate(lows[:2], axis=1), pair)
                ref[kb, :, 128:256] += dot(lows[2], one)
            return tuple(new)

        state = lax.fori_loop(
            low, high, step, tuple(jnp.zeros((HDIM, BLK), F32) for _ in range(3))
        )
        dq[k] = jnp.transpose(jnp.concatenate(state, axis=0))
    for k in range(4):
        at = 2 * (p ^ k)
        dmine[k] = jnp.concatenate([dk[at + c], dv[at + c]], axis=1)
        dother[k] = jnp.concatenate([dk[at + 1 - c], dv[at + 1 - c]], axis=1).astype(BF16)


def norm_kernel(pos, tokens, a0, a1, a2, a3, wo, vecs, low, xhat, rstd):
    z, p, c = place(pos)
    resid = tokens[...].astype(F32) + vecs[2:3, :]
    for k, a in enumerate((a0, a1, a2, a3)):
        start = (p ^ k) * 192
        resid += dot(a[...], wo[pl.ds(row_of(start, 64), 192), :])
    center = resid - jnp.mean(resid, axis=-1, keepdims=True)
    scale = lax.rsqrt(jnp.mean(center * center, axis=-1, keepdims=True) + EPSILON)
    hat = center * scale
    xhat[...] = hat
    rstd[...] = scale
    low[...] = (hat * vecs[3:4, :] + vecs[5:6, :]).astype(BF16)


def norm_grad(grad, gain, hat, scale):
    e = grad * gain
    mean_e = jnp.mean(e, axis=-1, keepdims=True)
    mean_x = jnp.mean(e * hat, axis=-1, keepdims=True)
    return scale * (e - mean_e - hat * mean_x)


def summed(i, own, rx, ry, sx, sy):
    half = slice(32 * (i % 4), 32 * (i % 4) + 32)
    first, last = (rx, sy) if i < 4 else (ry, sx)
    return own[32 * i : 32 * i + 32, :] + first[half, :].astype(F32) + last[half, :].astype(F32)


def total(values):
    return jnp.sum(values, axis=0, keepdims=True)


def norm_two_kernel(vecs, xhat, own, rx, ry, sx, sy, cot, block_out, low, grad_two, sums):
    acc = [jnp.zeros((1, 768), F32) for _ in range(3)]
    for i in range(8):
        at = slice(32 * i, 32 * i + 32)
        hidden = xhat[at, :] * vecs[3:4, :] + vecs[5:6, :]
        resid = hidden + summed(i, own, rx, ry, sx, sy) + vecs[7:8, :]
        center = resid - jnp.mean(resid, axis=-1, keepdims=True)
        scale = lax.rsqrt(jnp.mean(center * center, axis=-1, keepdims=True) + EPSILON)
        hat = center * scale
        block_out[at, :] = (hat * vecs[4:5, :] + vecs[6:7, :]).astype(BF16)
        grad = cot[at, :].astype(F32)
        back = norm_grad(grad, vecs[4:5, :], hat, scale)
        grad_two[at, :] = back
        low[at, :] = back.astype(BF16)
        acc = [acc[0] + total(grad * hat), acc[1] + total(grad), acc[2] + total(back)]
    sums[...] = jnp.concatenate(acc + [jnp.zeros((5, 768), F32)], axis=0)


def norm_one_kernel(
    pos, own, rx, ry, sx, sy, grad_two, xhat, rstd, vecs, wo, o0, o1, o2, o3, low, grad_one, sums
):
    z, p, c = place(pos)
    acc = [jnp.zeros((1, 768), F32) for _ in range(3)]
    for i in range(8):
        at = slice(32 * i, 32 * i + 32)
        grad = summed(i, own, rx, ry, sx, sy) + grad_two[at, :]
        hat = xhat[at, :]
        back = norm_grad(grad, vecs[3:4, :], hat, rstd[at, :])
        grad_one[at, :] = back
        low[at, :] = back.astype(BF16)
        acc = [acc[0] + total(grad * hat), acc[1] + total(grad), acc[2] + total(back)]
    sums[...] = jnp.concatenate(acc + [jnp.zeros((5, 768), F32)], axis=0)
    for k, out in enumerate((o0, o1, o2, o3)):
        start = (p ^ k) * 192
        out[...] = dot(low[...], wo[pl.ds(row_of(start, 64), 192), :], NT).astype(BF16)


def ff_block(h, wi, wx, bias, act, slope):
    acc = jnp.zeros((h.shape[0], 768), F32)
    for f in range(3):
        at = slice(256 * f, 256 * f + 256)
        u = dot(h, wi[:, at]) + bias[1:2, at]
        cdf = 0.5 * (1.0 + lax.erf(u * 0.7071067811865476))
        low = (u * cdf).astype(BF16)
        act[:, at] = low
        slope[:, at] = cdf + u * jnp.exp2(u * u * (-0.5 * LOG2E)) * 0.3989422804014327
        acc += dot(low, wx[at, :768])
    return acc


def ff_back_block(g, slope, wi, wx, low, sums):
    acc = jnp.zeros((256, 768), F32)
    for f in range(3):
        at = slice(256 * f, 256 * f + 256)
        pre = dot(g, wx[at, :768], NT) * slope[:, at]
        pre_low = pre.astype(BF16)
        low[:, at] = pre_low
        sums[0:1, at] += total(pre)
        acc += dot(pre_low, wi[:, at], NT)
    return acc


def ff_own_kernel(h, wi, wx, bias, part, act, slope):
    part[...] = ff_block(h[...], wi, wx, bias, act, slope)


def ff_near_kernel(h1, h2, wi, wx, bias, part1, part2, act1, act2, slope1, slope2):
    part1[...] = ff_block(h1[...], wi, wx, bias, act1, slope1).astype(BF16)
    part2[...] = ff_block(h2[...], wi, wx, bias, act2, slope2).astype(BF16)


def first_round(part, part1, part2, mx, my):
    low = part.astype(BF16)
    mx[...] = jnp.concatenate([part1[:128, :], low[:128]], axis=0)
    my[...] = jnp.concatenate([part2[128:, :], low[128:]], axis=0)


def ff_far_kernel(ha, hb, part1, part2, wi, wx, bias, mx, my, act, slope):
    h = jnp.concatenate([ha[...], hb[...]], axis=0)
    first_round(ff_block(h, wi, wx, bias, act, slope), part1, part2, mx, my)


def ff_back_own_kernel(g, slope, wi, wx, back, low, sums):
    sums[...] = jnp.zeros((8, 768), F32)
    back[...] = ff_back_block(g[...], slope, wi, wx, low, sums)


def ff_back_near_kernel(g1, g2, slope1, slope2, wi, wx, back1, back2, low1, low2, sums):
    sums[...] = jnp.zeros((8, 768), F32)
    back1[...] = ff_back_block(g1[...], slope1, wi, wx, low1, sums).astype(BF16)
    back2[...] = ff_back_block(g2[...], slope2, wi, wx, low2, sums).astype(BF16)


def ff_back_far_kernel(ga, gb, slope, back1, back2, wi, wx, mx, my, low, sums):
    sums[...] = jnp.zeros((8, 768), F32)
    g = jnp.concatenate([ga[...], gb[...]], axis=0)
    first_round(ff_back_block(g, slope, wi, wx, low, sums), back1, back2, mx, my)


def column_of(row):
    n = row.shape[1]
    first = lax.broadcasted_iota(jnp.int32, (128, n), 0) == 0
    return jnp.transpose(jnp.where(first, jnp.broadcast_to(row, (128, n)), 0.0))


def ff_grad_kernel(
    pos, h0, h1, h2, ha, hb, b0, b1, b2, b3, a0, a1, a2, a3, g0, g1, g2, ga, gb, s0, s1, s2,
    keep, send, gi, go
):
    z, p, c = place(pos)
    acc = dot(h0[...], b0[...], TN) + dot(h1[...], b1[...], TN) + dot(h2[...], b2[...], TN)
    gi[...] = acc + dot(ha[...], b3[:128, :], TN) + dot(hb[...], b3[128:, :], TN)
    acc = dot(a0[...], g0[...], TN) + dot(a1[...], g1[...], TN) + dot(a2[...], g2[...], TN)
    go[:, :768] = acc + dot(a3[:128, :], ga[...], TN) + dot(a3[128:, :], gb[...], TN)
    go[:, 768:] = column_of(s0[0:1, :] + s1[0:1, :] + s2[0:1, :])
    for i in range(4):
        for out, core in ((keep, c), (send, 1 - c)):
            for k in range(4):
                start = (4 * (z ^ SLOTS[i]) + (p ^ k)) * 48 + core * 24
                out[i, 24 * k : 24 * k + 24, 0:768] = gi[pl.ds(row_of(start), 24), :].astype(BF16)
            start = (z ^ SLOTS[i]) * 192 + core * 96
            out[i, :, 768:1664] = go[pl.ds(row_of(start), 96), :].astype(BF16)


def wo_grad_kernel(pos, a0, a1, a2, a3, low, sum_one, sum_two, keep, send, acc):
    z, p, c = place(pos)
    for k, a in enumerate((a0, a1, a2, a3)):
        start = (p ^ k) * 192
        acc[pl.ds(row_of(start), 192), 0:768] = dot(a[...], low[...], TN)
    rows = jnp.concatenate(
        [
            sum_one[2:3, :],
            sum_one[0:1, :],
            sum_two[0:1, :],
            sum_one[1:2, :],
            sum_two[1:2, :],
            sum_two[2:3, :],
            jnp.zeros((122, 768), F32),
        ],
        axis=0,
    )
    acc[:, 768:896] = jnp.transpose(rows)
    for k in range(4):
        for j in range(4):
            for out, core in ((keep, c), (send, 1 - c)):
                start = (4 * (z ^ SLOTS[j]) + (p ^ k)) * 48 + core * 24
                out[k, 24 * j : 24 * j + 24, :] = acc[pl.ds(row_of(start), 24), :].astype(BF16)


def qkv_back_kernel(dq, dmine, dother, wq, i0, mx, my, rest, low, sums):
    bias_q = jnp.zeros((1, 192), F32)
    bias_v = jnp.zeros((1, 192), F32)
    for k in range(4):
        grad_q = dq[k]
        grad_kv = dmine[k] + dother[k].astype(F32)
        grad_v = grad_kv[:, 256:448]
        bias_q += total(grad_q)
        bias_v += total(grad_v)
        parts = [grad_q, grad_kv[:, :192], grad_v, jnp.zeros((256, 64), F32)]
        whole = jnp.concatenate(parts, axis=1).astype(BF16)
        low[k] = whole
        part = dot(whole, wq[...], NT)
        if k == 0:
            i0[...] = part
        elif k == 1:
            mx[0:128, :] = part[:128].astype(BF16)
            rest[1, 128:] = part[128:].astype(BF16)
        elif k == 2:
            my[0:128, :] = part[128:].astype(BF16)
            rest[0, :128] = part[:128].astype(BF16)
        else:
            mx[128:256, :] = part[:128].astype(BF16)
            my[128:256, :] = part[128:].astype(BF16)
    sums[...] = jnp.concatenate(
        [
            jnp.concatenate([bias_q, jnp.zeros((1, 64), F32)], axis=1),
            jnp.concatenate([bias_v, jnp.zeros((1, 64), F32)], axis=1),
            jnp.zeros((6, 256), F32),
        ],
        axis=0,
    )


def qkv_grad_kernel(pos, x0, x1, x2, x3, low, sums, keep, send, acc):
    z, p, c = place(pos)
    acc[...] = sum(dot(x[...], low[k], TN) for k, x in enumerate((x0, x1, x2, x3)))
    rows = jnp.concatenate(
        [jnp.zeros((64, 256), F32), sums[...], jnp.zeros((56, 256), F32)], axis=0
    )
    extra = jnp.transpose(rows)[:192]
    for i in range(4):
        acc[192 * i : 192 * i + 192, 512:640] += extra
    for j in range(4):
        for k in range(4):
            for out, core in ((keep, c), (send, 1 - c)):
                start = (4 * (z ^ SLOTS[j]) + (p ^ k)) * 48 + core * 24
                out[j, 24 * k : 24 * k + 24, :] = acc[pl.ds(row_of(start), 24), :].astype(BF16)


def turned(block):
    n = block.shape[0]
    return jnp.transpose(jnp.concatenate([block, jnp.zeros((128 - n, 128), F32)], axis=0))


def finish_kernel(
    pos, tq, tm, f1, f2, f3, uo, gqkv, gbqv, gwo, gbo, gain, shift, gwin, gbin, gwout, gbout
):
    z, p, c = place(pos)
    gwout[...] = tm[:, 768:1536]
    gbin[...] = turned(tm[:, 1536:1664])[0:1, 0:96]
    gwo[...] = uo[:, 0:768]
    side = turned(uo[:, 768:896])
    gbo[...] = side[0:1, 0:24]
    gain[...] = side[1:3, 0:24]
    shift[...] = side[3:5, 0:24]
    gbout[...] = side[5:6, 0:24]

    def run(own):
        biases = jnp.zeros((24, 128), F32)
        for k in range(4):
            chip = own ^ k
            if k == 0:
                qkv, win = tq[0:24, :], tm[0:24, 0:768]
            else:
                got = (f1, f2, f3)[k - 1][...].astype(F32)
                qkv, win = got[:, 0:640], got[:, 640:1408]
            for i in range(3):
                at = 768 * i + 192 * chip
                gqkv[:, at : at + 192] = qkv[:, 192 * i : 192 * i + 192]
            for i in range(4):
                at = 768 * i + 192 * chip
                gwin[:, at : at + 192] = win[:, 192 * i : 192 * i + 192]
            biases += jnp.where(z == chip, qkv[:, 512:640], 0.0)
        gbqv[...] = turned(biases)[64:66, 0:24]

    each_chip(p, run)


def chip_swap(value, k):
    return lax.ppermute(value, "seq", [(s, s ^ (2 * k)) for s in range(8)])


def core_swap(value):
    return lax.ppermute(value, "seq", [(s, s ^ 1) for s in range(8)])


def z_trade(value):
    return lax.all_to_all(value, "dp", 0, 0, tiled=True)


def z_swap(value, j):
    return lax.ppermute(value, "dp", [(i, i ^ j) for i in range(4)])


def gather_first(value):
    return chip_swap(value, 1), chip_swap(value, 2)


def gather_last(near_x, near_y):
    return chip_swap(near_y[:128], 1), chip_swap(near_x[128:], 2)


def reduce_parts(mx, my, part1, part2):
    rx, ry = chip_swap(mx, 1), chip_swap(my, 2)
    sy = chip_swap(low_add(part2[:128], rx[128:]).astype(BF16), 2)
    sx = chip_swap(low_add(part1[128:], ry[128:]).astype(BF16), 1)
    return rx, ry, sx, sy


def after(value, *others):
    return lax.optimization_barrier((value, *others))[0]


def low_add(*terms):
    return sum(t.astype(F32) for t in terms)


def fast_device(
    tokens,
    doc_ids,
    cotangent,
    w_qkv,
    bias_qv,
    w_o,
    bias_o,
    ln_gain,
    ln_bias,
    w_in,
    bias_in,
    w_out,
    bias_out,
):
    pos = lax.axis_index(("dp", "seq")).astype(jnp.int32).reshape(1)
    others = (1, 2, 3)
    smalls = sum(
        jnp.pad(v, ((at, 16 - at - v.shape[0]), (0, 96 - v.shape[1])))
        for v, at in (
            (bias_qv, 0),
            (bias_o[None], 2),
            (ln_gain, 3),
            (ln_bias, 5),
            (bias_out[None], 7),
            (doc_ids[None, :24].astype(BF16), 8),
            (bias_in[None], 9),
        )
    )
    zo_one = z_swap(w_o, 2)
    p0, p1, p2, p3, zw = call(
        pack_kernel,
        (pos, w_qkv, w_in, w_out, smalls),
        [sds((24, 1408), BF16)] * 4 + [sds((96, 896), BF16)],
        name="pack",
    )
    zo_pair = jnp.concatenate([w_o, zo_one], axis=0)
    zo_two = z_swap(zo_pair, 1)
    got = [p0] + [chip_swap(v, k) for v, k in zip((p1, p2, p3), others)]
    tokens_far = after(tokens, p0, zo_one)
    x1, x2 = chip_swap(tokens_far, 1), chip_swap(tokens_far, 2)
    first = jnp.concatenate([g[:, :640] for g in got], axis=0)
    first = after(first, zo_two)
    firsts = [first] + [z_swap(first, j) for j in others]
    x3 = chip_swap(after(tokens_far, *got[1:]), 3)
    xs = (tokens, x1, x2, x3)
    first_all = jnp.stack(firsts)
    first_other = core_swap(after(first_all, x1, x2, x3))
    bulk = jnp.concatenate([jnp.concatenate([g[:, 640:] for g in got], axis=0), zw], axis=1)
    bulk_one = z_swap(after(bulk, first_all), 2)
    wo_z = after(jnp.concatenate([zo_pair, zo_two], axis=0), first_all)
    wo_far = [chip_swap(wo_z, k) for k in others]

    q, kv, wq, vecs, nb = call(
        qkv_kernel,
        (pos, first_all, first_other, *xs),
        [
            sds((4, 256, 256), BF16),
            sds((4, 256, 512), BF16),
            sds((768, 640), BF16),
            sds((16, 768), F32),
            sds((1,), jnp.int32),
        ],
        scratch=[pltpu.VMEM((8, 640), F32)],
        smem_out=(4,),
        name="qkv",
    )
    kv_other = core_swap(kv)
    *attended, ot, lse = call(
        attention_kernel,
        (pos, nb, q, kv, kv_other),
        [sds((256, 192), BF16)] * 4 + [sds((4, 192, 256), F32), sds((4, 8, 256), F32)],
        scratch=[pltpu.VMEM((8, 256, 256), BF16)] * 2 + [pltpu.VMEM((8, 192, 256), BF16)],
        smem_in=(0, 1),
        flops=2e9,
        name="attention",
    )
    *attended, wo1, wo2, wo3, bulk_one = lax.optimization_barrier((*attended, *wo_far, bulk_one))
    wo_all = jnp.stack([wo_z, wo1, wo2, wo3])
    wo_other = core_swap(wo_all)
    bulk_pair = jnp.stack([bulk, bulk_one])
    bulk_two = z_swap(bulk_pair, 1)
    pieces = [attended[0]] + [chip_swap(attended[k], k) for k in others]
    (wo,) = call(join_wo_kernel, (pos, wo_all, wo_other), [sds((768, 768), BF16)], name="join_wo")
    hidden, xhat, rstd = call(
        norm_kernel,
        (pos, tokens, *pieces, wo, vecs),
        [sds((256, 768), BF16), sds((256, 768), F32), sds((256, 1), F32)],
        name="norm_one",
    )
    hx, hy = gather_first(hidden)
    bulk_all = after(jnp.concatenate([bulk_pair, bulk_two]), hx, hy)
    wi, wx, bin_ = call(
        join_ff_kernel,
        (pos, bulk_all, core_swap(bulk_all)),
        [sds((768, 768), BF16), sds((768, 896), BF16), sds((8, 768), F32)],
        name="join_ff",
    )
    block, low_block, half = sds((256, 768), F32), sds((256, 768), BF16), sds((128, 768), BF16)
    ff_sums = sds((8, 768), F32)
    part_own, act0, slope0 = call(
        ff_own_kernel,
        (hidden, wi, wx, bin_),
        [block, low_block, block],
        smem_in=(),
        name="ff_own",
    )
    hx = after(hx, part_own)
    ha, hb = gather_last(hx, hy)
    part1, part2, act1, act2, slope1, slope2 = call(
        ff_near_kernel,
        (hx, hy, wi, wx, bin_),
        [low_block] * 4 + [block] * 2,
        smem_in=(),
        name="ff_near",
    )
    ha = after(ha, part1)
    mx, my, act3, slope3 = call(
        ff_far_kernel,
        (ha, hb, part1, part2, wi, wx, bin_),
        [low_block] * 3 + [block],
        smem_in=(),
        name="ff_far",
    )
    block_out, grad_two_low, grad_two, sums_two = call(
        norm_two_kernel,
        (vecs, xhat, part_own, *reduce_parts(mx, my, part1, part2), cotangent),
        [low_block, low_block, block, ff_sums],
        smem_in=(),
        name="norm_two",
    )
    gx, gy = gather_first(grad_two_low)
    back_own, low0, sum0 = call(
        ff_back_own_kernel,
        (grad_two_low, slope0, wi, wx),
        [block, low_block, ff_sums],
        smem_in=(),
        name="ff_back_own",
    )
    gx = after(gx, back_own)
    ga, gb = gather_last(gx, gy)
    back1, back2, low1, low2, sum1 = call(
        ff_back_near_kernel,
        (gx, gy, slope1, slope2, wi, wx),
        [low_block] * 4 + [ff_sums],
        smem_in=(),
        name="ff_back_near",
    )
    ga = after(ga, back1)
    mx, my, low3, sum2 = call(
        ff_back_far_kernel,
        (ga, gb, slope3, back1, back2, wi, wx),
        [low_block] * 3 + [ff_sums],
        smem_in=(),
        name="ff_back_far",
    )
    rx, ry, sx, sy = reduce_parts(mx, my, back1, back2)
    ff_keep, ff_send = call(
        ff_grad_kernel,
        (pos, hidden, hx, hy, ha, hb, low0, low1, low2, low3, act0, act1, act2, act3)
        + (grad_two_low, gx, gy, ga, gb, sum0, sum1, sum2),
        [sds((4, 96, 1664), BF16)] * 2,
        scratch=[pltpu.VMEM((768, 768), F32), pltpu.VMEM((768, 896), F32)],
        flops=1e10,
        name="ff_grad",
    )
    sx = after(sx, ff_keep)
    ff_sum = low_add(ff_keep, core_swap(ff_send))
    ff_got = z_swap(ff_sum[2:].astype(BF16), 1)
    ff_left = low_add(ff_sum[1], ff_got[1]).astype(BF16)
    ff_mine = low_add(ff_sum[0], ff_got[0])

    *grad_att, low_one, grad_one, sums_one = call(
        norm_one_kernel,
        (pos, back_own, rx, ry, sx, sy, grad_two, xhat, rstd, vecs, wo),
        [sds((256, 192), BF16)] * 4
        + [sds((256, 768), BF16), sds((256, 768), F32), sds((8, 768), F32)],
        name="norm_one_back",
    )
    grad_pieces = [grad_att[0]] + [chip_swap(grad_att[k], k) for k in others]
    wo_keep, wo_send = call(
        wo_grad_kernel,
        (pos, *pieces, low_one, sums_one, sums_two),
        [sds((4, 96, 896), BF16)] * 2,
        scratch=[pltpu.VMEM((768, 896), F32)],
        name="wo_grad",
    )
    wo_got = core_swap(wo_send)
    wo_sum = low_add(wo_keep, wo_got)
    wo_low = [wo_sum[k].astype(BF16) for k in others]
    wo_part = [chip_swap(v, k) for v, k in zip(wo_low, others)]
    grad_pieces = lax.optimization_barrier((*grad_pieces, *wo_low))[:4]

    dq, dmine, dother = call(
        attention_back_kernel,
        (pos, nb, q, kv, kv_other, *grad_pieces, ot, lse),
        [sds((4, 256, 192), F32), sds((4, 256, 512), F32), sds((4, 256, 512), BF16)],
        scratch=[pltpu.VMEM((8, 256, 256), BF16)] * 2
        + [pltpu.VMEM((8, 192, 256), BF16)]
        + [pltpu.VMEM((8, 256, 256), F32)] * 2,
        smem_in=(0, 1),
        flops=1e10,
        name="attention_back",
    )
    dgot = core_swap(after(dother, *wo_part))
    ff_far = z_swap(after(ff_left, dq), 2)
    in_own, in_x, in_y, in_rest, low, sums_qv = call(
        qkv_back_kernel,
        (dq, dmine, dgot, wq),
        [sds((256, 768), F32)]
        + [sds((256, 768), BF16)] * 2
        + [sds((2, 256, 768), BF16), sds((4, 256, 640), BF16), sds((8, 256), F32)],
        smem_in=(),
        name="qkv_back",
    )
    q_keep, q_send = call(
        qkv_grad_kernel,
        (pos, *xs, low, sums_qv),
        [sds((4, 96, 640), BF16)] * 2,
        scratch=[pltpu.VMEM((768, 640), F32)],
        name="qkv_grad",
    )
    q_got = core_swap(q_send)
    wo_mine = low_add(wo_sum[0], *wo_part)
    tm = low_add(ff_mine, ff_far)
    q_sum = low_add(q_keep, after(q_got, ff_far))
    q_next = z_swap(q_sum[2:].astype(BF16), 1)
    wo_mine = after(wo_mine, q_next)
    wo_next = z_swap(wo_mine[48:].astype(BF16), 1)
    wo_left = low_add(wo_mine[24:48], wo_next[24:]).astype(BF16)
    uo = low_add(wo_mine[:24], wo_next[:24], z_swap(wo_left, 2))
    q_left = low_add(q_sum[1], q_next[1]).astype(BF16)
    tq = low_add(q_sum[0], q_next[0], z_swap(q_left, 2))
    got_x, got_y, last_x, last_y = reduce_parts(in_x, in_y, in_rest[1], in_rest[0])
    input_grad = low_add(
        in_own,
        grad_one,
        jnp.concatenate([got_x[:128], got_y[:128]], axis=0),
        jnp.concatenate([last_y, last_x], axis=0),
    )
    final = [
        chip_swap(
            jnp.concatenate(
                [tq[24 * k : 24 * k + 24], tm[24 * k : 24 * k + 24, :768]], axis=1
            ).astype(BF16),
            k,
        )
        for k in others
    ]
    gqkv, gbqv, gwo, gbo, gain, shift, gwin, gbin, gwout, gbout = call(
        finish_kernel,
        (pos, tq, tm, *final, uo),
        [
            sds((24, 2304), F32),
            sds((2, 24), F32),
            sds((24, 768), F32),
            sds((1, 24), F32),
            sds((2, 24), F32),
            sds((2, 24), F32),
            sds((24, 3072), F32),
            sds((1, 96), F32),
            sds((96, 768), F32),
            sds((1, 24), F32),
        ],
        name="finish",
    )
    return (
        block_out,
        input_grad,
        gqkv,
        gbqv,
        gwo,
        gbo.reshape(24),
        gain,
        shift,
        gwin,
        gbin.reshape(96),
        gwout,
        gbout.reshape(24),
    )


def layer_norm(resid, gain, shift):
    center = resid - jnp.mean(resid, axis=-1, keepdims=True)
    spread = jnp.mean(center * center, axis=-1, keepdims=True)
    return center * lax.rsqrt(spread + EPSILON) * gain + shift


def exact_gelu(value):
    return jax.nn.gelu(value, approximate=False)


def split_heads(matrix):
    return matrix.reshape(matrix.shape[0], HEADS, HDIM)


def allowed_pairs(query_doc, query_block, key_doc, key_block):
    return (query_doc[:, None] == key_doc[None, :]) & (key_block[None, :] <= query_block[:, None])


def over_parts(carry, arrays, update):
    count = arrays[0].shape[0]
    span = math.gcd(count, 1024)
    steps = count // span
    offsets = jnp.arange(steps, dtype=jnp.int32) * span
    parts = tuple((a.reshape((steps, span) + a.shape[1:]) for a in arrays))

    def inner(state, items):
        return (update(state, items[:-1], items[-1]), None)

    carry, unused = lax.scan(inner, carry, parts + (offsets,))
    return carry


def score_grads(query_heads, grad_heads, log_total, delta, allowed, key_heads, value_heads):
    raw = (
        jnp.einsum("qhd,khd->hqk", query_heads, key_heads, preferred_element_type=jnp.float32)
        * 0.125
    )
    probs = jnp.where(allowed[None], jnp.exp(raw - log_total[:, :, None]), 0.0)
    grad_probs = jnp.einsum(
        "qhd,khd->hqk", grad_heads, value_heads, preferred_element_type=jnp.float32
    )
    grad_scores = (probs * (grad_probs - delta[:, :, None]) * 0.125).astype(jnp.bfloat16)
    grad_query = jnp.einsum(
        "hqk,khd->qhd", grad_scores, key_heads, preferred_element_type=jnp.float32
    )
    grad_key = jnp.einsum(
        "hqk,qhd->khd", grad_scores, query_heads, preferred_element_type=jnp.float32
    )
    grad_value = jnp.einsum(
        "hqk,qhd->khd", probs.astype(jnp.bfloat16), grad_heads, preferred_element_type=jnp.float32
    )
    return (grad_query, grad_key, grad_value)


def on_device(
    tokens,
    doc_ids,
    cotangent,
    w_qkv,
    bias_qv,
    w_o,
    bias_o,
    ln_gain,
    ln_bias,
    w_in,
    bias_in,
    w_out,
    bias_out,
):
    rows = tokens.shape[0]
    width = tokens.shape[1]
    full = (
        lax.all_gather(w_qkv, ("dp", "seq"), axis=0, tiled=True),
        lax.all_gather(bias_qv, ("dp", "seq"), axis=1, tiled=True),
        lax.all_gather(w_o, ("dp", "seq"), axis=0, tiled=True),
        lax.all_gather(bias_o, ("dp", "seq"), axis=0, tiled=True),
        lax.all_gather(ln_gain, ("dp", "seq"), axis=1, tiled=True),
        lax.all_gather(ln_bias, ("dp", "seq"), axis=1, tiled=True),
        lax.all_gather(w_in, ("dp", "seq"), axis=0, tiled=True),
        lax.all_gather(bias_in, ("dp", "seq"), axis=0, tiled=True),
        lax.all_gather(w_out, ("dp", "seq"), axis=0, tiled=True),
        lax.all_gather(bias_out, ("dp", "seq"), axis=0, tiled=True),
    )
    (
        full_qkv,
        full_bias_qv,
        full_o,
        full_bias_o,
        full_gain,
        full_shift,
        full_in,
        full_bias_in,
        full_out,
        full_bias_out,
    ) = full
    positions = lax.axis_index("seq") * rows + jnp.arange(rows, dtype=jnp.int32)
    query_block = positions // BLK
    bias_three = jnp.concatenate(
        [
            full_bias_qv[0].astype(jnp.float32),
            jnp.zeros((width,), jnp.float32),
            full_bias_qv[1].astype(jnp.float32),
        ]
    )
    projected = (jnp.dot(tokens, full_qkv, preferred_element_type=jnp.float32) + bias_three).astype(
        jnp.bfloat16
    )
    queries = projected[:, :width]
    keys = projected[:, width : 2 * width]
    values = projected[:, 2 * width :]
    query_heads = split_heads(queries)

    def forward_update(state, parts, first):
        key_rows, value_rows, key_doc = parts
        count = key_rows.shape[0]
        key_block = (first + jnp.arange(count, dtype=jnp.int32)) // BLK
        allowed = allowed_pairs(doc_ids, query_block, key_doc, key_block)
        raw = (
            jnp.einsum(
                "qhd,khd->hqk",
                query_heads,
                split_heads(key_rows),
                preferred_element_type=jnp.float32,
            )
            * 0.125
        )
        masked = jnp.where(allowed[None], raw, NEG_LARGE)
        top, total, summed = state
        new_top = jnp.maximum(top, jnp.max(masked, axis=-1))
        weights = jnp.where(allowed[None], jnp.exp(masked - new_top[:, :, None]), 0.0)
        factor = jnp.exp(top - new_top)
        total = total * factor + jnp.sum(weights, axis=-1)
        summed = summed * factor[:, :, None] + jnp.einsum(
            "hqk,khd->hqd",
            weights.astype(jnp.bfloat16),
            split_heads(value_rows),
            preferred_element_type=jnp.float32,
        )
        return (new_top, total, summed)

    start_state = (
        jnp.full((HEADS, rows), NEG_LARGE, jnp.float32),
        jnp.zeros((HEADS, rows), jnp.float32),
        jnp.zeros((HEADS, rows, HDIM), jnp.float32),
    )
    top, total, summed = over_parts(
        start_state,
        (
            lax.all_gather(keys, "seq", axis=0, tiled=True),
            lax.all_gather(values, "seq", axis=0, tiled=True),
            lax.all_gather(doc_ids, "seq", axis=0, tiled=True),
        ),
        forward_update,
    )
    attn_heads = summed / total[:, :, None]
    log_total = top + jnp.log(total)
    attended_low = attn_heads.transpose(1, 0, 2).reshape(rows, width).astype(jnp.bfloat16)
    resid_one = (
        tokens.astype(jnp.float32)
        + jnp.dot(attended_low, full_o, preferred_element_type=jnp.float32)
        + full_bias_o.astype(jnp.float32)
    )
    hidden_one, norm_one_pull = jax.vjp(
        layer_norm, resid_one, full_gain[0].astype(jnp.float32), full_shift[0].astype(jnp.float32)
    )
    hidden_low = hidden_one.astype(jnp.bfloat16)
    pre_act = jnp.dot(
        hidden_low, full_in, preferred_element_type=jnp.float32
    ) + full_bias_in.astype(jnp.float32)
    activated, gelu_pull = jax.vjp(exact_gelu, pre_act)
    act_low = activated.astype(jnp.bfloat16)
    resid_two = (
        hidden_one
        + jnp.dot(act_low, full_out, preferred_element_type=jnp.float32)
        + full_bias_out.astype(jnp.float32)
    )
    normed, norm_two_pull = jax.vjp(
        layer_norm, resid_two, full_gain[1].astype(jnp.float32), full_shift[1].astype(jnp.float32)
    )
    block_out = normed.astype(jnp.bfloat16)
    again = (
        lax.all_gather(w_qkv, ("dp", "seq"), axis=0, tiled=True),
        lax.all_gather(bias_qv, ("dp", "seq"), axis=1, tiled=True),
        lax.all_gather(w_o, ("dp", "seq"), axis=0, tiled=True),
        lax.all_gather(bias_o, ("dp", "seq"), axis=0, tiled=True),
        lax.all_gather(ln_gain, ("dp", "seq"), axis=1, tiled=True),
        lax.all_gather(ln_bias, ("dp", "seq"), axis=1, tiled=True),
        lax.all_gather(w_in, ("dp", "seq"), axis=0, tiled=True),
        lax.all_gather(bias_in, ("dp", "seq"), axis=0, tiled=True),
        lax.all_gather(w_out, ("dp", "seq"), axis=0, tiled=True),
        lax.all_gather(bias_out, ("dp", "seq"), axis=0, tiled=True),
    )
    back_qkv = again[0]
    back_o = again[2]
    back_in = again[6]
    back_out = again[8]
    grad_resid_two, grad_gain_two, grad_shift_two = norm_two_pull(cotangent.astype(jnp.float32))
    grad_two_low = grad_resid_two.astype(jnp.bfloat16)
    grad_w_out = jnp.einsum("tf,td->fd", act_low, grad_two_low, preferred_element_type=jnp.float32)
    grad_bias_out = jnp.sum(grad_resid_two, axis=0)
    grad_act = jnp.einsum("td,fd->tf", grad_two_low, back_out, preferred_element_type=jnp.float32)
    (grad_pre,) = gelu_pull(grad_act)
    grad_pre_low = grad_pre.astype(jnp.bfloat16)
    grad_w_in = jnp.einsum(
        "td,tf->df", hidden_low, grad_pre_low, preferred_element_type=jnp.float32
    )
    grad_bias_in = jnp.sum(grad_pre, axis=0)
    grad_hidden = (
        jnp.einsum("tf,df->td", grad_pre_low, back_in, preferred_element_type=jnp.float32)
        + grad_resid_two
    )
    grad_resid_one, grad_gain_one, grad_shift_one = norm_one_pull(grad_hidden)
    grad_one_low = grad_resid_one.astype(jnp.bfloat16)
    grad_w_o = jnp.einsum(
        "te,td->ed", attended_low, grad_one_low, preferred_element_type=jnp.float32
    )
    grad_bias_o = jnp.sum(grad_resid_one, axis=0)
    grad_attn_low = jnp.einsum(
        "td,ed->te", grad_one_low, back_o, preferred_element_type=jnp.float32
    ).astype(jnp.bfloat16)
    grad_heads = split_heads(grad_attn_low)
    delta = jnp.sum(grad_heads.astype(jnp.float32).transpose(1, 0, 2) * attn_heads, axis=-1)
    keys_all, values_all, docs_all = (
        lax.all_gather(keys, "seq", axis=0, tiled=True),
        lax.all_gather(values, "seq", axis=0, tiled=True),
        lax.all_gather(doc_ids, "seq", axis=0, tiled=True),
    )
    length = keys_all.shape[0]
    span = math.gcd(length, 1024)
    steps = length // span
    offsets = jnp.arange(steps, dtype=jnp.int32) * span

    def back_step(grad_query, items):
        key_rows, value_rows, key_doc, first = items
        key_block = (first + jnp.arange(span, dtype=jnp.int32)) // BLK
        allowed = allowed_pairs(doc_ids, query_block, key_doc, key_block)
        part_query, part_key, part_value = score_grads(
            query_heads,
            grad_heads,
            log_total,
            delta,
            allowed,
            split_heads(key_rows),
            split_heads(value_rows),
        )
        return (
            grad_query + part_query,
            (part_key.reshape(span, width), part_value.reshape(span, width)),
        )

    grad_query, (key_terms, value_terms) = lax.scan(
        back_step,
        jnp.zeros((rows, HEADS, HDIM), jnp.float32),
        (
            keys_all.reshape(steps, span, width),
            values_all.reshape(steps, span, width),
            docs_all.reshape(steps, span),
            offsets,
        ),
    )
    grad_keys, grad_values = (
        lax.psum_scatter(
            key_terms.reshape(length, width).astype(jnp.bfloat16),
            "seq",
            scatter_dimension=0,
            tiled=True,
        ).astype(jnp.float32),
        lax.psum_scatter(
            value_terms.reshape(length, width).astype(jnp.bfloat16),
            "seq",
            scatter_dimension=0,
            tiled=True,
        ).astype(jnp.float32),
    )
    grad_queries = grad_query.reshape(rows, width)
    grad_qkv_low = jnp.concatenate([grad_queries, grad_keys, grad_values], axis=1).astype(
        jnp.bfloat16
    )
    grad_w_qkv = jnp.einsum("td,te->de", tokens, grad_qkv_low, preferred_element_type=jnp.float32)
    grad_bias_qv = jnp.stack([jnp.sum(grad_queries, axis=0), jnp.sum(grad_values, axis=0)])
    input_grad = (
        jnp.einsum("te,de->td", grad_qkv_low, back_qkv, preferred_element_type=jnp.float32)
        + grad_resid_one
    )
    grad_gain = jnp.stack([grad_gain_one, grad_gain_two])
    grad_shift = jnp.stack([grad_shift_one, grad_shift_two])
    owned = (
        lax.psum_scatter(grad_w_qkv, ("dp", "seq"), scatter_dimension=0, tiled=True),
        lax.psum_scatter(grad_bias_qv, ("dp", "seq"), scatter_dimension=1, tiled=True),
        lax.psum_scatter(grad_w_o, ("dp", "seq"), scatter_dimension=0, tiled=True),
        lax.psum_scatter(grad_bias_o, ("dp", "seq"), scatter_dimension=0, tiled=True),
        lax.psum_scatter(grad_gain, ("dp", "seq"), scatter_dimension=1, tiled=True),
        lax.psum_scatter(grad_shift, ("dp", "seq"), scatter_dimension=1, tiled=True),
        lax.psum_scatter(grad_w_in, ("dp", "seq"), scatter_dimension=0, tiled=True),
        lax.psum_scatter(grad_bias_in, ("dp", "seq"), scatter_dimension=0, tiled=True),
        lax.psum_scatter(grad_w_out, ("dp", "seq"), scatter_dimension=0, tiled=True),
        lax.psum_scatter(grad_bias_out, ("dp", "seq"), scatter_dimension=0, tiled=True),
    )
    return (
        block_out,
        input_grad,
        owned[0],
        owned[1],
        owned[2],
        owned[3],
        owned[4],
        owned[5],
        owned[6],
        owned[7],
        owned[8],
        owned[9],
    )


def solution(mesh):
    placed = (
        P(("dp", "seq"), None),
        P(("dp", "seq")),
        P(("dp", "seq"), None),
        P(("dp", "seq"), None),
        P(None, ("dp", "seq")),
        P(("dp", "seq"), None),
        P(("dp", "seq")),
        P(None, ("dp", "seq")),
        P(None, ("dp", "seq")),
        P(("dp", "seq"), None),
        P(("dp", "seq")),
        P(("dp", "seq"), None),
        P(("dp", "seq")),
    )
    sizes = dict(mesh.shape)
    fast = sizes["dp"] == 4 and sizes["seq"] == 8
    return jax.shard_map(
        fast_device if fast else on_device,
        mesh=mesh,
        in_specs=placed,
        out_specs=(
            P(("dp", "seq"), None),
            P(("dp", "seq"), None),
            P(("dp", "seq"), None),
            P(None, ("dp", "seq")),
            P(("dp", "seq"), None),
            P(("dp", "seq")),
            P(None, ("dp", "seq")),
            P(None, ("dp", "seq")),
            P(("dp", "seq"), None),
            P(("dp", "seq")),
            P(("dp", "seq"), None),
            P(("dp", "seq")),
        ),
        check_vma=False,
    )
```

```python
import math

import jax
import jax.numpy as jnp
from jax import lax
from jax.experimental import pallas as pl
from jax.experimental.pallas import tpu as pltpu
from jax.sharding import PartitionSpec as P

HEADS = 12
HDIM = 64
BLK = 256


EPSILON = 1e-12
NEG_LARGE = -1e30

F32 = jnp.float32
BF16 = jnp.bfloat16
LOG2E = 1.4426950408889634
NT = (((1,), (1,)), ((), ()))
TN = (((0,), (0,)), ((), ()))
NN = (((1,), (0,)), ((), ()))


def dot(left, right, dims=NN):
    return lax.dot_general(left, right, dims, preferred_element_type=F32)


def sds(shape, dtype):
    return jax.ShapeDtypeStruct(shape, dtype)


def call(kernel, args, outs, scratch=(), smem_in=(0,), smem_out=(), flops=1, name=None):
    space = lambda inside: pl.BlockSpec(memory_space=pltpu.SMEM if inside else pltpu.VMEM)
    return pl.pallas_call(
        kernel,
        out_shape=tuple(outs),
        in_specs=[space(i in smem_in) for i in range(len(args))],
        out_specs=tuple(space(i in smem_out) for i in range(len(outs))),
        scratch_shapes=list(scratch),
        compiler_params=pltpu.CompilerParams(vmem_limit_bytes=16 * 1024 * 1024),
        cost_estimate=pl.CostEstimate(flops=int(flops), transcendentals=0, bytes_accessed=1),
        name=name,
    )(*args)


def place(pos):
    d = pos[0]
    return d >> 3, (d >> 1) & 3, d & 1


def row_of(start, size=8):
    return pl.multiple_of(start, size)


def each_chip(p, run):
    for own in range(4):

        @pl.when(p == own)
        def _(own=own):
            run(own)


def pack_kernel(pos, wqkv, win, wout, smalls, p0, p1, p2, p3, wx):
    z, p, c = place(pos)
    rows = lax.broadcasted_iota(jnp.int32, (96, 96), 0)
    cols = lax.broadcasted_iota(jnp.int32, (96, 96), 1)
    eye = (rows == cols).astype(BF16)
    side = dot(eye, smalls[...], NT).astype(BF16)
    wx[...] = jnp.concatenate([wout[...], side, jnp.zeros((96, 112), BF16)], axis=1)
    small = jnp.concatenate([side[:24], jnp.zeros((24, 48), BF16)], axis=1)

    def run(own):
        for k, out in enumerate((p0, p1, p2, p3)):
            at = 192 * (own ^ k)
            parts = [wqkv[:, 768 * i + at : 768 * i + at + 192] for i in range(3)]
            parts.append(small)
            parts += [win[:, 768 * i + at : 768 * i + at + 192] for i in range(4)]
            out[...] = jnp.concatenate(parts, axis=1)

    each_chip(p, run)


SLOTS = (0, 2, 1, 3)


def interleave(pos, mine, other, out, at, slots):
    z, p, c = place(pos)

    def run(first, second):
        for k in range(4):
            for i in range(4):
                block = jnp.concatenate([first[at(i, k)], second[at(i, k)]], axis=0)
                start = (4 * (z ^ slots[i]) + (p ^ k)) * 48
                out[pl.ds(row_of(start, 16), 48), :] = block

    @pl.when(c == 0)
    def _():
        run(mine, other)

    @pl.when(c == 1)
    def _():
        run(other, mine)


def qkv_kernel(pos, am, ao, x0, x1, x2, x3, q, kv, wq, vecs, nb, bias):
    z, p, c = place(pos)
    everything = slice(None)
    interleave(
        pos, am, ao, wq, lambda i, k: (i, slice(24 * k, 24 * k + 24), everything), (0, 1, 2, 3)
    )
    flipped = jnp.transpose(wq[:, 512:640].astype(F32))
    vecs[...] = flipped[64:80]

    def run(own):
        at = slice(192 * own, 192 * own + 192)
        bias[0:1, :] = jnp.concatenate(
            [vecs[0:1, at], jnp.zeros((1, 192), F32), vecs[1:2, at], jnp.zeros((1, 64), F32)],
            axis=1,
        )

    each_chip(p, run)
    lane = lax.broadcasted_iota(jnp.int32, (1, 768), 1)
    mask = (lane >= 192 * z) & (lane < 192 * z + 192) & (lane % 24 == 0)
    second = jnp.sum(jnp.where(mask, vecs[8:9, :], 0.0))
    nb[0] = 8 - second.astype(jnp.int32)
    for k, x in enumerate((x0, x1, x2, x3)):
        got = (dot(x[...], wq[...]) + bias[0:1, :]).astype(BF16)
        pad = jnp.zeros((got.shape[0], 64), BF16)
        q[k] = jnp.concatenate([got[:, :192], pad], axis=1)
        kv[k] = jnp.concatenate([got[:, 192:384], pad, got[:, 384:576], pad], axis=1)


def join_ff_kernel(pos, mm, mo, wi, wx, bin_):
    z, p, c = place(pos)
    interleave(
        pos, mm, mo, wi, lambda i, k: (i, slice(24 * k, 24 * k + 24), slice(0, 768)), SLOTS
    )
    for i in range(4):
        base = (z ^ SLOTS[i]) * 192
        wx[pl.ds(row_of(base + c * 96, 32), 96), :] = mm[i, :, 768:1664]
        wx[pl.ds(row_of(base + (1 - c) * 96, 32), 96), :] = mo[i, :, 768:1664]
    flipped = jnp.transpose(wx[:, 768:896].astype(F32))
    bin_[...] = flipped[8:16]


def join_wo_kernel(pos, om, oo, wo):
    everything = slice(None)
    interleave(pos, om, oo, wo, lambda i, k: (k, slice(24 * i, 24 * i + 24), everything), SLOTS)


def key_range(pos, nb, k):
    z, p, c = place(pos)
    block = 2 * (p ^ k) + c
    return jnp.where(block < nb[0], 0, nb[0]), block + 1


def absolute_keys(pos, mine, other, keys, values, key_t, value_t):
    z, p, c = place(pos)
    for k in range(4):
        for ref, core in ((mine, c), (other, 1 - c)):
            at = 2 * (p ^ k) + core
            keys[at] = ref[k, :, 0:256]
            values[at] = ref[k, :, 256:512]
            if key_t is not None:
                key_t[at] = jnp.transpose(ref[k, :, 0:256])[:192] * 0.125
            if value_t is not None:
                value_t[at] = jnp.transpose(ref[k, :, 256:512])[:192]


def masked_heads(block):
    lane = lax.broadcasted_iota(jnp.int32, (256, 128), 1)
    zero = jnp.zeros((256, 128), block.dtype)
    return (
        jnp.where(lane < 64, block[:, 0:128], zero),
        jnp.where(lane >= 64, block[:, 0:128], zero),
        block[:, 128:256],
    )


GROUPS = (slice(0, 128), slice(0, 128), slice(128, 256))


def attention_kernel(pos, nb, q, mine, other, a0, a1, a2, a3, ot, lse, keys, values, value_t):
    scale = 0.125 * LOG2E
    absolute_keys(pos, mine, other, keys, values, None, value_t)
    for k, out in enumerate((a0, a1, a2, a3)):
        low, high = key_range(pos, nb, k)
        heads = masked_heads(q[k])

        def step(i, state):
            kb = low + 2 * i
            more = jnp.minimum(kb + 1, 7)
            valid = kb + 1 < high
            new = []
            scores = []
            for h in range(3):
                one = dot(keys[kb, :, GROUPS[h]], heads[h], NT)
                two = dot(keys[more, :, GROUPS[h]], heads[h], NT)
                scores.append((one, jnp.where(valid, two, NEG_LARGE)))
            for h in range(3):
                top, total, acc = state[h]
                one, two = scores[h]
                peak = jnp.max(jnp.maximum(one, two), axis=0, keepdims=True)
                next_top = jnp.maximum(top, peak * scale)
                one = jnp.exp2(one * scale - next_top)
                two = jnp.exp2(two * scale - next_top)
                factor = jnp.exp2(top - next_top)
                total = total * factor + jnp.sum(one + two, axis=0, keepdims=True)
                at = slice(64 * h, 64 * h + 64)
                acc = acc * factor + (
                    dot(value_t[kb, at, :], one.astype(BF16))
                    + dot(value_t[more, at, :], two.astype(BF16))
                )
                new.append((next_top, total, acc))
            return tuple(new)

        start = tuple(
            (jnp.full((1, BLK), NEG_LARGE, F32), jnp.zeros((1, BLK), F32), jnp.zeros((HDIM, BLK), F32))
            for _ in range(3)
        )
        state = lax.fori_loop(0, (high - low + 1) >> 1, step, start)
        done = []
        for h in range(3):
            top, total, acc = state[h]
            mixed = acc / total
            ot[k, 64 * h : 64 * h + 64, :] = mixed
            lse[k, h : h + 1, :] = top + jnp.log(total) * LOG2E
            done.append(mixed)
        out[...] = jnp.transpose(jnp.concatenate(done, axis=0)).astype(BF16)


def attention_back_kernel(
    pos, nb, q, mine, other, g0, g1, g2, g3, ot, lse, dq, dmine, dother, keys, values, key_t, dk, dv
):
    z, p, c = place(pos)
    scale = 0.125 * LOG2E
    absolute_keys(pos, mine, other, keys, values, key_t, None)
    dk[...] = jnp.zeros(dk.shape, F32)
    dv[...] = jnp.zeros(dv.shape, F32)
    for k, grad in enumerate((g0, g1, g2, g3)):
        low, high = key_range(pos, nb, k)
        heads = masked_heads(q[k])
        padded = jnp.concatenate([grad[...], jnp.zeros((256, 64), BF16)], axis=1)
        grads = masked_heads(padded)
        flipped = jnp.transpose(grad[...].astype(F32))
        product = flipped * ot[k]
        deltas = [
            jnp.sum(product[64 * h : 64 * h + 64], axis=0, keepdims=True) for h in range(3)
        ]
        logs = [lse[k, h : h + 1, :] for h in range(3)]
        pair_q = jnp.concatenate([heads[0], heads[1]], axis=0) * 0.125
        small_q = heads[2] * 0.125
        pair_g = jnp.concatenate([grads[0], grads[1]], axis=0)

        def step(kb, state):
            new, probs_low, scores_low = [], [], []
            for h in range(3):
                probs = jnp.exp2(dot(keys[kb, :, GROUPS[h]], heads[h], NT) * scale - logs[h])
                dprobs = dot(values[kb, :, GROUPS[h]], grads[h], NT)
                probs_low.append(probs.astype(BF16))
                scores_low.append((probs * (dprobs - deltas[h])).astype(BF16))
            for h in range(3):
                new.append(state[h] + dot(key_t[kb, 64 * h : 64 * h + 64, :], scores_low[h]))
            for ref, lows, pair, one in (
                (dk, scores_low, pair_q, small_q),
                (dv, probs_low, pair_g, grads[2]),
            ):
                ref[kb, :, 0:128] += dot(jnp.concatenate(lows[:2], axis=1), pair)
                ref[kb, :, 128:256] += dot(lows[2], one)
            return tuple(new)

        state = lax.fori_loop(
            low, high, step, tuple(jnp.zeros((HDIM, BLK), F32) for _ in range(3))
        )
        dq[k] = jnp.transpose(jnp.concatenate(state, axis=0))
    for k in range(4):
        at = 2 * (p ^ k)
        dmine[k] = jnp.concatenate([dk[at + c], dv[at + c]], axis=1)
        dother[k] = jnp.concatenate([dk[at + 1 - c], dv[at + 1 - c]], axis=1).astype(BF16)


def norm_kernel(pos, tokens, a0, a1, a2, a3, wo, vecs, low, xhat, rstd):
    z, p, c = place(pos)
    resid = tokens[...].astype(F32) + vecs[2:3, :]
    for k, a in enumerate((a0, a1, a2, a3)):
        start = (p ^ k) * 192
        resid += dot(a[...], wo[pl.ds(row_of(start, 64), 192), :])
    center = resid - jnp.mean(resid, axis=-1, keepdims=True)
    scale = lax.rsqrt(jnp.mean(center * center, axis=-1, keepdims=True) + EPSILON)
    hat = center * scale
    xhat[...] = hat
    rstd[...] = scale
    low[...] = (hat * vecs[3:4, :] + vecs[5:6, :]).astype(BF16)


def norm_grad(grad, gain, hat, scale):
    e = grad * gain
    mean_e = jnp.mean(e, axis=-1, keepdims=True)
    mean_x = jnp.mean(e * hat, axis=-1, keepdims=True)
    return scale * (e - mean_e - hat * mean_x)


def summed(i, own, rx, ry, sx, sy):
    half = slice(32 * (i % 4), 32 * (i % 4) + 32)
    first, last = (rx, sy) if i < 4 else (ry, sx)
    return own[32 * i : 32 * i + 32, :] + first[half, :].astype(F32) + last[half, :].astype(F32)


def total(values):
    return jnp.sum(values, axis=0, keepdims=True)


def norm_two_kernel(vecs, xhat, own, rx, ry, sx, sy, cot, block_out, low, grad_two, sums):
    acc = [jnp.zeros((1, 768), F32) for _ in range(3)]
    for i in range(8):
        at = slice(32 * i, 32 * i + 32)
        hidden = xhat[at, :] * vecs[3:4, :] + vecs[5:6, :]
        resid = hidden + summed(i, own, rx, ry, sx, sy) + vecs[7:8, :]
        center = resid - jnp.mean(resid, axis=-1, keepdims=True)
        scale = lax.rsqrt(jnp.mean(center * center, axis=-1, keepdims=True) + EPSILON)
        hat = center * scale
        block_out[at, :] = (hat * vecs[4:5, :] + vecs[6:7, :]).astype(BF16)
        grad = cot[at, :].astype(F32)
        back = norm_grad(grad, vecs[4:5, :], hat, scale)
        grad_two[at, :] = back
        low[at, :] = back.astype(BF16)
        acc = [acc[0] + total(grad * hat), acc[1] + total(grad), acc[2] + total(back)]
    sums[...] = jnp.concatenate(acc + [jnp.zeros((5, 768), F32)], axis=0)


def norm_one_kernel(
    pos, own, rx, ry, sx, sy, grad_two, xhat, rstd, vecs, wo, o0, o1, o2, o3, low, grad_one, sums
):
    z, p, c = place(pos)
    acc = [jnp.zeros((1, 768), F32) for _ in range(3)]
    for i in range(8):
        at = slice(32 * i, 32 * i + 32)
        grad = summed(i, own, rx, ry, sx, sy) + grad_two[at, :]
        hat = xhat[at, :]
        back = norm_grad(grad, vecs[3:4, :], hat, rstd[at, :])
        grad_one[at, :] = back
        low[at, :] = back.astype(BF16)
        acc = [acc[0] + total(grad * hat), acc[1] + total(grad), acc[2] + total(back)]
    sums[...] = jnp.concatenate(acc + [jnp.zeros((5, 768), F32)], axis=0)
    for k, out in enumerate((o0, o1, o2, o3)):
        start = (p ^ k) * 192
        out[...] = dot(low[...], wo[pl.ds(row_of(start, 64), 192), :], NT).astype(BF16)


def ff_block(h, wi, wx, bias, act, slope):
    acc = jnp.zeros((h.shape[0], 768), F32)
    for f in range(3):
        at = slice(256 * f, 256 * f + 256)
        u = dot(h, wi[:, at]) + bias[1:2, at]
        cdf = 0.5 * (1.0 + lax.erf(u * 0.7071067811865476))
        low = (u * cdf).astype(BF16)
        act[:, at] = low
        slope[:, at] = cdf + u * jnp.exp2(u * u * (-0.5 * LOG2E)) * 0.3989422804014327
        acc += dot(low, wx[at, :768])
    return acc


def ff_back_block(g, slope, wi, wx, low, sums):
    acc = jnp.zeros((256, 768), F32)
    for f in range(3):
        at = slice(256 * f, 256 * f + 256)
        pre = dot(g, wx[at, :768], NT) * slope[:, at]
        pre_low = pre.astype(BF16)
        low[:, at] = pre_low
        sums[0:1, at] += total(pre)
        acc += dot(pre_low, wi[:, at], NT)
    return acc


def ff_own_kernel(h, wi, wx, bias, part, act, slope):
    part[...] = ff_block(h[...], wi, wx, bias, act, slope)


def ff_near_kernel(h1, h2, wi, wx, bias, part1, part2, act1, act2, slope1, slope2):
    part1[...] = ff_block(h1[...], wi, wx, bias, act1, slope1).astype(BF16)
    part2[...] = ff_block(h2[...], wi, wx, bias, act2, slope2).astype(BF16)


def first_round(part, part1, part2, mx, my):
    low = part.astype(BF16)
    mx[...] = jnp.concatenate([part1[:128, :], low[:128]], axis=0)
    my[...] = jnp.concatenate([part2[128:, :], low[128:]], axis=0)


def ff_far_kernel(ha, hb, part1, part2, wi, wx, bias, mx, my, act, slope):
    h = jnp.concatenate([ha[...], hb[...]], axis=0)
    first_round(ff_block(h, wi, wx, bias, act, slope), part1, part2, mx, my)


def ff_back_own_kernel(g, slope, wi, wx, back, low, sums):
    sums[...] = jnp.zeros((8, 768), F32)
    back[...] = ff_back_block(g[...], slope, wi, wx, low, sums)


def ff_back_near_kernel(g1, g2, slope1, slope2, wi, wx, back1, back2, low1, low2, sums):
    sums[...] = jnp.zeros((8, 768), F32)
    back1[...] = ff_back_block(g1[...], slope1, wi, wx, low1, sums).astype(BF16)
    back2[...] = ff_back_block(g2[...], slope2, wi, wx, low2, sums).astype(BF16)


def ff_back_far_kernel(ga, gb, slope, back1, back2, wi, wx, mx, my, low, sums):
    sums[...] = jnp.zeros((8, 768), F32)
    g = jnp.concatenate([ga[...], gb[...]], axis=0)
    first_round(ff_back_block(g, slope, wi, wx, low, sums), back1, back2, mx, my)


def column_of(row):
    n = row.shape[1]
    first = lax.broadcasted_iota(jnp.int32, (128, n), 0) == 0
    return jnp.transpose(jnp.where(first, jnp.broadcast_to(row, (128, n)), 0.0))


def ff_grad_kernel(
    pos, h0, h1, h2, ha, hb, b0, b1, b2, b3, a0, a1, a2, a3, g0, g1, g2, ga, gb, s0, s1, s2,
    keep, send, gi, go
):
    z, p, c = place(pos)
    acc = dot(h0[...], b0[...], TN) + dot(h1[...], b1[...], TN) + dot(h2[...], b2[...], TN)
    gi[...] = acc + dot(ha[...], b3[:128, :], TN) + dot(hb[...], b3[128:, :], TN)
    acc = dot(a0[...], g0[...], TN) + dot(a1[...], g1[...], TN) + dot(a2[...], g2[...], TN)
    go[:, :768] = acc + dot(a3[:128, :], ga[...], TN) + dot(a3[128:, :], gb[...], TN)
    go[:, 768:] = column_of(s0[0:1, :] + s1[0:1, :] + s2[0:1, :])
    for i in range(4):
        for out, core in ((keep, c), (send, 1 - c)):
            for k in range(4):
                start = (4 * (z ^ SLOTS[i]) + (p ^ k)) * 48 + core * 24
                out[i, 24 * k : 24 * k + 24, 0:768] = gi[pl.ds(row_of(start), 24), :].astype(BF16)
            start = (z ^ SLOTS[i]) * 192 + core * 96
            out[i, :, 768:1664] = go[pl.ds(row_of(start), 96), :].astype(BF16)


def wo_grad_kernel(pos, a0, a1, a2, a3, low, sum_one, sum_two, keep, send, acc):
    z, p, c = place(pos)
    for k, a in enumerate((a0, a1, a2, a3)):
        start = (p ^ k) * 192
        acc[pl.ds(row_of(start), 192), 0:768] = dot(a[...], low[...], TN)
    rows = jnp.concatenate(
        [
            sum_one[2:3, :],
            sum_one[0:1, :],
            sum_two[0:1, :],
            sum_one[1:2, :],
            sum_two[1:2, :],
            sum_two[2:3, :],
            jnp.zeros((122, 768), F32),
        ],
        axis=0,
    )
    acc[:, 768:896] = jnp.transpose(rows)
    for k in range(4):
        for j in range(4):
            for out, core in ((keep, c), (send, 1 - c)):
                start = (4 * (z ^ SLOTS[j]) + (p ^ k)) * 48 + core * 24
                out[k, 24 * j : 24 * j + 24, :] = acc[pl.ds(row_of(start), 24), :].astype(BF16)


def qkv_back_kernel(dq, dmine, dother, wq, i0, mx, my, rest, low, sums):
    bias_q = jnp.zeros((1, 192), F32)
    bias_v = jnp.zeros((1, 192), F32)
    for k in range(4):
        grad_q = dq[k]
        grad_kv = dmine[k] + dother[k].astype(F32)
        grad_v = grad_kv[:, 256:448]
        bias_q += total(grad_q)
        bias_v += total(grad_v)
        parts = [grad_q, grad_kv[:, :192], grad_v, jnp.zeros((256, 64), F32)]
        whole = jnp.concatenate(parts, axis=1).astype(BF16)
        low[k] = whole
        part = dot(whole, wq[...], NT)
        if k == 0:
            i0[...] = part
        elif k == 1:
            mx[0:128, :] = part[:128].astype(BF16)
            rest[1, 128:] = part[128:].astype(BF16)
        elif k == 2:
            my[0:128, :] = part[128:].astype(BF16)
            rest[0, :128] = part[:128].astype(BF16)
        else:
            mx[128:256, :] = part[:128].astype(BF16)
            my[128:256, :] = part[128:].astype(BF16)
    sums[...] = jnp.concatenate(
        [
            jnp.concatenate([bias_q, jnp.zeros((1, 64), F32)], axis=1),
            jnp.concatenate([bias_v, jnp.zeros((1, 64), F32)], axis=1),
            jnp.zeros((6, 256), F32),
        ],
        axis=0,
    )


def qkv_grad_kernel(pos, x0, x1, x2, x3, low, sums, keep, send, acc):
    z, p, c = place(pos)
    acc[...] = sum(dot(x[...], low[k], TN) for k, x in enumerate((x0, x1, x2, x3)))
    rows = jnp.concatenate(
        [jnp.zeros((64, 256), F32), sums[...], jnp.zeros((56, 256), F32)], axis=0
    )
    extra = jnp.transpose(rows)[:192]
    for i in range(4):
        acc[192 * i : 192 * i + 192, 512:640] += extra
    for j in range(4):
        for k in range(4):
            for out, core in ((keep, c), (send, 1 - c)):
                start = (4 * (z ^ SLOTS[j]) + (p ^ k)) * 48 + core * 24
                out[j, 24 * k : 24 * k + 24, :] = acc[pl.ds(row_of(start), 24), :].astype(BF16)


def turned(block):
    n = block.shape[0]
    return jnp.transpose(jnp.concatenate([block, jnp.zeros((128 - n, 128), F32)], axis=0))


def finish_kernel(
    pos, tq, tm, f1, f2, f3, uo, gqkv, gbqv, gwo, gbo, gain, shift, gwin, gbin, gwout, gbout
):
    z, p, c = place(pos)
    gwout[...] = tm[:, 768:1536]
    gbin[...] = turned(tm[:, 1536:1664])[0:1, 0:96]
    gwo[...] = uo[:, 0:768]
    side = turned(uo[:, 768:896])
    gbo[...] = side[0:1, 0:24]
    gain[...] = side[1:3, 0:24]
    shift[...] = side[3:5, 0:24]
    gbout[...] = side[5:6, 0:24]

    def run(own):
        biases = jnp.zeros((24, 128), F32)
        for k in range(4):
            chip = own ^ k
            if k == 0:
                qkv, win = tq[0:24, :], tm[0:24, 0:768]
            else:
                got = (f1, f2, f3)[k - 1][...].astype(F32)
                qkv, win = got[:, 0:640], got[:, 640:1408]
            for i in range(3):
                at = 768 * i + 192 * chip
                gqkv[:, at : at + 192] = qkv[:, 192 * i : 192 * i + 192]
            for i in range(4):
                at = 768 * i + 192 * chip
                gwin[:, at : at + 192] = win[:, 192 * i : 192 * i + 192]
            biases += jnp.where(z == chip, qkv[:, 512:640], 0.0)
        gbqv[...] = turned(biases)[64:66, 0:24]

    each_chip(p, run)


def chip_swap(value, k):
    return lax.ppermute(value, "seq", [(s, s ^ (2 * k)) for s in range(8)])


def core_swap(value):
    return lax.ppermute(value, "seq", [(s, s ^ 1) for s in range(8)])


def z_trade(value):
    return lax.all_to_all(value, "dp", 0, 0, tiled=True)


def z_swap(value, j):
    return lax.ppermute(value, "dp", [(i, i ^ j) for i in range(4)])


def gather_first(value):
    return chip_swap(value, 1), chip_swap(value, 2)


def gather_last(near_x, near_y):
    return chip_swap(near_y[:128], 1), chip_swap(near_x[128:], 2)


def reduce_parts(mx, my, part1, part2):
    rx, ry = chip_swap(mx, 1), chip_swap(my, 2)
    sy = chip_swap(low_add(part2[:128], rx[128:]).astype(BF16), 2)
    sx = chip_swap(low_add(part1[128:], ry[128:]).astype(BF16), 1)
    return rx, ry, sx, sy


def after(value, *others):
    return lax.optimization_barrier((value, *others))[0]


def low_add(*terms):
    return sum(t.astype(F32) for t in terms)


def fast_device(
    tokens,
    doc_ids,
    cotangent,
    w_qkv,
    bias_qv,
    w_o,
    bias_o,
    ln_gain,
    ln_bias,
    w_in,
    bias_in,
    w_out,
    bias_out,
):
    pos = lax.axis_index(("dp", "seq")).astype(jnp.int32).reshape(1)
    others = (1, 2, 3)
    smalls = sum(
        jnp.pad(v, ((at, 16 - at - v.shape[0]), (0, 96 - v.shape[1])))
        for v, at in (
            (bias_qv, 0),
            (bias_o[None], 2),
            (ln_gain, 3),
            (ln_bias, 5),
            (bias_out[None], 7),
            (doc_ids[None, :24].astype(BF16), 8),
            (bias_in[None], 9),
        )
    )
    zo_one = z_swap(w_o, 2)
    p0, p1, p2, p3, zw = call(
        pack_kernel,
        (pos, w_qkv, w_in, w_out, smalls),
        [sds((24, 1408), BF16)] * 4 + [sds((96, 896), BF16)],
        name="pack",
    )
    zo_pair = jnp.concatenate([w_o, zo_one], axis=0)
    zo_two = z_swap(zo_pair, 1)
    got = [p0] + [chip_swap(v, k) for v, k in zip((p1, p2, p3), others)]
    tokens_far = after(tokens, p0, zo_one)
    x1, x2 = chip_swap(tokens_far, 1), chip_swap(tokens_far, 2)
    first = jnp.concatenate([g[:, :640] for g in got], axis=0)
    first = after(first, zo_two)
    firsts = [first] + [z_swap(first, j) for j in others]
    x3 = chip_swap(after(tokens_far, *got[1:]), 3)
    xs = (tokens, x1, x2, x3)
    first_all = jnp.stack(firsts)
    first_other = core_swap(after(first_all, x1, x2, x3))
    bulk = jnp.concatenate([jnp.concatenate([g[:, 640:] for g in got], axis=0), zw], axis=1)
    bulk_one = z_swap(after(bulk, first_all), 2)
    wo_z = after(jnp.concatenate([zo_pair, zo_two], axis=0), first_all)
    wo_far = [chip_swap(wo_z, k) for k in others]

    q, kv, wq, vecs, nb = call(
        qkv_kernel,
        (pos, first_all, first_other, *xs),
        [
            sds((4, 256, 256), BF16),
            sds((4, 256, 512), BF16),
            sds((768, 640), BF16),
            sds((16, 768), F32),
            sds((1,), jnp.int32),
        ],
        scratch=[pltpu.VMEM((8, 640), F32)],
        smem_out=(4,),
        name="qkv",
    )
    kv_other = core_swap(kv)
    *attended, ot, lse = call(
        attention_kernel,
        (pos, nb, q, kv, kv_other),
        [sds((256, 192), BF16)] * 4 + [sds((4, 192, 256), F32), sds((4, 8, 256), F32)],
        scratch=[pltpu.VMEM((8, 256, 256), BF16)] * 2 + [pltpu.VMEM((8, 192, 256), BF16)],
        smem_in=(0, 1),
        flops=2e9,
        name="attention",
    )
    *attended, wo1, wo2, wo3, bulk_one = lax.optimization_barrier((*attended, *wo_far, bulk_one))
    wo_all = jnp.stack([wo_z, wo1, wo2, wo3])
    wo_other = core_swap(wo_all)
    bulk_pair = jnp.stack([bulk, bulk_one])
    bulk_two = z_swap(bulk_pair, 1)
    pieces = [attended[0]] + [chip_swap(attended[k], k) for k in others]
    (wo,) = call(join_wo_kernel, (pos, wo_all, wo_other), [sds((768, 768), BF16)], name="join_wo")
    hidden, xhat, rstd = call(
        norm_kernel,
        (pos, tokens, *pieces, wo, vecs),
        [sds((256, 768), BF16), sds((256, 768), F32), sds((256, 1), F32)],
        name="norm_one",
    )
    hx, hy = gather_first(hidden)
    bulk_all = after(jnp.concatenate([bulk_pair, bulk_two]), hx, hy)
    wi, wx, bin_ = call(
        join_ff_kernel,
        (pos, bulk_all, core_swap(bulk_all)),
        [sds((768, 768), BF16), sds((768, 896), BF16), sds((8, 768), F32)],
        name="join_ff",
    )
    block, low_block, half = sds((256, 768), F32), sds((256, 768), BF16), sds((128, 768), BF16)
    ff_sums = sds((8, 768), F32)
    part_own, act0, slope0 = call(
        ff_own_kernel,
        (hidden, wi, wx, bin_),
        [block, low_block, block],
        smem_in=(),
        name="ff_own",
    )
    ha, hb = gather_last(hx, hy)
    hx = after(hx, part_own)
    part1, part2, act1, act2, slope1, slope2 = call(
        ff_near_kernel,
        (hx, hy, wi, wx, bin_),
        [low_block] * 4 + [block] * 2,
        smem_in=(),
        name="ff_near",
    )
    ha = after(ha, part1)
    mx, my, act3, slope3 = call(
        ff_far_kernel,
        (ha, hb, part1, part2, wi, wx, bin_),
        [low_block] * 3 + [block],
        smem_in=(),
        name="ff_far",
    )
    block_out, grad_two_low, grad_two, sums_two = call(
        norm_two_kernel,
        (vecs, xhat, part_own, *reduce_parts(mx, my, part1, part2), cotangent),
        [low_block, low_block, block, ff_sums],
        smem_in=(),
        name="norm_two",
    )
    gx, gy = gather_first(grad_two_low)
    back_own, low0, sum0 = call(
        ff_back_own_kernel,
        (grad_two_low, slope0, wi, wx),
        [block, low_block, ff_sums],
        smem_in=(),
        name="ff_back_own",
    )
    ga, gb = gather_last(gx, gy)
    gx = after(gx, back_own)
    back1, back2, low1, low2, sum1 = call(
        ff_back_near_kernel,
        (gx, gy, slope1, slope2, wi, wx),
        [low_block] * 4 + [ff_sums],
        smem_in=(),
        name="ff_back_near",
    )
    ga = after(ga, back1)
    mx, my, low3, sum2 = call(
        ff_back_far_kernel,
        (ga, gb, slope3, back1, back2, wi, wx),
        [low_block] * 3 + [ff_sums],
        smem_in=(),
        name="ff_back_far",
    )
    rx, ry, sx, sy = reduce_parts(mx, my, back1, back2)
    ff_keep, ff_send = call(
        ff_grad_kernel,
        (pos, hidden, hx, hy, ha, hb, low0, low1, low2, low3, act0, act1, act2, act3)
        + (grad_two_low, gx, gy, ga, gb, sum0, sum1, sum2),
        [sds((4, 96, 1664), BF16)] * 2,
        scratch=[pltpu.VMEM((768, 768), F32), pltpu.VMEM((768, 896), F32)],
        flops=1e10,
        name="ff_grad",
    )
    sx = after(sx, ff_keep)
    ff_sum = low_add(ff_keep, core_swap(ff_send))
    ff_got = z_swap(ff_sum[2:].astype(BF16), 1)
    ff_left = low_add(ff_sum[1], ff_got[1]).astype(BF16)
    ff_mine = low_add(ff_sum[0], ff_got[0])

    *grad_att, low_one, grad_one, sums_one = call(
        norm_one_kernel,
        (pos, back_own, rx, ry, sx, sy, grad_two, xhat, rstd, vecs, wo),
        [sds((256, 192), BF16)] * 4
        + [sds((256, 768), BF16), sds((256, 768), F32), sds((8, 768), F32)],
        name="norm_one_back",
    )
    grad_pieces = [grad_att[0]] + [chip_swap(grad_att[k], k) for k in others]
    wo_keep, wo_send = call(
        wo_grad_kernel,
        (pos, *pieces, low_one, sums_one, sums_two),
        [sds((4, 96, 896), BF16)] * 2,
        scratch=[pltpu.VMEM((768, 896), F32)],
        name="wo_grad",
    )
    wo_got = core_swap(wo_send)
    wo_sum = low_add(wo_keep, wo_got)
    wo_low = [wo_sum[k].astype(BF16) for k in others]
    wo_part = [chip_swap(v, k) for v, k in zip(wo_low, others)]
    grad_pieces = lax.optimization_barrier((*grad_pieces, *wo_low))[:4]

    dq, dmine, dother = call(
        attention_back_kernel,
        (pos, nb, q, kv, kv_other, *grad_pieces, ot, lse),
        [sds((4, 256, 192), F32), sds((4, 256, 512), F32), sds((4, 256, 512), BF16)],
        scratch=[pltpu.VMEM((8, 256, 256), BF16)] * 2
        + [pltpu.VMEM((8, 192, 256), BF16)]
        + [pltpu.VMEM((8, 256, 256), F32)] * 2,
        smem_in=(0, 1),
        flops=1e10,
        name="attention_back",
    )
    dgot = core_swap(after(dother, *wo_part))
    ff_far = z_swap(after(ff_left, dq), 2)
    in_own, in_x, in_y, in_rest, low, sums_qv = call(
        qkv_back_kernel,
        (dq, dmine, dgot, wq),
        [sds((256, 768), F32)]
        + [sds((256, 768), BF16)] * 2
        + [sds((2, 256, 768), BF16), sds((4, 256, 640), BF16), sds((8, 256), F32)],
        smem_in=(),
        name="qkv_back",
    )
    q_keep, q_send = call(
        qkv_grad_kernel,
        (pos, *xs, low, sums_qv),
        [sds((4, 96, 640), BF16)] * 2,
        scratch=[pltpu.VMEM((768, 640), F32)],
        name="qkv_grad",
    )
    q_got = core_swap(q_send)
    wo_mine = low_add(wo_sum[0], *wo_part)
    tm = low_add(ff_mine, ff_far)
    q_sum = low_add(q_keep, after(q_got, ff_far))
    q_next = z_swap(q_sum[2:].astype(BF16), 1)
    wo_mine = after(wo_mine, q_next)
    wo_next = z_swap(wo_mine[48:].astype(BF16), 1)
    wo_left = low_add(wo_mine[24:48], wo_next[24:]).astype(BF16)
    uo = low_add(wo_mine[:24], wo_next[:24], z_swap(wo_left, 2))
    q_left = low_add(q_sum[1], q_next[1]).astype(BF16)
    tq = low_add(q_sum[0], q_next[0], z_swap(q_left, 2))
    got_x, got_y, last_x, last_y = reduce_parts(in_x, in_y, in_rest[1], in_rest[0])
    input_grad = low_add(
        in_own,
        grad_one,
        jnp.concatenate([got_x[:128], got_y[:128]], axis=0),
        jnp.concatenate([last_y, last_x], axis=0),
    )
    final = [
        chip_swap(
            jnp.concatenate(
                [tq[24 * k : 24 * k + 24], tm[24 * k : 24 * k + 24, :768]], axis=1
            ).astype(BF16),
            k,
        )
        for k in others
    ]
    gqkv, gbqv, gwo, gbo, gain, shift, gwin, gbin, gwout, gbout = call(
        finish_kernel,
        (pos, tq, tm, *final, uo),
        [
            sds((24, 2304), F32),
            sds((2, 24), F32),
            sds((24, 768), F32),
            sds((1, 24), F32),
            sds((2, 24), F32),
            sds((2, 24), F32),
            sds((24, 3072), F32),
            sds((1, 96), F32),
            sds((96, 768), F32),
            sds((1, 24), F32),
        ],
        name="finish",
    )
    return (
        block_out,
        input_grad,
        gqkv,
        gbqv,
        gwo,
        gbo.reshape(24),
        gain,
        shift,
        gwin,
        gbin.reshape(96),
        gwout,
        gbout.reshape(24),
    )


def layer_norm(resid, gain, shift):
    center = resid - jnp.mean(resid, axis=-1, keepdims=True)
    spread = jnp.mean(center * center, axis=-1, keepdims=True)
    return center * lax.rsqrt(spread + EPSILON) * gain + shift


def exact_gelu(value):
    return jax.nn.gelu(value, approximate=False)


def split_heads(matrix):
    return matrix.reshape(matrix.shape[0], HEADS, HDIM)


def allowed_pairs(query_doc, query_block, key_doc, key_block):
    return (query_doc[:, None] == key_doc[None, :]) & (key_block[None, :] <= query_block[:, None])


def over_parts(carry, arrays, update):
    count = arrays[0].shape[0]
    span = math.gcd(count, 1024)
    steps = count // span
    offsets = jnp.arange(steps, dtype=jnp.int32) * span
    parts = tuple((a.reshape((steps, span) + a.shape[1:]) for a in arrays))

    def inner(state, items):
        return (update(state, items[:-1], items[-1]), None)

    carry, unused = lax.scan(inner, carry, parts + (offsets,))
    return carry


def score_grads(query_heads, grad_heads, log_total, delta, allowed, key_heads, value_heads):
    raw = (
        jnp.einsum("qhd,khd->hqk", query_heads, key_heads, preferred_element_type=jnp.float32)
        * 0.125
    )
    probs = jnp.where(allowed[None], jnp.exp(raw - log_total[:, :, None]), 0.0)
    grad_probs = jnp.einsum(
        "qhd,khd->hqk", grad_heads, value_heads, preferred_element_type=jnp.float32
    )
    grad_scores = (probs * (grad_probs - delta[:, :, None]) * 0.125).astype(jnp.bfloat16)
    grad_query = jnp.einsum(
        "hqk,khd->qhd", grad_scores, key_heads, preferred_element_type=jnp.float32
    )
    grad_key = jnp.einsum(
        "hqk,qhd->khd", grad_scores, query_heads, preferred_element_type=jnp.float32
    )
    grad_value = jnp.einsum(
        "hqk,qhd->khd", probs.astype(jnp.bfloat16), grad_heads, preferred_element_type=jnp.float32
    )
    return (grad_query, grad_key, grad_value)


def on_device(
    tokens,
    doc_ids,
    cotangent,
    w_qkv,
    bias_qv,
    w_o,
    bias_o,
    ln_gain,
    ln_bias,
    w_in,
    bias_in,
    w_out,
    bias_out,
):
    rows = tokens.shape[0]
    width = tokens.shape[1]
    full = (
        lax.all_gather(w_qkv, ("dp", "seq"), axis=0, tiled=True),
        lax.all_gather(bias_qv, ("dp", "seq"), axis=1, tiled=True),
        lax.all_gather(w_o, ("dp", "seq"), axis=0, tiled=True),
        lax.all_gather(bias_o, ("dp", "seq"), axis=0, tiled=True),
        lax.all_gather(ln_gain, ("dp", "seq"), axis=1, tiled=True),
        lax.all_gather(ln_bias, ("dp", "seq"), axis=1, tiled=True),
        lax.all_gather(w_in, ("dp", "seq"), axis=0, tiled=True),
        lax.all_gather(bias_in, ("dp", "seq"), axis=0, tiled=True),
        lax.all_gather(w_out, ("dp", "seq"), axis=0, tiled=True),
        lax.all_gather(bias_out, ("dp", "seq"), axis=0, tiled=True),
    )
    (
        full_qkv,
        full_bias_qv,
        full_o,
        full_bias_o,
        full_gain,
        full_shift,
        full_in,
        full_bias_in,
        full_out,
        full_bias_out,
    ) = full
    positions = lax.axis_index("seq") * rows + jnp.arange(rows, dtype=jnp.int32)
    query_block = positions // BLK
    bias_three = jnp.concatenate(
        [
            full_bias_qv[0].astype(jnp.float32),
            jnp.zeros((width,), jnp.float32),
            full_bias_qv[1].astype(jnp.float32),
        ]
    )
    projected = (jnp.dot(tokens, full_qkv, preferred_element_type=jnp.float32) + bias_three).astype(
        jnp.bfloat16
    )
    queries = projected[:, :width]
    keys = projected[:, width : 2 * width]
    values = projected[:, 2 * width :]
    query_heads = split_heads(queries)

    def forward_update(state, parts, first):
        key_rows, value_rows, key_doc = parts
        count = key_rows.shape[0]
        key_block = (first + jnp.arange(count, dtype=jnp.int32)) // BLK
        allowed = allowed_pairs(doc_ids, query_block, key_doc, key_block)
        raw = (
            jnp.einsum(
                "qhd,khd->hqk",
                query_heads,
                split_heads(key_rows),
                preferred_element_type=jnp.float32,
            )
            * 0.125
        )
        masked = jnp.where(allowed[None], raw, NEG_LARGE)
        top, total, summed = state
        new_top = jnp.maximum(top, jnp.max(masked, axis=-1))
        weights = jnp.where(allowed[None], jnp.exp(masked - new_top[:, :, None]), 0.0)
        factor = jnp.exp(top - new_top)
        total = total * factor + jnp.sum(weights, axis=-1)
        summed = summed * factor[:, :, None] + jnp.einsum(
            "hqk,khd->hqd",
            weights.astype(jnp.bfloat16),
            split_heads(value_rows),
            preferred_element_type=jnp.float32,
        )
        return (new_top, total, summed)

    start_state = (
        jnp.full((HEADS, rows), NEG_LARGE, jnp.float32),
        jnp.zeros((HEADS, rows), jnp.float32),
        jnp.zeros((HEADS, rows, HDIM), jnp.float32),
    )
    top, total, summed = over_parts(
        start_state,
        (
            lax.all_gather(keys, "seq", axis=0, tiled=True),
            lax.all_gather(values, "seq", axis=0, tiled=True),
            lax.all_gather(doc_ids, "seq", axis=0, tiled=True),
        ),
        forward_update,
    )
    attn_heads = summed / total[:, :, None]
    log_total = top + jnp.log(total)
    attended_low = attn_heads.transpose(1, 0, 2).reshape(rows, width).astype(jnp.bfloat16)
    resid_one = (
        tokens.astype(jnp.float32)
        + jnp.dot(attended_low, full_o, preferred_element_type=jnp.float32)
        + full_bias_o.astype(jnp.float32)
    )
    hidden_one, norm_one_pull = jax.vjp(
        layer_norm, resid_one, full_gain[0].astype(jnp.float32), full_shift[0].astype(jnp.float32)
    )
    hidden_low = hidden_one.astype(jnp.bfloat16)
    pre_act = jnp.dot(
        hidden_low, full_in, preferred_element_type=jnp.float32
    ) + full_bias_in.astype(jnp.float32)
    activated, gelu_pull = jax.vjp(exact_gelu, pre_act)
    act_low = activated.astype(jnp.bfloat16)
    resid_two = (
        hidden_one
        + jnp.dot(act_low, full_out, preferred_element_type=jnp.float32)
        + full_bias_out.astype(jnp.float32)
    )
    normed, norm_two_pull = jax.vjp(
        layer_norm, resid_two, full_gain[1].astype(jnp.float32), full_shift[1].astype(jnp.float32)
    )
    block_out = normed.astype(jnp.bfloat16)
    again = (
        lax.all_gather(w_qkv, ("dp", "seq"), axis=0, tiled=True),
        lax.all_gather(bias_qv, ("dp", "seq"), axis=1, tiled=True),
        lax.all_gather(w_o, ("dp", "seq"), axis=0, tiled=True),
        lax.all_gather(bias_o, ("dp", "seq"), axis=0, tiled=True),
        lax.all_gather(ln_gain, ("dp", "seq"), axis=1, tiled=True),
        lax.all_gather(ln_bias, ("dp", "seq"), axis=1, tiled=True),
        lax.all_gather(w_in, ("dp", "seq"), axis=0, tiled=True),
        lax.all_gather(bias_in, ("dp", "seq"), axis=0, tiled=True),
        lax.all_gather(w_out, ("dp", "seq"), axis=0, tiled=True),
        lax.all_gather(bias_out, ("dp", "seq"), axis=0, tiled=True),
    )
    back_qkv = again[0]
    back_o = again[2]
    back_in = again[6]
    back_out = again[8]
    grad_resid_two, grad_gain_two, grad_shift_two = norm_two_pull(cotangent.astype(jnp.float32))
    grad_two_low = grad_resid_two.astype(jnp.bfloat16)
    grad_w_out = jnp.einsum("tf,td->fd", act_low, grad_two_low, preferred_element_type=jnp.float32)
    grad_bias_out = jnp.sum(grad_resid_two, axis=0)
    grad_act = jnp.einsum("td,fd->tf", grad_two_low, back_out, preferred_element_type=jnp.float32)
    (grad_pre,) = gelu_pull(grad_act)
    grad_pre_low = grad_pre.astype(jnp.bfloat16)
    grad_w_in = jnp.einsum(
        "td,tf->df", hidden_low, grad_pre_low, preferred_element_type=jnp.float32
    )
    grad_bias_in = jnp.sum(grad_pre, axis=0)
    grad_hidden = (
        jnp.einsum("tf,df->td", grad_pre_low, back_in, preferred_element_type=jnp.float32)
        + grad_resid_two
    )
    grad_resid_one, grad_gain_one, grad_shift_one = norm_one_pull(grad_hidden)
    grad_one_low = grad_resid_one.astype(jnp.bfloat16)
    grad_w_o = jnp.einsum(
        "te,td->ed", attended_low, grad_one_low, preferred_element_type=jnp.float32
    )
    grad_bias_o = jnp.sum(grad_resid_one, axis=0)
    grad_attn_low = jnp.einsum(
        "td,ed->te", grad_one_low, back_o, preferred_element_type=jnp.float32
    ).astype(jnp.bfloat16)
    grad_heads = split_heads(grad_attn_low)
    delta = jnp.sum(grad_heads.astype(jnp.float32).transpose(1, 0, 2) * attn_heads, axis=-1)
    keys_all, values_all, docs_all = (
        lax.all_gather(keys, "seq", axis=0, tiled=True),
        lax.all_gather(values, "seq", axis=0, tiled=True),
        lax.all_gather(doc_ids, "seq", axis=0, tiled=True),
    )
    length = keys_all.shape[0]
    span = math.gcd(length, 1024)
    steps = length // span
    offsets = jnp.arange(steps, dtype=jnp.int32) * span

    def back_step(grad_query, items):
        key_rows, value_rows, key_doc, first = items
        key_block = (first + jnp.arange(span, dtype=jnp.int32)) // BLK
        allowed = allowed_pairs(doc_ids, query_block, key_doc, key_block)
        part_query, part_key, part_value = score_grads(
            query_heads,
            grad_heads,
            log_total,
            delta,
            allowed,
            split_heads(key_rows),
            split_heads(value_rows),
        )
        return (
            grad_query + part_query,
            (part_key.reshape(span, width), part_value.reshape(span, width)),
        )

    grad_query, (key_terms, value_terms) = lax.scan(
        back_step,
        jnp.zeros((rows, HEADS, HDIM), jnp.float32),
        (
            keys_all.reshape(steps, span, width),
            values_all.reshape(steps, span, width),
            docs_all.reshape(steps, span),
            offsets,
        ),
    )
    grad_keys, grad_values = (
        lax.psum_scatter(
            key_terms.reshape(length, width).astype(jnp.bfloat16),
            "seq",
            scatter_dimension=0,
            tiled=True,
        ).astype(jnp.float32),
        lax.psum_scatter(
            value_terms.reshape(length, width).astype(jnp.bfloat16),
            "seq",
            scatter_dimension=0,
            tiled=True,
        ).astype(jnp.float32),
    )
    grad_queries = grad_query.reshape(rows, width)
    grad_qkv_low = jnp.concatenate([grad_queries, grad_keys, grad_values], axis=1).astype(
        jnp.bfloat16
    )
    grad_w_qkv = jnp.einsum("td,te->de", tokens, grad_qkv_low, preferred_element_type=jnp.float32)
    grad_bias_qv = jnp.stack([jnp.sum(grad_queries, axis=0), jnp.sum(grad_values, axis=0)])
    input_grad = (
        jnp.einsum("te,de->td", grad_qkv_low, back_qkv, preferred_element_type=jnp.float32)
        + grad_resid_one
    )
    grad_gain = jnp.stack([grad_gain_one, grad_gain_two])
    grad_shift = jnp.stack([grad_shift_one, grad_shift_two])
    owned = (
        lax.psum_scatter(grad_w_qkv, ("dp", "seq"), scatter_dimension=0, tiled=True),
        lax.psum_scatter(grad_bias_qv, ("dp", "seq"), scatter_dimension=1, tiled=True),
        lax.psum_scatter(grad_w_o, ("dp", "seq"), scatter_dimension=0, tiled=True),
        lax.psum_scatter(grad_bias_o, ("dp", "seq"), scatter_dimension=0, tiled=True),
        lax.psum_scatter(grad_gain, ("dp", "seq"), scatter_dimension=1, tiled=True),
        lax.psum_scatter(grad_shift, ("dp", "seq"), scatter_dimension=1, tiled=True),
        lax.psum_scatter(grad_w_in, ("dp", "seq"), scatter_dimension=0, tiled=True),
        lax.psum_scatter(grad_bias_in, ("dp", "seq"), scatter_dimension=0, tiled=True),
        lax.psum_scatter(grad_w_out, ("dp", "seq"), scatter_dimension=0, tiled=True),
        lax.psum_scatter(grad_bias_out, ("dp", "seq"), scatter_dimension=0, tiled=True),
    )
    return (
        block_out,
        input_grad,
        owned[0],
        owned[1],
        owned[2],
        owned[3],
        owned[4],
        owned[5],
        owned[6],
        owned[7],
        owned[8],
        owned[9],
    )


def solution(mesh):
    placed = (
        P(("dp", "seq"), None),
        P(("dp", "seq")),
        P(("dp", "seq"), None),
        P(("dp", "seq"), None),
        P(None, ("dp", "seq")),
        P(("dp", "seq"), None),
        P(("dp", "seq")),
        P(None, ("dp", "seq")),
        P(None, ("dp", "seq")),
        P(("dp", "seq"), None),
        P(("dp", "seq")),
        P(("dp", "seq"), None),
        P(("dp", "seq")),
    )
    sizes = dict(mesh.shape)
    fast = sizes["dp"] == 4 and sizes["seq"] == 8
    return jax.shard_map(
        fast_device if fast else on_device,
        mesh=mesh,
        in_specs=placed,
        out_specs=(
            P(("dp", "seq"), None),
            P(("dp", "seq"), None),
            P(("dp", "seq"), None),
            P(None, ("dp", "seq")),
            P(("dp", "seq"), None),
            P(("dp", "seq")),
            P(None, ("dp", "seq")),
            P(None, ("dp", "seq")),
            P(("dp", "seq"), None),
            P(("dp", "seq")),
            P(("dp", "seq"), None),
            P(("dp", "seq")),
        ),
        check_vma=False,
    )
```

```python
import math

import jax
import jax.numpy as jnp
from jax import lax
from jax.experimental import pallas as pl
from jax.experimental.pallas import tpu as pltpu
from jax.sharding import PartitionSpec as P

HEADS = 12
HDIM = 64
BLK = 256


EPSILON = 1e-12
NEG_LARGE = -1e30

F32 = jnp.float32
BF16 = jnp.bfloat16
LOG2E = 1.4426950408889634
NT = (((1,), (1,)), ((), ()))
TN = (((0,), (0,)), ((), ()))
NN = (((1,), (0,)), ((), ()))


def dot(left, right, dims=NN):
    return lax.dot_general(left, right, dims, preferred_element_type=F32)


def sds(shape, dtype):
    return jax.ShapeDtypeStruct(shape, dtype)


def call(kernel, args, outs, scratch=(), smem_in=(0,), smem_out=(), flops=1, name=None):
    space = lambda inside: pl.BlockSpec(memory_space=pltpu.SMEM if inside else pltpu.VMEM)
    return pl.pallas_call(
        kernel,
        out_shape=tuple(outs),
        in_specs=[space(i in smem_in) for i in range(len(args))],
        out_specs=tuple(space(i in smem_out) for i in range(len(outs))),
        scratch_shapes=list(scratch),
        compiler_params=pltpu.CompilerParams(vmem_limit_bytes=16 * 1024 * 1024),
        cost_estimate=pl.CostEstimate(flops=int(flops), transcendentals=0, bytes_accessed=1),
        name=name,
    )(*args)


def place(pos):
    d = pos[0]
    return d >> 3, (d >> 1) & 3, d & 1


def row_of(start, size=8):
    return pl.multiple_of(start, size)


def each_chip(p, run):
    for own in range(4):

        @pl.when(p == own)
        def _(own=own):
            run(own)


def pack_kernel(pos, wqkv, win, wout, smalls, p0, p1, p2, p3, wx):
    z, p, c = place(pos)
    rows = lax.broadcasted_iota(jnp.int32, (96, 96), 0)
    cols = lax.broadcasted_iota(jnp.int32, (96, 96), 1)
    eye = (rows == cols).astype(BF16)
    side = dot(eye, smalls[...], NT).astype(BF16)
    wx[...] = jnp.concatenate([wout[...], side, jnp.zeros((96, 112), BF16)], axis=1)
    small = jnp.concatenate([side[:24], jnp.zeros((24, 48), BF16)], axis=1)

    def run(own):
        for k, out in enumerate((p0, p1, p2, p3)):
            at = 192 * (own ^ k)
            parts = [wqkv[:, 768 * i + at : 768 * i + at + 192] for i in range(3)]
            parts.append(small)
            parts += [win[:, 768 * i + at : 768 * i + at + 192] for i in range(4)]
            out[...] = jnp.concatenate(parts, axis=1)

    each_chip(p, run)


SLOTS = (0, 2, 1, 3)


def interleave(pos, mine, other, out, at, slots):
    z, p, c = place(pos)

    def run(first, second):
        for k in range(4):
            for i in range(4):
                block = jnp.concatenate([first[at(i, k)], second[at(i, k)]], axis=0)
                start = (4 * (z ^ slots[i]) + (p ^ k)) * 48
                out[pl.ds(row_of(start, 16), 48), :] = block

    @pl.when(c == 0)
    def _():
        run(mine, other)

    @pl.when(c == 1)
    def _():
        run(other, mine)


def qkv_kernel(pos, am, ao, x0, x1, x2, x3, q, kv, wq, vecs, nb, bias):
    z, p, c = place(pos)
    everything = slice(None)
    interleave(
        pos, am, ao, wq, lambda i, k: (i, slice(24 * k, 24 * k + 24), everything), (0, 1, 2, 3)
    )
    flipped = jnp.transpose(wq[:, 512:640].astype(F32))
    vecs[...] = flipped[64:80]

    def run(own):
        at = slice(192 * own, 192 * own + 192)
        bias[0:1, :] = jnp.concatenate(
            [vecs[0:1, at], jnp.zeros((1, 192), F32), vecs[1:2, at], jnp.zeros((1, 64), F32)],
            axis=1,
        )

    each_chip(p, run)
    lane = lax.broadcasted_iota(jnp.int32, (1, 768), 1)
    mask = (lane >= 192 * z) & (lane < 192 * z + 192) & (lane % 24 == 0)
    second = jnp.sum(jnp.where(mask, vecs[8:9, :], 0.0))
    nb[0] = 8 - second.astype(jnp.int32)
    for k, x in enumerate((x0, x1, x2, x3)):
        got = (dot(x[...], wq[...]) + bias[0:1, :]).astype(BF16)
        pad = jnp.zeros((got.shape[0], 64), BF16)
        q[k] = jnp.concatenate([got[:, :192], pad], axis=1)
        kv[k] = jnp.concatenate([got[:, 192:384], pad, got[:, 384:576], pad], axis=1)


def join_ff_kernel(pos, mm, mo, wi, wx, bin_):
    z, p, c = place(pos)
    interleave(
        pos, mm, mo, wi, lambda i, k: (i, slice(24 * k, 24 * k + 24), slice(0, 768)), SLOTS
    )
    for i in range(4):
        base = (z ^ SLOTS[i]) * 192
        wx[pl.ds(row_of(base + c * 96, 32), 96), :] = mm[i, :, 768:1664]
        wx[pl.ds(row_of(base + (1 - c) * 96, 32), 96), :] = mo[i, :, 768:1664]
    flipped = jnp.transpose(wx[:, 768:896].astype(F32))
    bin_[...] = flipped[8:16]


def join_wo_kernel(pos, om, oo, wo):
    everything = slice(None)
    interleave(pos, om, oo, wo, lambda i, k: (k, slice(24 * i, 24 * i + 24), everything), SLOTS)


def key_range(pos, nb, k):
    z, p, c = place(pos)
    block = 2 * (p ^ k) + c
    return jnp.where(block < nb[0], 0, nb[0]), block + 1


def absolute_keys(pos, mine, other, keys, values, key_t, value_t):
    z, p, c = place(pos)
    for k in range(4):
        for ref, core in ((mine, c), (other, 1 - c)):
            at = 2 * (p ^ k) + core
            keys[at] = ref[k, :, 0:256]
            values[at] = ref[k, :, 256:512]
            if key_t is not None:
                key_t[at] = jnp.transpose(ref[k, :, 0:256])[:192] * 0.125
            if value_t is not None:
                value_t[at] = jnp.transpose(ref[k, :, 256:512])[:192]


def masked_heads(block):
    lane = lax.broadcasted_iota(jnp.int32, (256, 128), 1)
    zero = jnp.zeros((256, 128), block.dtype)
    return (
        jnp.where(lane < 64, block[:, 0:128], zero),
        jnp.where(lane >= 64, block[:, 0:128], zero),
        block[:, 128:256],
    )


GROUPS = (slice(0, 128), slice(0, 128), slice(128, 256))


def attention_kernel(pos, nb, q, mine, other, a0, a1, a2, a3, ot, lse, keys, values, value_t):
    scale = 0.125 * LOG2E
    absolute_keys(pos, mine, other, keys, values, None, value_t)
    for k, out in enumerate((a0, a1, a2, a3)):
        low, high = key_range(pos, nb, k)
        heads = masked_heads(q[k])

        def step(i, state):
            kb = low + 2 * i
            more = jnp.minimum(kb + 1, 7)
            valid = kb + 1 < high
            new = []
            scores = []
            for h in range(3):
                one = dot(keys[kb, :, GROUPS[h]], heads[h], NT)
                two = dot(keys[more, :, GROUPS[h]], heads[h], NT)
                scores.append((one, jnp.where(valid, two, NEG_LARGE)))
            for h in range(3):
                top, total, acc = state[h]
                one, two = scores[h]
                peak = jnp.max(jnp.maximum(one, two), axis=0, keepdims=True)
                next_top = jnp.maximum(top, peak * scale)
                one = jnp.exp2(one * scale - next_top)
                two = jnp.exp2(two * scale - next_top)
                factor = jnp.exp2(top - next_top)
                total = total * factor + jnp.sum(one + two, axis=0, keepdims=True)
                at = slice(64 * h, 64 * h + 64)
                acc = acc * factor + (
                    dot(value_t[kb, at, :], one.astype(BF16))
                    + dot(value_t[more, at, :], two.astype(BF16))
                )
                new.append((next_top, total, acc))
            return tuple(new)

        start = tuple(
            (jnp.full((1, BLK), NEG_LARGE, F32), jnp.zeros((1, BLK), F32), jnp.zeros((HDIM, BLK), F32))
            for _ in range(3)
        )
        state = lax.fori_loop(0, (high - low + 1) >> 1, step, start)
        done = []
        for h in range(3):
            top, total, acc = state[h]
            mixed = acc / total
            ot[k, 64 * h : 64 * h + 64, :] = mixed
            lse[k, h : h + 1, :] = top + jnp.log(total) * LOG2E
            done.append(mixed)
        out[...] = jnp.transpose(jnp.concatenate(done, axis=0)).astype(BF16)


def attention_back_kernel(
    pos, nb, q, mine, other, g0, g1, g2, g3, ot, lse, dq, dmine, dother, keys, values, key_t, dk, dv
):
    z, p, c = place(pos)
    scale = 0.125 * LOG2E
    absolute_keys(pos, mine, other, keys, values, key_t, None)
    dk[...] = jnp.zeros(dk.shape, F32)
    dv[...] = jnp.zeros(dv.shape, F32)
    for k, grad in enumerate((g0, g1, g2, g3)):
        low, high = key_range(pos, nb, k)
        heads = masked_heads(q[k])
        padded = jnp.concatenate([grad[...], jnp.zeros((256, 64), BF16)], axis=1)
        grads = masked_heads(padded)
        flipped = jnp.transpose(grad[...].astype(F32))
        product = flipped * ot[k]
        deltas = [
            jnp.sum(product[64 * h : 64 * h + 64], axis=0, keepdims=True) for h in range(3)
        ]
        logs = [lse[k, h : h + 1, :] for h in range(3)]
        pair_q = jnp.concatenate([heads[0], heads[1]], axis=0) * 0.125
        small_q = heads[2] * 0.125
        pair_g = jnp.concatenate([grads[0], grads[1]], axis=0)

        def step(kb, state):
            new, probs_low, scores_low = [], [], []
            for h in range(3):
                probs = jnp.exp2(dot(keys[kb, :, GROUPS[h]], heads[h], NT) * scale - logs[h])
                dprobs = dot(values[kb, :, GROUPS[h]], grads[h], NT)
                probs_low.append(probs.astype(BF16))
                scores_low.append((probs * (dprobs - deltas[h])).astype(BF16))
            for h in range(3):
                new.append(state[h] + dot(key_t[kb, 64 * h : 64 * h + 64, :], scores_low[h]))
            for ref, lows, pair, one in (
                (dk, scores_low, pair_q, small_q),
                (dv, probs_low, pair_g, grads[2]),
            ):
                ref[kb, :, 0:128] += dot(jnp.concatenate(lows[:2], axis=1), pair)
                ref[kb, :, 128:256] += dot(lows[2], one)
            return tuple(new)

        state = lax.fori_loop(
            low, high, step, tuple(jnp.zeros((HDIM, BLK), F32) for _ in range(3))
        )
        dq[k] = jnp.transpose(jnp.concatenate(state, axis=0))
    for k in range(4):
        at = 2 * (p ^ k)
        dmine[k] = jnp.concatenate([dk[at + c], dv[at + c]], axis=1)
        dother[k] = jnp.concatenate([dk[at + 1 - c], dv[at + 1 - c]], axis=1).astype(BF16)


def norm_kernel(pos, tokens, a0, a1, a2, a3, wo, vecs, low, xhat, rstd):
    z, p, c = place(pos)
    resid = tokens[...].astype(F32) + vecs[2:3, :]
    for k, a in enumerate((a0, a1, a2, a3)):
        start = (p ^ k) * 192
        resid += dot(a[...], wo[pl.ds(row_of(start, 64), 192), :])
    center = resid - jnp.mean(resid, axis=-1, keepdims=True)
    scale = lax.rsqrt(jnp.mean(center * center, axis=-1, keepdims=True) + EPSILON)
    hat = center * scale
    xhat[...] = hat
    rstd[...] = scale
    low[...] = (hat * vecs[3:4, :] + vecs[5:6, :]).astype(BF16)


def norm_grad(grad, gain, hat, scale):
    e = grad * gain
    mean_e = jnp.mean(e, axis=-1, keepdims=True)
    mean_x = jnp.mean(e * hat, axis=-1, keepdims=True)
    return scale * (e - mean_e - hat * mean_x)


def summed(i, own, rx, ry, sx, sy):
    half = slice(32 * (i % 4), 32 * (i % 4) + 32)
    first, last = (rx, sy) if i < 4 else (ry, sx)
    return own[32 * i : 32 * i + 32, :] + first[half, :].astype(F32) + last[half, :].astype(F32)


def total(values):
    return jnp.sum(values, axis=0, keepdims=True)


def norm_two_kernel(vecs, xhat, own, rx, ry, sx, sy, cot, block_out, low, grad_two, sums):
    acc = [jnp.zeros((1, 768), F32) for _ in range(3)]
    for i in range(8):
        at = slice(32 * i, 32 * i + 32)
        hidden = xhat[at, :] * vecs[3:4, :] + vecs[5:6, :]
        resid = hidden + summed(i, own, rx, ry, sx, sy) + vecs[7:8, :]
        center = resid - jnp.mean(resid, axis=-1, keepdims=True)
        scale = lax.rsqrt(jnp.mean(center * center, axis=-1, keepdims=True) + EPSILON)
        hat = center * scale
        block_out[at, :] = (hat * vecs[4:5, :] + vecs[6:7, :]).astype(BF16)
        grad = cot[at, :].astype(F32)
        back = norm_grad(grad, vecs[4:5, :], hat, scale)
        grad_two[at, :] = back
        low[at, :] = back.astype(BF16)
        acc = [acc[0] + total(grad * hat), acc[1] + total(grad), acc[2] + total(back)]
    sums[...] = jnp.concatenate(acc + [jnp.zeros((5, 768), F32)], axis=0)


def norm_one_kernel(
    pos, own, rx, ry, sx, sy, grad_two, xhat, rstd, vecs, wo, o0, o1, o2, o3, low, grad_one, sums
):
    z, p, c = place(pos)
    acc = [jnp.zeros((1, 768), F32) for _ in range(3)]
    for i in range(8):
        at = slice(32 * i, 32 * i + 32)
        grad = summed(i, own, rx, ry, sx, sy) + grad_two[at, :]
        hat = xhat[at, :]
        back = norm_grad(grad, vecs[3:4, :], hat, rstd[at, :])
        grad_one[at, :] = back
        low[at, :] = back.astype(BF16)
        acc = [acc[0] + total(grad * hat), acc[1] + total(grad), acc[2] + total(back)]
    sums[...] = jnp.concatenate(acc + [jnp.zeros((5, 768), F32)], axis=0)
    for k, out in enumerate((o0, o1, o2, o3)):
        start = (p ^ k) * 192
        out[...] = dot(low[...], wo[pl.ds(row_of(start, 64), 192), :], NT).astype(BF16)


def ff_block(h, wi, wx, bias, act, slope):
    acc = jnp.zeros((h.shape[0], 768), F32)
    for f in range(3):
        at = slice(256 * f, 256 * f + 256)
        u = dot(h, wi[:, at]) + bias[1:2, at]
        cdf = 0.5 * (1.0 + lax.erf(u * 0.7071067811865476))
        low = (u * cdf).astype(BF16)
        act[:, at] = low
        slope[:, at] = cdf + u * jnp.exp2(u * u * (-0.5 * LOG2E)) * 0.3989422804014327
        acc += dot(low, wx[at, :768])
    return acc


def ff_back_block(g, slope, wi, wx, low, sums):
    acc = jnp.zeros((256, 768), F32)
    for f in range(3):
        at = slice(256 * f, 256 * f + 256)
        pre = dot(g, wx[at, :768], NT) * slope[:, at]
        pre_low = pre.astype(BF16)
        low[:, at] = pre_low
        sums[0:1, at] += total(pre)
        acc += dot(pre_low, wi[:, at], NT)
    return acc


def ff_own_kernel(h, wi, wx, bias, part, act, slope):
    part[...] = ff_block(h[...], wi, wx, bias, act, slope)


def ff_near_kernel(h1, h2, wi, wx, bias, part1, part2, act1, act2, slope1, slope2):
    part1[...] = ff_block(h1[...], wi, wx, bias, act1, slope1).astype(BF16)
    part2[...] = ff_block(h2[...], wi, wx, bias, act2, slope2).astype(BF16)


def first_round(part, part1, part2, mx, my):
    low = part.astype(BF16)
    mx[...] = jnp.concatenate([part1[:128, :], low[:128]], axis=0)
    my[...] = jnp.concatenate([part2[128:, :], low[128:]], axis=0)


def ff_far_kernel(ha, hb, part1, part2, wi, wx, bias, mx, my, act, slope):
    h = jnp.concatenate([ha[...], hb[...]], axis=0)
    first_round(ff_block(h, wi, wx, bias, act, slope), part1, part2, mx, my)


def ff_back_own_kernel(g, slope, wi, wx, back, low, sums):
    sums[...] = jnp.zeros((8, 768), F32)
    back[...] = ff_back_block(g[...], slope, wi, wx, low, sums)


def ff_back_near_kernel(g1, g2, slope1, slope2, wi, wx, back1, back2, low1, low2, sums):
    sums[...] = jnp.zeros((8, 768), F32)
    back1[...] = ff_back_block(g1[...], slope1, wi, wx, low1, sums).astype(BF16)
    back2[...] = ff_back_block(g2[...], slope2, wi, wx, low2, sums).astype(BF16)


def ff_back_far_kernel(ga, gb, slope, back1, back2, wi, wx, mx, my, low, sums):
    sums[...] = jnp.zeros((8, 768), F32)
    g = jnp.concatenate([ga[...], gb[...]], axis=0)
    first_round(ff_back_block(g, slope, wi, wx, low, sums), back1, back2, mx, my)


def column_of(row):
    n = row.shape[1]
    first = lax.broadcasted_iota(jnp.int32, (128, n), 0) == 0
    return jnp.transpose(jnp.where(first, jnp.broadcast_to(row, (128, n)), 0.0))


def ff_grad_kernel(
    pos, h0, h1, h2, ha, hb, b0, b1, b2, b3, a0, a1, a2, a3, g0, g1, g2, ga, gb, s0, s1, s2,
    keep, send, gi, go
):
    z, p, c = place(pos)
    acc = dot(h0[...], b0[...], TN) + dot(h1[...], b1[...], TN) + dot(h2[...], b2[...], TN)
    gi[...] = acc + dot(ha[...], b3[:128, :], TN) + dot(hb[...], b3[128:, :], TN)
    acc = dot(a0[...], g0[...], TN) + dot(a1[...], g1[...], TN) + dot(a2[...], g2[...], TN)
    go[:, :768] = acc + dot(a3[:128, :], ga[...], TN) + dot(a3[128:, :], gb[...], TN)
    go[:, 768:] = column_of(s0[0:1, :] + s1[0:1, :] + s2[0:1, :])
    for i in range(4):
        for out, core in ((keep, c), (send, 1 - c)):
            for k in range(4):
                start = (4 * (z ^ SLOTS[i]) + (p ^ k)) * 48 + core * 24
                out[i, 24 * k : 24 * k + 24, 0:768] = gi[pl.ds(row_of(start), 24), :].astype(BF16)
            start = (z ^ SLOTS[i]) * 192 + core * 96
            out[i, :, 768:1664] = go[pl.ds(row_of(start), 96), :].astype(BF16)


def wo_grad_kernel(pos, a0, a1, a2, a3, low, sum_one, sum_two, keep, send, acc):
    z, p, c = place(pos)
    for k, a in enumerate((a0, a1, a2, a3)):
        start = (p ^ k) * 192
        acc[pl.ds(row_of(start), 192), 0:768] = dot(a[...], low[...], TN)
    rows = jnp.concatenate(
        [
            sum_one[2:3, :],
            sum_one[0:1, :],
            sum_two[0:1, :],
            sum_one[1:2, :],
            sum_two[1:2, :],
            sum_two[2:3, :],
            jnp.zeros((122, 768), F32),
        ],
        axis=0,
    )
    acc[:, 768:896] = jnp.transpose(rows)
    for k in range(4):
        for j in range(4):
            for out, core in ((keep, c), (send, 1 - c)):
                start = (4 * (z ^ SLOTS[j]) + (p ^ k)) * 48 + core * 24
                out[k, 24 * j : 24 * j + 24, :] = acc[pl.ds(row_of(start), 24), :].astype(BF16)


def qkv_back_kernel(dq, dmine, dother, wq, i0, mx, my, rest, low, sums):
    bias_q = jnp.zeros((1, 192), F32)
    bias_v = jnp.zeros((1, 192), F32)
    for k in range(4):
        grad_q = dq[k]
        grad_kv = dmine[k] + dother[k].astype(F32)
        grad_v = grad_kv[:, 256:448]
        bias_q += total(grad_q)
        bias_v += total(grad_v)
        parts = [grad_q, grad_kv[:, :192], grad_v, jnp.zeros((256, 64), F32)]
        whole = jnp.concatenate(parts, axis=1).astype(BF16)
        low[k] = whole
        part = dot(whole, wq[...], NT)
        if k == 0:
            i0[...] = part
        elif k == 1:
            mx[0:128, :] = part[:128].astype(BF16)
            rest[1, 128:] = part[128:].astype(BF16)
        elif k == 2:
            my[0:128, :] = part[128:].astype(BF16)
            rest[0, :128] = part[:128].astype(BF16)
        else:
            mx[128:256, :] = part[:128].astype(BF16)
            my[128:256, :] = part[128:].astype(BF16)
    sums[...] = jnp.concatenate(
        [
            jnp.concatenate([bias_q, jnp.zeros((1, 64), F32)], axis=1),
            jnp.concatenate([bias_v, jnp.zeros((1, 64), F32)], axis=1),
            jnp.zeros((6, 256), F32),
        ],
        axis=0,
    )


def qkv_grad_kernel(pos, x0, x1, x2, x3, low, sums, keep, send, acc):
    z, p, c = place(pos)
    acc[...] = sum(dot(x[...], low[k], TN) for k, x in enumerate((x0, x1, x2, x3)))
    rows = jnp.concatenate(
        [jnp.zeros((64, 256), F32), sums[...], jnp.zeros((56, 256), F32)], axis=0
    )
    extra = jnp.transpose(rows)[:192]
    for i in range(4):
        acc[192 * i : 192 * i + 192, 512:640] += extra
    for j in range(4):
        for k in range(4):
            for out, core in ((keep, c), (send, 1 - c)):
                start = (4 * (z ^ SLOTS[j]) + (p ^ k)) * 48 + core * 24
                out[j, 24 * k : 24 * k + 24, :] = acc[pl.ds(row_of(start), 24), :].astype(BF16)


def turned(block):
    n = block.shape[0]
    return jnp.transpose(jnp.concatenate([block, jnp.zeros((128 - n, 128), F32)], axis=0))


def finish_kernel(
    pos, tq, tm, f1, f2, f3, uo, gqkv, gbqv, gwo, gbo, gain, shift, gwin, gbin, gwout, gbout
):
    z, p, c = place(pos)
    gwout[...] = tm[:, 768:1536]
    gbin[...] = turned(tm[:, 1536:1664])[0:1, 0:96]
    gwo[...] = uo[:, 0:768]
    side = turned(uo[:, 768:896])
    gbo[...] = side[0:1, 0:24]
    gain[...] = side[1:3, 0:24]
    shift[...] = side[3:5, 0:24]
    gbout[...] = side[5:6, 0:24]

    def run(own):
        biases = jnp.zeros((24, 128), F32)
        for k in range(4):
            chip = own ^ k
            if k == 0:
                qkv, win = tq[0:24, :], tm[0:24, 0:768]
            else:
                got = (f1, f2, f3)[k - 1][...].astype(F32)
                qkv, win = got[:, 0:640], got[:, 640:1408]
            for i in range(3):
                at = 768 * i + 192 * chip
                gqkv[:, at : at + 192] = qkv[:, 192 * i : 192 * i + 192]
            for i in range(4):
                at = 768 * i + 192 * chip
                gwin[:, at : at + 192] = win[:, 192 * i : 192 * i + 192]
            biases += jnp.where(z == chip, qkv[:, 512:640], 0.0)
        gbqv[...] = turned(biases)[64:66, 0:24]

    each_chip(p, run)


def chip_swap(value, k):
    return lax.ppermute(value, "seq", [(s, s ^ (2 * k)) for s in range(8)])


def core_swap(value):
    return lax.ppermute(value, "seq", [(s, s ^ 1) for s in range(8)])


def z_trade(value):
    return lax.all_to_all(value, "dp", 0, 0, tiled=True)


def z_swap(value, j):
    return lax.ppermute(value, "dp", [(i, i ^ j) for i in range(4)])


def gather_first(value):
    return chip_swap(value, 1), chip_swap(value, 2)


def gather_last(near_x, near_y):
    return chip_swap(near_y[:128], 1), chip_swap(near_x[128:], 2)


def reduce_parts(mx, my, part1, part2):
    rx, ry = chip_swap(mx, 1), chip_swap(my, 2)
    sy = chip_swap(low_add(part2[:128], rx[128:]).astype(BF16), 2)
    sx = chip_swap(low_add(part1[128:], ry[128:]).astype(BF16), 1)
    return rx, ry, sx, sy


def after(value, *others):
    return lax.optimization_barrier((value, *others))[0]


def low_add(*terms):
    return sum(t.astype(F32) for t in terms)


def fast_device(
    tokens,
    doc_ids,
    cotangent,
    w_qkv,
    bias_qv,
    w_o,
    bias_o,
    ln_gain,
    ln_bias,
    w_in,
    bias_in,
    w_out,
    bias_out,
):
    pos = lax.axis_index(("dp", "seq")).astype(jnp.int32).reshape(1)
    others = (1, 2, 3)
    smalls = sum(
        jnp.pad(v, ((at, 16 - at - v.shape[0]), (0, 96 - v.shape[1])))
        for v, at in (
            (bias_qv, 0),
            (bias_o[None], 2),
            (ln_gain, 3),
            (ln_bias, 5),
            (bias_out[None], 7),
            (doc_ids[None, :24].astype(BF16), 8),
            (bias_in[None], 9),
        )
    )
    zo_one = z_swap(w_o, 2)
    p0, p1, p2, p3, zw = call(
        pack_kernel,
        (pos, w_qkv, w_in, w_out, smalls),
        [sds((24, 1408), BF16)] * 4 + [sds((96, 896), BF16)],
        name="pack",
    )
    zo_pair = jnp.concatenate([w_o, zo_one], axis=0)
    zo_two = z_swap(zo_pair, 1)
    got = [p0] + [chip_swap(v, k) for v, k in zip((p1, p2, p3), others)]
    tokens_far = after(tokens, p0, zo_one)
    x1, x2 = chip_swap(tokens_far, 1), chip_swap(tokens_far, 2)
    first = jnp.concatenate([g[:, :640] for g in got], axis=0)
    first = after(first, zo_two)
    firsts = [first] + [z_swap(first, j) for j in others]
    x3 = chip_swap(after(tokens_far, *got[1:]), 3)
    xs = (tokens, x1, x2, x3)
    first_all = jnp.stack(firsts)
    first_other = core_swap(after(first_all, x1, x2, x3))
    bulk = jnp.concatenate([jnp.concatenate([g[:, 640:] for g in got], axis=0), zw], axis=1)
    bulk_one = z_swap(after(bulk, first_all), 2)
    wo_z = after(jnp.concatenate([zo_pair, zo_two], axis=0), first_all)
    wo_far = [chip_swap(wo_z, k) for k in others]

    q, kv, wq, vecs, nb = call(
        qkv_kernel,
        (pos, first_all, first_other, *xs),
        [
            sds((4, 256, 256), BF16),
            sds((4, 256, 512), BF16),
            sds((768, 640), BF16),
            sds((16, 768), F32),
            sds((1,), jnp.int32),
        ],
        scratch=[pltpu.VMEM((8, 640), F32)],
        smem_out=(4,),
        name="qkv",
    )
    kv_other = core_swap(kv)
    *attended, ot, lse = call(
        attention_kernel,
        (pos, nb, q, kv, kv_other),
        [sds((256, 192), BF16)] * 4 + [sds((4, 192, 256), F32), sds((4, 8, 256), F32)],
        scratch=[pltpu.VMEM((8, 256, 256), BF16)] * 2 + [pltpu.VMEM((8, 192, 256), BF16)],
        smem_in=(0, 1),
        flops=2e9,
        name="attention",
    )
    *attended, wo1, wo2, wo3 = lax.optimization_barrier((*attended, *wo_far))
    wo_all = jnp.stack([wo_z, wo1, wo2, wo3])
    wo_other = core_swap(wo_all)
    pieces = [attended[0]] + [chip_swap(attended[k], k) for k in others]
    bulk_pair = jnp.stack([bulk, after(bulk_one, *pieces[1:])])
    bulk_two = z_swap(bulk_pair, 1)
    (wo,) = call(join_wo_kernel, (pos, wo_all, wo_other), [sds((768, 768), BF16)], name="join_wo")
    hidden, xhat, rstd = call(
        norm_kernel,
        (pos, tokens, *pieces, wo, vecs),
        [sds((256, 768), BF16), sds((256, 768), F32), sds((256, 1), F32)],
        name="norm_one",
    )
    hx, hy = gather_first(hidden)
    bulk_all = after(jnp.concatenate([bulk_pair, bulk_two]), hx, hy)
    wi, wx, bin_ = call(
        join_ff_kernel,
        (pos, bulk_all, core_swap(bulk_all)),
        [sds((768, 768), BF16), sds((768, 896), BF16), sds((8, 768), F32)],
        name="join_ff",
    )
    block, low_block, half = sds((256, 768), F32), sds((256, 768), BF16), sds((128, 768), BF16)
    ff_sums = sds((8, 768), F32)
    part_own, act0, slope0 = call(
        ff_own_kernel,
        (hidden, wi, wx, bin_),
        [block, low_block, block],
        smem_in=(),
        name="ff_own",
    )
    ha, hb = gather_last(hx, hy)
    hx = after(hx, part_own)
    part1, part2, act1, act2, slope1, slope2 = call(
        ff_near_kernel,
        (hx, hy, wi, wx, bin_),
        [low_block] * 4 + [block] * 2,
        smem_in=(),
        name="ff_near",
    )
    ha = after(ha, part1)
    mx, my, act3, slope3 = call(
        ff_far_kernel,
        (ha, hb, part1, part2, wi, wx, bin_),
        [low_block] * 3 + [block],
        smem_in=(),
        name="ff_far",
    )
    block_out, grad_two_low, grad_two, sums_two = call(
        norm_two_kernel,
        (vecs, xhat, part_own, *reduce_parts(mx, my, part1, part2), cotangent),
        [low_block, low_block, block, ff_sums],
        smem_in=(),
        name="norm_two",
    )
    gx, gy = gather_first(grad_two_low)
    back_own, low0, sum0 = call(
        ff_back_own_kernel,
        (grad_two_low, slope0, wi, wx),
        [block, low_block, ff_sums],
        smem_in=(),
        name="ff_back_own",
    )
    ga, gb = gather_last(gx, gy)
    gx = after(gx, back_own)
    back1, back2, low1, low2, sum1 = call(
        ff_back_near_kernel,
        (gx, gy, slope1, slope2, wi, wx),
        [low_block] * 4 + [ff_sums],
        smem_in=(),
        name="ff_back_near",
    )
    ga = after(ga, back1)
    mx, my, low3, sum2 = call(
        ff_back_far_kernel,
        (ga, gb, slope3, back1, back2, wi, wx),
        [low_block] * 3 + [ff_sums],
        smem_in=(),
        name="ff_back_far",
    )
    rx, ry, sx, sy = reduce_parts(mx, my, back1, back2)
    ff_keep, ff_send = call(
        ff_grad_kernel,
        (pos, hidden, hx, hy, ha, hb, low0, low1, low2, low3, act0, act1, act2, act3)
        + (grad_two_low, gx, gy, ga, gb, sum0, sum1, sum2),
        [sds((4, 96, 1664), BF16)] * 2,
        scratch=[pltpu.VMEM((768, 768), F32), pltpu.VMEM((768, 896), F32)],
        flops=1e10,
        name="ff_grad",
    )
    sx = after(sx, ff_keep)
    ff_sum = low_add(ff_keep, core_swap(ff_send))
    ff_low = ff_sum[2:].astype(BF16)

    *grad_att, low_one, grad_one, sums_one = call(
        norm_one_kernel,
        (pos, back_own, rx, ry, sx, sy, grad_two, xhat, rstd, vecs, wo),
        [sds((256, 192), BF16)] * 4
        + [sds((256, 768), BF16), sds((256, 768), F32), sds((8, 768), F32)],
        name="norm_one_back",
    )
    grad_pieces = [grad_att[0]] + [chip_swap(grad_att[k], k) for k in others]
    wo_keep, wo_send = call(
        wo_grad_kernel,
        (pos, *pieces, low_one, sums_one, sums_two),
        [sds((4, 96, 896), BF16)] * 2,
        scratch=[pltpu.VMEM((768, 896), F32)],
        name="wo_grad",
    )
    wo_got = core_swap(wo_send)
    wo_sum = low_add(wo_keep, wo_got)
    wo_low = [wo_sum[k].astype(BF16) for k in others]
    wo_part = [chip_swap(v, k) for v, k in zip(wo_low, others)]
    *grad_pieces, ff_low = lax.optimization_barrier((*grad_pieces, ff_low, *wo_low))[:5]
    ff_got = z_swap(ff_low, 1)
    ff_left = low_add(ff_sum[1], ff_got[1]).astype(BF16)
    ff_mine = low_add(ff_sum[0], ff_got[0])

    dq, dmine, dother = call(
        attention_back_kernel,
        (pos, nb, q, kv, kv_other, *grad_pieces, ot, lse),
        [sds((4, 256, 192), F32), sds((4, 256, 512), F32), sds((4, 256, 512), BF16)],
        scratch=[pltpu.VMEM((8, 256, 256), BF16)] * 2
        + [pltpu.VMEM((8, 192, 256), BF16)]
        + [pltpu.VMEM((8, 256, 256), F32)] * 2,
        smem_in=(0, 1),
        flops=1e10,
        name="attention_back",
    )
    dgot = core_swap(after(dother, *wo_part, ff_got))
    ff_far = z_swap(after(ff_left, dq), 2)
    in_own, in_x, in_y, in_rest, low, sums_qv = call(
        qkv_back_kernel,
        (dq, dmine, dgot, wq),
        [sds((256, 768), F32)]
        + [sds((256, 768), BF16)] * 2
        + [sds((2, 256, 768), BF16), sds((4, 256, 640), BF16), sds((8, 256), F32)],
        smem_in=(),
        name="qkv_back",
    )
    q_keep, q_send = call(
        qkv_grad_kernel,
        (pos, *xs, low, sums_qv),
        [sds((4, 96, 640), BF16)] * 2,
        scratch=[pltpu.VMEM((768, 640), F32)],
        name="qkv_grad",
    )
    q_got = core_swap(q_send)
    wo_mine = low_add(wo_sum[0], *wo_part)
    q_sum = low_add(q_keep, q_got)
    q_next = z_swap(q_sum[2:].astype(BF16), 1)
    got_x, got_y = chip_swap(in_x, 1), chip_swap(in_y, 2)
    got_x, got_y, q_next, ff_far = lax.optimization_barrier((got_x, got_y, q_next, ff_far))
    tm = low_add(ff_mine, ff_far)
    wo_mine = after(wo_mine, q_next)
    wo_next = z_swap(wo_mine[48:].astype(BF16), 1)
    wo_left = low_add(wo_mine[24:48], wo_next[24:]).astype(BF16)
    uo = low_add(wo_mine[:24], wo_next[:24], z_swap(wo_left, 2))
    q_left = low_add(q_sum[1], q_next[1]).astype(BF16)
    tq = low_add(q_sum[0], q_next[0], z_swap(q_left, 2))
    last_y = chip_swap(low_add(in_rest[0, :128], got_x[128:]).astype(BF16), 2)
    last_x = chip_swap(low_add(in_rest[1, 128:], got_y[128:]).astype(BF16), 1)
    input_grad = low_add(
        in_own,
        grad_one,
        jnp.concatenate([got_x[:128], got_y[:128]], axis=0),
        jnp.concatenate([last_y, last_x], axis=0),
    )
    final = [
        chip_swap(
            jnp.concatenate(
                [tq[24 * k : 24 * k + 24], tm[24 * k : 24 * k + 24, :768]], axis=1
            ).astype(BF16),
            k,
        )
        for k in others
    ]
    gqkv, gbqv, gwo, gbo, gain, shift, gwin, gbin, gwout, gbout = call(
        finish_kernel,
        (pos, after(tq, input_grad), tm, *final, uo),
        [
            sds((24, 2304), F32),
            sds((2, 24), F32),
            sds((24, 768), F32),
            sds((1, 24), F32),
            sds((2, 24), F32),
            sds((2, 24), F32),
            sds((24, 3072), F32),
            sds((1, 96), F32),
            sds((96, 768), F32),
            sds((1, 24), F32),
        ],
        name="finish",
    )
    return (
        block_out,
        input_grad,
        gqkv,
        gbqv,
        gwo,
        gbo.reshape(24),
        gain,
        shift,
        gwin,
        gbin.reshape(96),
        gwout,
        gbout.reshape(24),
    )


def layer_norm(resid, gain, shift):
    center = resid - jnp.mean(resid, axis=-1, keepdims=True)
    spread = jnp.mean(center * center, axis=-1, keepdims=True)
    return center * lax.rsqrt(spread + EPSILON) * gain + shift


def exact_gelu(value):
    return jax.nn.gelu(value, approximate=False)


def split_heads(matrix):
    return matrix.reshape(matrix.shape[0], HEADS, HDIM)


def allowed_pairs(query_doc, query_block, key_doc, key_block):
    return (query_doc[:, None] == key_doc[None, :]) & (key_block[None, :] <= query_block[:, None])


def over_parts(carry, arrays, update):
    count = arrays[0].shape[0]
    span = math.gcd(count, 1024)
    steps = count // span
    offsets = jnp.arange(steps, dtype=jnp.int32) * span
    parts = tuple((a.reshape((steps, span) + a.shape[1:]) for a in arrays))

    def inner(state, items):
        return (update(state, items[:-1], items[-1]), None)

    carry, unused = lax.scan(inner, carry, parts + (offsets,))
    return carry


def score_grads(query_heads, grad_heads, log_total, delta, allowed, key_heads, value_heads):
    raw = (
        jnp.einsum("qhd,khd->hqk", query_heads, key_heads, preferred_element_type=jnp.float32)
        * 0.125
    )
    probs = jnp.where(allowed[None], jnp.exp(raw - log_total[:, :, None]), 0.0)
    grad_probs = jnp.einsum(
        "qhd,khd->hqk", grad_heads, value_heads, preferred_element_type=jnp.float32
    )
    grad_scores = (probs * (grad_probs - delta[:, :, None]) * 0.125).astype(jnp.bfloat16)
    grad_query = jnp.einsum(
        "hqk,khd->qhd", grad_scores, key_heads, preferred_element_type=jnp.float32
    )
    grad_key = jnp.einsum(
        "hqk,qhd->khd", grad_scores, query_heads, preferred_element_type=jnp.float32
    )
    grad_value = jnp.einsum(
        "hqk,qhd->khd", probs.astype(jnp.bfloat16), grad_heads, preferred_element_type=jnp.float32
    )
    return (grad_query, grad_key, grad_value)


def on_device(
    tokens,
    doc_ids,
    cotangent,
    w_qkv,
    bias_qv,
    w_o,
    bias_o,
    ln_gain,
    ln_bias,
    w_in,
    bias_in,
    w_out,
    bias_out,
):
    rows = tokens.shape[0]
    width = tokens.shape[1]
    full = (
        lax.all_gather(w_qkv, ("dp", "seq"), axis=0, tiled=True),
        lax.all_gather(bias_qv, ("dp", "seq"), axis=1, tiled=True),
        lax.all_gather(w_o, ("dp", "seq"), axis=0, tiled=True),
        lax.all_gather(bias_o, ("dp", "seq"), axis=0, tiled=True),
        lax.all_gather(ln_gain, ("dp", "seq"), axis=1, tiled=True),
        lax.all_gather(ln_bias, ("dp", "seq"), axis=1, tiled=True),
        lax.all_gather(w_in, ("dp", "seq"), axis=0, tiled=True),
        lax.all_gather(bias_in, ("dp", "seq"), axis=0, tiled=True),
        lax.all_gather(w_out, ("dp", "seq"), axis=0, tiled=True),
        lax.all_gather(bias_out, ("dp", "seq"), axis=0, tiled=True),
    )
    (
        full_qkv,
        full_bias_qv,
        full_o,
        full_bias_o,
        full_gain,
        full_shift,
        full_in,
        full_bias_in,
        full_out,
        full_bias_out,
    ) = full
    positions = lax.axis_index("seq") * rows + jnp.arange(rows, dtype=jnp.int32)
    query_block = positions // BLK
    bias_three = jnp.concatenate(
        [
            full_bias_qv[0].astype(jnp.float32),
            jnp.zeros((width,), jnp.float32),
            full_bias_qv[1].astype(jnp.float32),
        ]
    )
    projected = (jnp.dot(tokens, full_qkv, preferred_element_type=jnp.float32) + bias_three).astype(
        jnp.bfloat16
    )
    queries = projected[:, :width]
    keys = projected[:, width : 2 * width]
    values = projected[:, 2 * width :]
    query_heads = split_heads(queries)

    def forward_update(state, parts, first):
        key_rows, value_rows, key_doc = parts
        count = key_rows.shape[0]
        key_block = (first + jnp.arange(count, dtype=jnp.int32)) // BLK
        allowed = allowed_pairs(doc_ids, query_block, key_doc, key_block)
        raw = (
            jnp.einsum(
                "qhd,khd->hqk",
                query_heads,
                split_heads(key_rows),
                preferred_element_type=jnp.float32,
            )
            * 0.125
        )
        masked = jnp.where(allowed[None], raw, NEG_LARGE)
        top, total, summed = state
        new_top = jnp.maximum(top, jnp.max(masked, axis=-1))
        weights = jnp.where(allowed[None], jnp.exp(masked - new_top[:, :, None]), 0.0)
        factor = jnp.exp(top - new_top)
        total = total * factor + jnp.sum(weights, axis=-1)
        summed = summed * factor[:, :, None] + jnp.einsum(
            "hqk,khd->hqd",
            weights.astype(jnp.bfloat16),
            split_heads(value_rows),
            preferred_element_type=jnp.float32,
        )
        return (new_top, total, summed)

    start_state = (
        jnp.full((HEADS, rows), NEG_LARGE, jnp.float32),
        jnp.zeros((HEADS, rows), jnp.float32),
        jnp.zeros((HEADS, rows, HDIM), jnp.float32),
    )
    top, total, summed = over_parts(
        start_state,
        (
            lax.all_gather(keys, "seq", axis=0, tiled=True),
            lax.all_gather(values, "seq", axis=0, tiled=True),
            lax.all_gather(doc_ids, "seq", axis=0, tiled=True),
        ),
        forward_update,
    )
    attn_heads = summed / total[:, :, None]
    log_total = top + jnp.log(total)
    attended_low = attn_heads.transpose(1, 0, 2).reshape(rows, width).astype(jnp.bfloat16)
    resid_one = (
        tokens.astype(jnp.float32)
        + jnp.dot(attended_low, full_o, preferred_element_type=jnp.float32)
        + full_bias_o.astype(jnp.float32)
    )
    hidden_one, norm_one_pull = jax.vjp(
        layer_norm, resid_one, full_gain[0].astype(jnp.float32), full_shift[0].astype(jnp.float32)
    )
    hidden_low = hidden_one.astype(jnp.bfloat16)
    pre_act = jnp.dot(
        hidden_low, full_in, preferred_element_type=jnp.float32
    ) + full_bias_in.astype(jnp.float32)
    activated, gelu_pull = jax.vjp(exact_gelu, pre_act)
    act_low = activated.astype(jnp.bfloat16)
    resid_two = (
        hidden_one
        + jnp.dot(act_low, full_out, preferred_element_type=jnp.float32)
        + full_bias_out.astype(jnp.float32)
    )
    normed, norm_two_pull = jax.vjp(
        layer_norm, resid_two, full_gain[1].astype(jnp.float32), full_shift[1].astype(jnp.float32)
    )
    block_out = normed.astype(jnp.bfloat16)
    again = (
        lax.all_gather(w_qkv, ("dp", "seq"), axis=0, tiled=True),
        lax.all_gather(bias_qv, ("dp", "seq"), axis=1, tiled=True),
        lax.all_gather(w_o, ("dp", "seq"), axis=0, tiled=True),
        lax.all_gather(bias_o, ("dp", "seq"), axis=0, tiled=True),
        lax.all_gather(ln_gain, ("dp", "seq"), axis=1, tiled=True),
        lax.all_gather(ln_bias, ("dp", "seq"), axis=1, tiled=True),
        lax.all_gather(w_in, ("dp", "seq"), axis=0, tiled=True),
        lax.all_gather(bias_in, ("dp", "seq"), axis=0, tiled=True),
        lax.all_gather(w_out, ("dp", "seq"), axis=0, tiled=True),
        lax.all_gather(bias_out, ("dp", "seq"), axis=0, tiled=True),
    )
    back_qkv = again[0]
    back_o = again[2]
    back_in = again[6]
    back_out = again[8]
    grad_resid_two, grad_gain_two, grad_shift_two = norm_two_pull(cotangent.astype(jnp.float32))
    grad_two_low = grad_resid_two.astype(jnp.bfloat16)
    grad_w_out = jnp.einsum("tf,td->fd", act_low, grad_two_low, preferred_element_type=jnp.float32)
    grad_bias_out = jnp.sum(grad_resid_two, axis=0)
    grad_act = jnp.einsum("td,fd->tf", grad_two_low, back_out, preferred_element_type=jnp.float32)
    (grad_pre,) = gelu_pull(grad_act)
    grad_pre_low = grad_pre.astype(jnp.bfloat16)
    grad_w_in = jnp.einsum(
        "td,tf->df", hidden_low, grad_pre_low, preferred_element_type=jnp.float32
    )
    grad_bias_in = jnp.sum(grad_pre, axis=0)
    grad_hidden = (
        jnp.einsum("tf,df->td", grad_pre_low, back_in, preferred_element_type=jnp.float32)
        + grad_resid_two
    )
    grad_resid_one, grad_gain_one, grad_shift_one = norm_one_pull(grad_hidden)
    grad_one_low = grad_resid_one.astype(jnp.bfloat16)
    grad_w_o = jnp.einsum(
        "te,td->ed", attended_low, grad_one_low, preferred_element_type=jnp.float32
    )
    grad_bias_o = jnp.sum(grad_resid_one, axis=0)
    grad_attn_low = jnp.einsum(
        "td,ed->te", grad_one_low, back_o, preferred_element_type=jnp.float32
    ).astype(jnp.bfloat16)
    grad_heads = split_heads(grad_attn_low)
    delta = jnp.sum(grad_heads.astype(jnp.float32).transpose(1, 0, 2) * attn_heads, axis=-1)
    keys_all, values_all, docs_all = (
        lax.all_gather(keys, "seq", axis=0, tiled=True),
        lax.all_gather(values, "seq", axis=0, tiled=True),
        lax.all_gather(doc_ids, "seq", axis=0, tiled=True),
    )
    length = keys_all.shape[0]
    span = math.gcd(length, 1024)
    steps = length // span
    offsets = jnp.arange(steps, dtype=jnp.int32) * span

    def back_step(grad_query, items):
        key_rows, value_rows, key_doc, first = items
        key_block = (first + jnp.arange(span, dtype=jnp.int32)) // BLK
        allowed = allowed_pairs(doc_ids, query_block, key_doc, key_block)
        part_query, part_key, part_value = score_grads(
            query_heads,
            grad_heads,
            log_total,
            delta,
            allowed,
            split_heads(key_rows),
            split_heads(value_rows),
        )
        return (
            grad_query + part_query,
            (part_key.reshape(span, width), part_value.reshape(span, width)),
        )

    grad_query, (key_terms, value_terms) = lax.scan(
        back_step,
        jnp.zeros((rows, HEADS, HDIM), jnp.float32),
        (
            keys_all.reshape(steps, span, width),
            values_all.reshape(steps, span, width),
            docs_all.reshape(steps, span),
            offsets,
        ),
    )
    grad_keys, grad_values = (
        lax.psum_scatter(
            key_terms.reshape(length, width).astype(jnp.bfloat16),
            "seq",
            scatter_dimension=0,
            tiled=True,
        ).astype(jnp.float32),
        lax.psum_scatter(
            value_terms.reshape(length, width).astype(jnp.bfloat16),
            "seq",
            scatter_dimension=0,
            tiled=True,
        ).astype(jnp.float32),
    )
    grad_queries = grad_query.reshape(rows, width)
    grad_qkv_low = jnp.concatenate([grad_queries, grad_keys, grad_values], axis=1).astype(
        jnp.bfloat16
    )
    grad_w_qkv = jnp.einsum("td,te->de", tokens, grad_qkv_low, preferred_element_type=jnp.float32)
    grad_bias_qv = jnp.stack([jnp.sum(grad_queries, axis=0), jnp.sum(grad_values, axis=0)])
    input_grad = (
        jnp.einsum("te,de->td", grad_qkv_low, back_qkv, preferred_element_type=jnp.float32)
        + grad_resid_one
    )
    grad_gain = jnp.stack([grad_gain_one, grad_gain_two])
    grad_shift = jnp.stack([grad_shift_one, grad_shift_two])
    owned = (
        lax.psum_scatter(grad_w_qkv, ("dp", "seq"), scatter_dimension=0, tiled=True),
        lax.psum_scatter(grad_bias_qv, ("dp", "seq"), scatter_dimension=1, tiled=True),
        lax.psum_scatter(grad_w_o, ("dp", "seq"), scatter_dimension=0, tiled=True),
        lax.psum_scatter(grad_bias_o, ("dp", "seq"), scatter_dimension=0, tiled=True),
        lax.psum_scatter(grad_gain, ("dp", "seq"), scatter_dimension=1, tiled=True),
        lax.psum_scatter(grad_shift, ("dp", "seq"), scatter_dimension=1, tiled=True),
        lax.psum_scatter(grad_w_in, ("dp", "seq"), scatter_dimension=0, tiled=True),
        lax.psum_scatter(grad_bias_in, ("dp", "seq"), scatter_dimension=0, tiled=True),
        lax.psum_scatter(grad_w_out, ("dp", "seq"), scatter_dimension=0, tiled=True),
        lax.psum_scatter(grad_bias_out, ("dp", "seq"), scatter_dimension=0, tiled=True),
    )
    return (
        block_out,
        input_grad,
        owned[0],
        owned[1],
        owned[2],
        owned[3],
        owned[4],
        owned[5],
        owned[6],
        owned[7],
        owned[8],
        owned[9],
    )


def solution(mesh):
    placed = (
        P(("dp", "seq"), None),
        P(("dp", "seq")),
        P(("dp", "seq"), None),
        P(("dp", "seq"), None),
        P(None, ("dp", "seq")),
        P(("dp", "seq"), None),
        P(("dp", "seq")),
        P(None, ("dp", "seq")),
        P(None, ("dp", "seq")),
        P(("dp", "seq"), None),
        P(("dp", "seq")),
        P(("dp", "seq"), None),
        P(("dp", "seq")),
    )
    sizes = dict(mesh.shape)
    fast = sizes["dp"] == 4 and sizes["seq"] == 8
    return jax.shard_map(
        fast_device if fast else on_device,
        mesh=mesh,
        in_specs=placed,
        out_specs=(
            P(("dp", "seq"), None),
            P(("dp", "seq"), None),
            P(("dp", "seq"), None),
            P(None, ("dp", "seq")),
            P(("dp", "seq"), None),
            P(("dp", "seq")),
            P(None, ("dp", "seq")),
            P(None, ("dp", "seq")),
            P(("dp", "seq"), None),
            P(("dp", "seq")),
            P(("dp", "seq"), None),
            P(("dp", "seq")),
        ),
        check_vma=False,
    )
```
